128 devices in a mesh: chan: 16 (over y, z), tm: 8 (over x, core).
Axes of the slice: x: 4, y: 4, z: 4, core: 2. Of those that a mesh axis runs over, the one named last changes fastest.
Arguments:
- filterbank: bfloat16 [4096, 8192], P('chan', 'tm'), may hold values from -6 to 6
- first_rows: int32 [12, 2048], replicated, may hold values from 0 to 1023, as said below
- second_rows: int32 [12, 2048], replicated, may hold values from 0 to 1023, as said below
- shifts: int32 [12, 2048], replicated, may hold values from 0 to 15, as said below
- harmonic_bins: int32 [8, 512], replicated, may hold values from 0 to 4095, as said below
Outputs:
- power: float32 [2048, 4096], P(('chan', 'tm'))
- harmonic_sum: float32 [2048, 512], P(('chan', 'tm'))
The draws below stay inside these ranges and needn't reach their ends.
Inputs may be any that keep to these rules, and one draw needn't show every extreme that they name: Only entries with r < min(2^(l+1), 2048) of row l are read. first_rows[l, r] lies below min(2^l, 1024). Only entries with r < min(2^(l+1), 2048) of row l are read. second_rows[l, r] lies below min(2^l, 1024). `shifts`: only entries with r < min(2^(l+1), 2048) of row l are read. harmonic_bins[h, k] = floor((h + 1) * (8 * k + u_k) / 8) with whole u_k from 0 to 7; u of the last fundamental is 7.
All inputs are finite; a program needn't handle non-finite values.
Results may differ from the reference program's by a relative error of at most 0.0003.
Values may be sent and summed in bfloat16 or wider, within the bound.
A program may use at most 192 MiB of HBM per device.

```python
import jax
import jax.numpy as jnp

C = 4096
LEVELS = 12
NDM = 2048
SHIFT = 16
HARM = 8
TIMES = 8192
NFUND = 512


def fdmt_tables(key):
    base = jax.random.fold_in(key, 5)
    key_slope, key_offset, key_delay = jax.random.split(base, 3)
    level = jnp.arange(LEVELS, dtype=jnp.int32)[:, None]
    row_index = jnp.arange(NDM, dtype=jnp.int32)[None, :]
    rows_out = jnp.minimum(jnp.left_shift(jnp.ones_like(level), level + 1), NDM)
    half_rows = rows_out // 2
    slope_first = jax.random.randint(jax.random.fold_in(key_slope, 1), (LEVELS, 1), 4, 9)
    slope_second = jax.random.randint(jax.random.fold_in(key_slope, 2), (LEVELS, 1), 4, 9)
    offset_first = jax.random.randint(jax.random.fold_in(key_offset, 1), (LEVELS, 1), 0, NDM // 2)
    offset_second = jax.random.randint(jax.random.fold_in(key_offset, 2), (LEVELS, 1), 0, NDM // 2)
    jitter_delay = jax.random.randint(key_delay, (LEVELS, NDM), 0, 2)
    first_part = (row_index * slope_first // 8 + offset_first) % half_rows
    second_part = (row_index * slope_second // 8 + offset_second) % half_rows
    delay_part = jnp.minimum(first_part * SHIFT // half_rows + jitter_delay * (row_index % 2), SHIFT - 1)
    return (first_part.astype(jnp.int32), second_part.astype(jnp.int32), delay_part.astype(jnp.int32))


def draw_first_rows(key, part):
    return fdmt_tables(key)[0]


def draw_second_rows(key, part):
    return fdmt_tables(key)[1]


def draw_shifts(key, part):
    return fdmt_tables(key)[2]


def draw_harmonic_bins(key, part):
    fund = jnp.arange(NFUND, dtype=jnp.int32)[None, :]
    order = jnp.arange(HARM, dtype=jnp.int32)[:, None]
    fraction = jax.random.randint(jax.random.fold_in(key, 11), (1, NFUND), 0, HARM)
    fraction = jnp.where(fund == NFUND - 1, HARM - 1, fraction)
    return ((order + 1) * (HARM * fund + fraction) // HARM).astype(jnp.int32)


def level_of(key, extent, pieces, low, high):
    factor_of, own = 1.0, jax.random.fold_in(key, 6)
    for position, shards_of in pieces:
        steps = jnp.exp(jax.random.uniform(jax.random.fold_in(own, position), (shards_of,), jnp.float32, low / len(pieces), high / len(pieces)))
        factor_of = factor_of * jnp.repeat(steps, extent[position] // shards_of).reshape([-1 if axis == position else 1 for axis in range(len(extent))])
    return factor_of


def normal_values(rng, shape, deviation, limit, shards=(), held_as=jnp.bfloat16):
    array = deviation * jax.random.normal(rng, shape, jnp.float32)
    if shards:
        array = array * level_of(rng, shape, shards, -0.22, 0.18)
    return jnp.clip(array, -limit, limit).astype(held_as)


def setup_inputs(seed: int = 0) -> dict:
    streams_of = jax.random.split(jax.random.key(seed), 6)
    filterbank = normal_values(streams_of[0], (C, TIMES), 1.0, 6.0, ((0, 16), (1, 8)))
    first_rows = draw_first_rows(jax.random.fold_in(streams_of[5], 71), 0)
    second_rows = draw_second_rows(jax.random.fold_in(streams_of[5], 71), 0)
    shifts = draw_shifts(jax.random.fold_in(streams_of[5], 71), 0)
    harmonic_bins = draw_harmonic_bins(jax.random.fold_in(streams_of[5], 71), 0)
    return {"filterbank": filterbank, "first_rows": first_rows, "second_rows": second_rows, "shifts": shifts, "harmonic_bins": harmonic_bins}


def merge_level(paired, rows_first, rows_second, delays):
    lower_bands = jnp.take(paired[0::2], rows_first, axis=1)
    upper_bands = jnp.take(paired[1::2], rows_second, axis=1)
    width = paired.shape[2]
    padded = jnp.pad(upper_bands, ((0, 0), (0, 0), (SHIFT, 0)))
    columns = jnp.arange(width, dtype=jnp.int32)[None, :] + SHIFT - delays.astype(jnp.int32)[:, None]
    columns = jnp.broadcast_to(columns[None], upper_bands.shape)
    return lower_bands + jnp.take_along_axis(padded, columns, axis=2)


def reference(filterbank, first_rows, second_rows, shifts, harmonic_bins):
    layers = filterbank.astype(jnp.float32)[:, None, :]
    for level in range(LEVELS):
        count = min(2 ** (level + 1), NDM)
        layers = merge_level(layers, first_rows[level, :count], second_rows[level, :count], shifts[level, :count])
    plane = layers[0]
    spectrum = jnp.fft.rfft(plane, axis=1)[:, : TIMES // 2]
    power = (spectrum.real * spectrum.real + spectrum.imag * spectrum.imag) / (C * TIMES)
    harmonic = jnp.sum(jnp.take(power, harmonic_bins, axis=1), axis=1) / HARM
    return power, harmonic
```

```python
import math

import jax
import jax.numpy as jnp
from jax import lax
from jax.sharding import PartitionSpec as P

C = 4096
NDM = 2048
SHIFT = 16
DFT_OUTER = 64
HARM = 8
RAW_HALO = 256
SUB_HALO = 64


def shift_right(value, amount):
    width = value.shape[-1]
    pad = [(0, 0)] * (value.ndim - 1) + [(amount, 0)]
    return jnp.pad(value, pad)[..., :width]


def merge_level(paired, rows_first, rows_second, delays):
    lower_bands = jnp.take(paired[0::2], rows_first, axis=1)
    upper_bands = jnp.take(paired[1::2], rows_second, axis=1)
    delay_col = delays[None, :, None]
    shifted = upper_bands
    for bit in (1, 2, 4, 8):
        shifted = jnp.where((delay_col & bit) != 0, shift_right(shifted, bit), shifted)
    return lower_bands + shifted


def level_merge(layers, first_rows, second_rows, shifts, level):
    count = min(2 ** (level + 1), NDM)
    return merge_level(
        layers, first_rows[level, :count], second_rows[level, :count], shifts[level, :count]
    )


def spectra(series, harmonic_bins):
    count = series.shape[0]
    total = series.shape[1]
    outer = DFT_OUTER
    inner = total // outer
    half_inner = inner // 2
    highest = lax.Precision.HIGHEST
    grid = series.reshape(count, outer, inner)
    outer_index = jnp.arange(outer, dtype=jnp.int32)
    inner_index = jnp.arange(inner, dtype=jnp.int32)
    half_index = jnp.arange(half_inner, dtype=jnp.int32)
    angle_outer = (
        2.0
        * math.pi
        / outer
        * (outer_index[:, None] * outer_index[None, :] % outer).astype(jnp.float32)
    )
    outer_table = jnp.concatenate([jnp.cos(angle_outer), jnp.sin(angle_outer)], axis=1)
    section_one = jnp.einsum("npq,pk->nkq", grid, outer_table, precision=highest)
    section_re = section_one[:, :outer]
    section_im = -section_one[:, outer:]
    angle_twist = (
        2.0
        * math.pi
        / total
        * (outer_index[:, None] * inner_index[None, :] % total).astype(jnp.float32)
    )
    twist_cos = jnp.cos(angle_twist)
    twist_sin = jnp.sin(angle_twist)
    rotated = jnp.stack(
        [
            section_re * twist_cos + section_im * twist_sin,
            section_im * twist_cos - section_re * twist_sin,
        ]
    )
    angle_inner = (
        2.0
        * math.pi
        / inner
        * (inner_index[:, None] * half_index[None, :] % inner).astype(jnp.float32)
    )
    inner_table = jnp.concatenate([jnp.cos(angle_inner), jnp.sin(angle_inner)], axis=1)
    section_two = jnp.einsum("snkq,qm->snkm", rotated, inner_table, precision=highest)
    final_re = section_two[0, :, :, :half_inner] + section_two[1, :, :, half_inner:]
    final_im = section_two[1, :, :, :half_inner] - section_two[0, :, :, half_inner:]
    spectrum_power = (final_re * final_re + final_im * final_im) / (C * total)
    spectrum_power = jnp.transpose(spectrum_power, (0, 2, 1)).reshape(count, total // 2)
    harmonic = jnp.sum(jnp.take(spectrum_power, harmonic_bins, axis=1), axis=1) / HARM
    return spectrum_power, harmonic


def on_device(filterbank, first_rows, second_rows, shifts, harmonic_bins):
    channels = filterbank.shape[0]
    samples = filterbank.shape[1]
    local_levels = channels.bit_length() - 1
    chan_count = lax.axis_size("chan")
    tm_count = lax.axis_size("tm")
    cross_levels = chan_count.bit_length() - 1
    levels = local_levels + cross_levels
    rim = lax.ppermute(
        filterbank[:, samples - RAW_HALO :],
        "tm",
        [(source, source + 1) for source in range(tm_count - 1)],
    )
    widened = jnp.concatenate([rim, filterbank], axis=1)
    layers = widened.astype(jnp.float32)[:, None, :]
    for level in range(local_levels):
        layers = level_merge(layers, first_rows, second_rows, shifts, level)
    band = layers[0]
    sub = samples // chan_count
    window = sub + SUB_HALO
    base = RAW_HALO - SUB_HALO
    pieces = jnp.stack(
        [band[:, base + sub * dest : base + sub * dest + window] for dest in range(chan_count)]
    )
    layers = lax.all_to_all(pieces, "chan", split_axis=0, concat_axis=0, tiled=True)
    for level in range(local_levels, levels):
        layers = level_merge(layers, first_rows, second_rows, shifts, level)
    plane = layers[0][:, SUB_HALO:]
    groups = chan_count * tm_count
    share = NDM // groups
    outgoing = plane.reshape(groups, share, sub)
    incoming = lax.all_to_all(outgoing, ("chan", "tm"), split_axis=0, concat_axis=0, tiled=True)
    series = (
        incoming.reshape(chan_count, tm_count, share, sub)
        .transpose(2, 1, 0, 3)
        .reshape(share, tm_count * samples)
    )
    return spectra(series, harmonic_bins)


def solution(mesh):
    in_specs = (P("chan", "tm"), P(), P(), P(), P())
    out_specs = (P(("chan", "tm"), None), P(("chan", "tm"), None))
    return jax.shard_map(
        on_device, mesh=mesh, in_specs=in_specs, out_specs=out_specs, check_vma=False
    )
```

```python
import functools
import math

import jax
import jax.numpy as jnp
from jax import lax
from jax.experimental import pallas as pl
from jax.experimental.pallas import tpu as pltpu
from jax.sharding import PartitionSpec as P

C = 4096
NDM = 2048
SHIFT = 16
DFT_OUTER = 64
HARM = 8
RAW_HALO = 256
SUB_HALO = 64


def shift_right(value, amount):
    width = value.shape[-1]
    pad = [(0, 0)] * (value.ndim - 1) + [(amount, 0)]
    return jnp.pad(value, pad)[..., :width]


def merge_level(paired, rows_first, rows_second, delays):
    lower_bands = jnp.take(paired[0::2], rows_first, axis=1)
    upper_bands = jnp.take(paired[1::2], rows_second, axis=1)
    delay_col = delays[None, :, None]
    shifted = upper_bands
    for bit in (1, 2, 4, 8):
        shifted = jnp.where((delay_col & bit) != 0, shift_right(shifted, bit), shifted)
    return lower_bands + shifted


def level_merge(layers, first_rows, second_rows, shifts, level):
    count = min(2 ** (level + 1), NDM)
    return merge_level(
        layers, first_rows[level, :count], second_rows[level, :count], shifts[level, :count]
    )


def levels_kernel(plan, first_ref, second_ref, shift_ref, x_ref, out_ref, buf_a, buf_b):
    source = x_ref
    for step, (row_in, row_out, rows_total) in enumerate(plan):
        target = out_ref if step == len(plan) - 1 else (buf_a, buf_b)[step % 2]
        log_out = row_out.bit_length() - 1

        def body(out_row, carry, source=source, target=target, step=step,
                 row_in=row_in, row_out=row_out, log_out=log_out):
            band = lax.shift_right_logical(out_row, log_out)
            row = lax.bitwise_and(out_row, row_out - 1)
            low = 2 * band * row_in + first_ref[step, row]
            high = (2 * band + 1) * row_in + second_ref[step, row]
            amount = shift_ref[step, row]
            lower = source[pl.ds(low, 1), :]
            upper = source[pl.ds(high, 1), :]
            target[pl.ds(out_row, 1), :] = lower + pltpu.roll(upper, amount, 1)
            return carry

        lax.fori_loop(0, rows_total, body, 0, unroll=8)
        source = target


def run_levels(state, first_rows, second_rows, shifts, plan):
    rows, width = state.shape
    out_rows = plan[-1][2]
    buf_rows = max(p[2] for p in plan)
    smem = pl.BlockSpec(memory_space=pltpu.SMEM)
    vmem = pl.BlockSpec(memory_space=pltpu.VMEM)
    return pl.pallas_call(
        functools.partial(levels_kernel, plan),
        out_shape=jax.ShapeDtypeStruct((out_rows, width), jnp.float32),
        in_specs=[smem, smem, smem, vmem],
        out_specs=vmem,
        scratch_shapes=[pltpu.VMEM((buf_rows, width), jnp.float32)] * 2,
        compiler_params=pltpu.CompilerParams(vmem_limit_bytes=48 * 1024 * 1024),
    )(first_rows, second_rows, shifts, state)


def spectra(series, harmonic_bins):
    count = series.shape[0]
    total = series.shape[1]
    outer = DFT_OUTER
    inner = total // outer
    half_inner = inner // 2
    highest = lax.Precision.HIGHEST
    grid = series.reshape(count, outer, inner)
    outer_index = jnp.arange(outer, dtype=jnp.int32)
    inner_index = jnp.arange(inner, dtype=jnp.int32)
    half_index = jnp.arange(half_inner, dtype=jnp.int32)
    angle_outer = (
        2.0
        * math.pi
        / outer
        * (outer_index[:, None] * outer_index[None, :] % outer).astype(jnp.float32)
    )
    outer_table = jnp.concatenate([jnp.cos(angle_outer), jnp.sin(angle_outer)], axis=1)
    section_one = jnp.einsum("npq,pk->nkq", grid, outer_table, precision=highest)
    section_re = section_one[:, :outer]
    section_im = -section_one[:, outer:]
    angle_twist = (
        2.0
        * math.pi
        / total
        * (outer_index[:, None] * inner_index[None, :] % total).astype(jnp.float32)
    )
    twist_cos = jnp.cos(angle_twist)
    twist_sin = jnp.sin(angle_twist)
    rotated = jnp.stack(
        [
            section_re * twist_cos + section_im * twist_sin,
            section_im * twist_cos - section_re * twist_sin,
        ]
    )
    angle_inner = (
        2.0
        * math.pi
        / inner
        * (inner_index[:, None] * half_index[None, :] % inner).astype(jnp.float32)
    )
    inner_table = jnp.concatenate([jnp.cos(angle_inner), jnp.sin(angle_inner)], axis=1)
    section_two = jnp.einsum("snkq,qm->snkm", rotated, inner_table, precision=highest)
    final_re = section_two[0, :, :, :half_inner] + section_two[1, :, :, half_inner:]
    final_im = section_two[1, :, :, :half_inner] - section_two[0, :, :, half_inner:]
    spectrum_power = (final_re * final_re + final_im * final_im) / (C * total)
    spectrum_power = jnp.transpose(spectrum_power, (0, 2, 1)).reshape(count, total // 2)
    harmonic = jnp.sum(jnp.take(spectrum_power, harmonic_bins, axis=1), axis=1) / HARM
    return spectrum_power, harmonic


def on_device(filterbank, first_rows, second_rows, shifts, harmonic_bins):
    channels = filterbank.shape[0]
    samples = filterbank.shape[1]
    local_levels = channels.bit_length() - 1
    chan_count = lax.axis_size("chan")
    tm_count = lax.axis_size("tm")
    cross_levels = chan_count.bit_length() - 1
    levels = local_levels + cross_levels
    rim = lax.ppermute(
        filterbank[:, samples - RAW_HALO :],
        "tm",
        [(source, source + 1) for source in range(tm_count - 1)],
    )
    widened = jnp.concatenate([rim, filterbank], axis=1)
    local_plan = [(2**level, 2 ** (level + 1), channels) for level in range(local_levels)]
    band = run_levels(
        widened.astype(jnp.float32),
        first_rows[:local_levels, :channels],
        second_rows[:local_levels, :channels],
        shifts[:local_levels, :channels],
        local_plan,
    )
    sub = samples // chan_count
    window = sub + SUB_HALO
    base = RAW_HALO - SUB_HALO
    pieces = jnp.stack(
        [band[:, base + sub * dest : base + sub * dest + window] for dest in range(chan_count)]
    )
    layers = lax.all_to_all(pieces, "chan", split_axis=0, concat_axis=0, tiled=True)
    cross_plan = []
    bands = chan_count
    for level in range(local_levels, levels):
        bands //= 2
        rows_out = min(2 ** (level + 1), NDM)
        cross_plan.append((min(2**level, NDM), rows_out, bands * rows_out))
    plane = run_levels(
        layers.reshape(chan_count * channels, window),
        first_rows[local_levels:],
        second_rows[local_levels:],
        shifts[local_levels:],
        cross_plan,
    )[:, SUB_HALO:]
    groups = chan_count * tm_count
    share = NDM // groups
    outgoing = plane.reshape(groups, share, sub)
    incoming = lax.all_to_all(outgoing, ("chan", "tm"), split_axis=0, concat_axis=0, tiled=True)
    series = (
        incoming.reshape(chan_count, tm_count, share, sub)
        .transpose(2, 1, 0, 3)
        .reshape(share, tm_count * samples)
    )
    return spectra(series, harmonic_bins)


def solution(mesh):
    in_specs = (P("chan", "tm"), P(), P(), P(), P())
    out_specs = (P(("chan", "tm"), None), P(("chan", "tm"), None))
    return jax.shard_map(
        on_device, mesh=mesh, in_specs=in_specs, out_specs=out_specs, check_vma=False
    )
```

```python
import functools
import math

import jax
import jax.numpy as jnp
from jax import lax
from jax.experimental import pallas as pl
from jax.experimental.pallas import tpu as pltpu
from jax.sharding import PartitionSpec as P

C = 4096
NDM = 2048
SHIFT = 16
DFT_OUTER = 64
HARM = 8
RAW_HALO = 256
SUB_HALO = 64
TILE = 256


def shift_right(value, amount):
    width = value.shape[-1]
    pad = [(0, 0)] * (value.ndim - 1) + [(amount, 0)]
    return jnp.pad(value, pad)[..., :width]


def merge_level(paired, rows_first, rows_second, delays):
    lower_bands = jnp.take(paired[0::2], rows_first, axis=1)
    upper_bands = jnp.take(paired[1::2], rows_second, axis=1)
    delay_col = delays[None, :, None]
    shifted = upper_bands
    for bit in (1, 2, 4, 8):
        shifted = jnp.where((delay_col & bit) != 0, shift_right(shifted, bit), shifted)
    return lower_bands + shifted


def level_merge(layers, first_rows, second_rows, shifts, level):
    count = min(2 ** (level + 1), NDM)
    return merge_level(
        layers, first_rows[level, :count], second_rows[level, :count], shifts[level, :count]
    )


def levels_kernel(plan, first_ref, second_ref, shift_ref, x_ref, out_ref, buf_a, buf_b):
    source = x_ref
    for step, (row_in, row_out, rows_total) in enumerate(plan):
        target = out_ref if step == len(plan) - 1 else (buf_a, buf_b)[step % 2]
        log_out = row_out.bit_length() - 1

        def body(out_row, carry, source=source, target=target, step=step,
                 row_in=row_in, row_out=row_out, log_out=log_out):
            band = lax.shift_right_logical(out_row, log_out)
            row = lax.bitwise_and(out_row, row_out - 1)
            low = 2 * band * row_in + first_ref[step, row]
            high = (2 * band + 1) * row_in + second_ref[step, row]
            amount = shift_ref[step, row]
            lower = source[pl.ds(low, 1), :]
            upper = source[pl.ds(high, 1), :]
            target[pl.ds(out_row, 1), :] = lower + pltpu.roll(upper, amount, 1)
            return carry

        lax.fori_loop(0, rows_total, body, 0, unroll=8)
        source = target


def run_levels(state, first_rows, second_rows, shifts, plan):
    rows, width = state.shape
    out_rows = plan[-1][2]
    buf_rows = max(p[2] for p in plan)
    smem = pl.BlockSpec(memory_space=pltpu.SMEM)
    vmem = pl.BlockSpec(memory_space=pltpu.VMEM)
    return pl.pallas_call(
        functools.partial(levels_kernel, plan),
        out_shape=jax.ShapeDtypeStruct((out_rows, width), jnp.float32),
        in_specs=[smem, smem, smem, vmem],
        out_specs=vmem,
        scratch_shapes=[pltpu.VMEM((buf_rows, width), jnp.float32)] * 2,
        compiler_params=pltpu.CompilerParams(vmem_limit_bytes=48 * 1024 * 1024),
    )(first_rows, second_rows, shifts, state)


def split_three(block):
    high = block.astype(jnp.bfloat16)
    rest = block - high.astype(jnp.float32)
    middle = rest.astype(jnp.bfloat16)
    low = (rest - middle.astype(jnp.float32)).astype(jnp.bfloat16)
    return high, middle, low


def matmul_kernel(plan, x_ref, *refs):
    count = len(plan)
    tables = refs[: 3 * count]
    out_ref, buf_a, buf_b, parts = refs[3 * count :]
    source = x_ref
    for step, (row_in, row_out, bands_out, depth) in enumerate(plan):
        pick_low, pick_high, delay = tables[3 * step : 3 * step + 3]
        target = out_ref if step == count - 1 else (buf_a, buf_b)[step % 2]
        for band in range(bands_out):
            for side in range(2):
                block = source[pl.ds((2 * band + side) * row_in, depth), :]
                for piece, value in enumerate(split_three(block)):
                    parts[side, piece, pl.ds(0, depth), :] = value

            def tile(index, carry, target=target, band=band, depth=depth, row_out=row_out,
                     pick_low=pick_low, pick_high=pick_high, delay=delay):
                rows = pl.ds(pl.multiple_of(index * TILE, TILE), TILE)
                low_sel = pick_low[rows, :]
                high_sel = pick_high[rows, :]
                lower = None
                upper = None
                for piece in range(3):
                    term = jnp.dot(low_sel, parts[0, piece, pl.ds(0, depth), :],
                                   preferred_element_type=jnp.float32)
                    lower = term if lower is None else lower + term
                    term = jnp.dot(high_sel, parts[1, piece, pl.ds(0, depth), :],
                                   preferred_element_type=jnp.float32)
                    upper = term if upper is None else upper + term
                amount = delay[rows, :]
                for bit in (1, 2, 4, 8):
                    upper = jnp.where((amount & bit) != 0, pltpu.roll(upper, bit, 1), upper)
                start = pl.multiple_of(band * row_out + index * TILE, TILE)
                target[pl.ds(start, TILE), :] = lower + upper
                return carry

            lax.fori_loop(0, row_out // TILE, tile, 0)
        source = target


def run_matmul_levels(state, first_rows, second_rows, shifts, levels, plan):
    width = state.shape[1]
    tables = []
    for level, (row_in, row_out, bands_out, depth) in zip(levels, plan):
        columns = jnp.arange(depth, dtype=jnp.int32)[None, :]
        tables.append((first_rows[level, :row_out, None] == columns).astype(jnp.bfloat16))
        tables.append((second_rows[level, :row_out, None] == columns).astype(jnp.bfloat16))
        tables.append(shifts[level, :row_out, None])
    buf_rows = max(p[1] * p[2] for p in plan)
    depth_most = max(p[3] for p in plan)
    vmem = pl.BlockSpec(memory_space=pltpu.VMEM)
    return pl.pallas_call(
        functools.partial(matmul_kernel, plan),
        out_shape=jax.ShapeDtypeStruct((plan[-1][1] * plan[-1][2], width), jnp.float32),
        in_specs=[vmem] * (1 + len(tables)),
        out_specs=vmem,
        scratch_shapes=[
            pltpu.VMEM((buf_rows, width), jnp.float32),
            pltpu.VMEM((buf_rows, width), jnp.float32),
            pltpu.VMEM((2, 3, depth_most, width), jnp.bfloat16),
        ],
        compiler_params=pltpu.CompilerParams(vmem_limit_bytes=60 * 1024 * 1024),
    )(state, *tables)


def spectra(series, harmonic_bins):
    count = series.shape[0]
    total = series.shape[1]
    outer = DFT_OUTER
    inner = total // outer
    half_inner = inner // 2
    highest = lax.Precision.HIGHEST
    grid = series.reshape(count, outer, inner)
    outer_index = jnp.arange(outer, dtype=jnp.int32)
    inner_index = jnp.arange(inner, dtype=jnp.int32)
    half_index = jnp.arange(half_inner, dtype=jnp.int32)
    angle_outer = (
        2.0
        * math.pi
        / outer
        * (outer_index[:, None] * outer_index[None, :] % outer).astype(jnp.float32)
    )
    outer_table = jnp.concatenate([jnp.cos(angle_outer), jnp.sin(angle_outer)], axis=1)
    section_one = jnp.einsum("npq,pk->nkq", grid, outer_table, precision=highest)
    section_re = section_one[:, :outer]
    section_im = -section_one[:, outer:]
    angle_twist = (
        2.0
        * math.pi
        / total
        * (outer_index[:, None] * inner_index[None, :] % total).astype(jnp.float32)
    )
    twist_cos = jnp.cos(angle_twist)
    twist_sin = jnp.sin(angle_twist)
    rotated = jnp.stack(
        [
            section_re * twist_cos + section_im * twist_sin,
            section_im * twist_cos - section_re * twist_sin,
        ]
    )
    angle_inner = (
        2.0
        * math.pi
        / inner
        * (inner_index[:, None] * half_index[None, :] % inner).astype(jnp.float32)
    )
    inner_table = jnp.concatenate([jnp.cos(angle_inner), jnp.sin(angle_inner)], axis=1)
    section_two = jnp.einsum("snkq,qm->snkm", rotated, inner_table, precision=highest)
    final_re = section_two[0, :, :, :half_inner] + section_two[1, :, :, half_inner:]
    final_im = section_two[1, :, :, :half_inner] - section_two[0, :, :, half_inner:]
    spectrum_power = (final_re * final_re + final_im * final_im) / (C * total)
    spectrum_power = jnp.transpose(spectrum_power, (0, 2, 1)).reshape(count, total // 2)
    harmonic = jnp.sum(jnp.take(spectrum_power, harmonic_bins, axis=1), axis=1) / HARM
    return spectrum_power, harmonic


def on_device(filterbank, first_rows, second_rows, shifts, harmonic_bins):
    channels = filterbank.shape[0]
    samples = filterbank.shape[1]
    local_levels = channels.bit_length() - 1
    chan_count = lax.axis_size("chan")
    tm_count = lax.axis_size("tm")
    cross_levels = chan_count.bit_length() - 1
    levels = local_levels + cross_levels
    rim = lax.ppermute(
        filterbank[:, samples - RAW_HALO :],
        "tm",
        [(source, source + 1) for source in range(tm_count - 1)],
    )
    widened = jnp.concatenate([rim, filterbank], axis=1)
    local_plan = [(2**level, 2 ** (level + 1), channels) for level in range(local_levels)]
    band = run_levels(
        widened.astype(jnp.float32),
        first_rows[:local_levels, :channels],
        second_rows[:local_levels, :channels],
        shifts[:local_levels, :channels],
        local_plan,
    )
    sub = samples // chan_count
    window = sub + SUB_HALO
    base = RAW_HALO - SUB_HALO
    pieces = jnp.stack(
        [band[:, base + sub * dest : base + sub * dest + window] for dest in range(chan_count)]
    )
    layers = lax.all_to_all(pieces, "chan", split_axis=0, concat_axis=0, tiled=True)
    cross_plan = []
    bands = chan_count
    for level in range(local_levels, levels):
        bands //= 2
        rows_in = min(2**level, NDM)
        cross_plan.append((rows_in, min(2 ** (level + 1), NDM), bands, min(rows_in, NDM // 2)))
    plane = run_matmul_levels(
        layers.reshape(chan_count * channels, window),
        first_rows,
        second_rows,
        shifts,
        list(range(local_levels, levels)),
        cross_plan,
    )[:, SUB_HALO:]
    groups = chan_count * tm_count
    share = NDM // groups
    outgoing = plane.reshape(groups, share, sub)
    incoming = lax.all_to_all(outgoing, ("chan", "tm"), split_axis=0, concat_axis=0, tiled=True)
    series = (
        incoming.reshape(chan_count, tm_count, share, sub)
        .transpose(2, 1, 0, 3)
        .reshape(share, tm_count * samples)
    )
    return spectra(series, harmonic_bins)


def solution(mesh):
    in_specs = (P("chan", "tm"), P(), P(), P(), P())
    out_specs = (P(("chan", "tm"), None), P(("chan", "tm"), None))
    return jax.shard_map(
        on_device, mesh=mesh, in_specs=in_specs, out_specs=out_specs, check_vma=False
    )
```

```python
import functools
import math

import jax
import jax.numpy as jnp
from jax import lax
from jax.experimental import pallas as pl
from jax.experimental.pallas import tpu as pltpu
from jax.sharding import PartitionSpec as P

C = 4096
NDM = 2048
SHIFT = 16
DFT_OUTER = 64
HARM = 8
RAW_HALO = 256
SUB_HALO = 64
TILE = 256


def shift_right(value, amount):
    width = value.shape[-1]
    pad = [(0, 0)] * (value.ndim - 1) + [(amount, 0)]
    return jnp.pad(value, pad)[..., :width]


def merge_level(paired, rows_first, rows_second, delays):
    lower_bands = jnp.take(paired[0::2], rows_first, axis=1)
    upper_bands = jnp.take(paired[1::2], rows_second, axis=1)
    delay_col = delays[None, :, None]
    shifted = upper_bands
    for bit in (1, 2, 4, 8):
        shifted = jnp.where((delay_col & bit) != 0, shift_right(shifted, bit), shifted)
    return lower_bands + shifted


def level_merge(layers, first_rows, second_rows, shifts, level):
    count = min(2 ** (level + 1), NDM)
    return merge_level(
        layers, first_rows[level, :count], second_rows[level, :count], shifts[level, :count]
    )


def levels_kernel(plan, first_ref, second_ref, shift_ref, x_ref, out_ref, buf_a, buf_b):
    source = x_ref
    for step, (row_in, row_out, rows_total) in enumerate(plan):
        target = out_ref if step == len(plan) - 1 else (buf_a, buf_b)[step % 2]
        log_out = row_out.bit_length() - 1

        def body(out_row, carry, source=source, target=target, step=step,
                 row_in=row_in, row_out=row_out, log_out=log_out):
            band = lax.shift_right_logical(out_row, log_out)
            row = lax.bitwise_and(out_row, row_out - 1)
            low = 2 * band * row_in + first_ref[step, row]
            high = (2 * band + 1) * row_in + second_ref[step, row]
            amount = shift_ref[step, row]
            lower = source[pl.ds(low, 1), :]
            upper = source[pl.ds(high, 1), :]
            target[pl.ds(out_row, 1), :] = lower + pltpu.roll(upper, amount, 1)
            return carry

        lax.fori_loop(0, rows_total, body, 0, unroll=8)
        source = target


def run_levels(state, first_rows, second_rows, shifts, plan):
    rows, width = state.shape
    out_rows = plan[-1][2]
    buf_rows = max(p[2] for p in plan)
    smem = pl.BlockSpec(memory_space=pltpu.SMEM)
    vmem = pl.BlockSpec(memory_space=pltpu.VMEM)
    return pl.pallas_call(
        functools.partial(levels_kernel, plan),
        out_shape=jax.ShapeDtypeStruct((out_rows, width), jnp.float32),
        in_specs=[smem, smem, smem, vmem],
        out_specs=vmem,
        scratch_shapes=[pltpu.VMEM((buf_rows, width), jnp.float32)] * 2,
        compiler_params=pltpu.CompilerParams(vmem_limit_bytes=48 * 1024 * 1024),
    )(first_rows, second_rows, shifts, state)


def split_three(block):
    high = block.astype(jnp.bfloat16)
    rest = block - high.astype(jnp.float32)
    middle = rest.astype(jnp.bfloat16)
    low = (rest - middle.astype(jnp.float32)).astype(jnp.bfloat16)
    return high, middle, low


def matmul_kernel(plan, x_ref, *refs):
    count = len(plan)
    tables = refs[: 3 * count]
    out_ref, buf_a, buf_b, parts = refs[3 * count :]
    width = x_ref.shape[1]
    source = x_ref
    for step, (row_in, row_out, bands_out, depth) in enumerate(plan):
        pick_low, pick_high, delay = tables[3 * step : 3 * step + 3]
        target = out_ref if step == count - 1 else (buf_a, buf_b)[step % 2]
        group = 2 if bands_out >= 2 else 1
        lanes = group * width
        for first_band in range(0, bands_out, group):
            for member in range(group):
                band = first_band + member
                for side in range(2):
                    block = source[pl.ds((2 * band + side) * row_in, depth), :]
                    for piece, value in enumerate(split_three(block)):
                        parts[side, piece, pl.ds(0, depth), pl.ds(member * width, width)] = value

            def tile(index, carry, target=target, first_band=first_band, depth=depth,
                     row_out=row_out, group=group, lanes=lanes,
                     pick_low=pick_low, pick_high=pick_high, delay=delay):
                rows = pl.ds(pl.multiple_of(index * TILE, TILE), TILE)
                low_sel = pick_low[rows, :]
                high_sel = pick_high[rows, :]
                lower = None
                upper = None
                for piece in range(3):
                    term = jnp.dot(low_sel, parts[0, piece, pl.ds(0, depth), pl.ds(0, lanes)],
                                   preferred_element_type=jnp.float32)
                    lower = term if lower is None else lower + term
                    term = jnp.dot(high_sel, parts[1, piece, pl.ds(0, depth), pl.ds(0, lanes)],
                                   preferred_element_type=jnp.float32)
                    upper = term if upper is None else upper + term
                amount = delay[rows, :]
                for bit in (1, 2, 4, 8):
                    upper = jnp.where((amount & bit) != 0, pltpu.roll(upper, bit, 1), upper)
                merged = lower + upper
                for member in range(group):
                    start = pl.multiple_of((first_band + member) * row_out + index * TILE, TILE)
                    target[pl.ds(start, TILE), :] = merged[:, member * width : (member + 1) * width]
                return carry

            lax.fori_loop(0, row_out // TILE, tile, 0)
        source = target


def run_matmul_levels(state, first_rows, second_rows, shifts, levels, plan):
    width = state.shape[1]
    tables = []
    for level, (row_in, row_out, bands_out, depth) in zip(levels, plan):
        columns = jnp.arange(depth, dtype=jnp.int32)[None, :]
        tables.append((first_rows[level, :row_out, None] == columns).astype(jnp.bfloat16))
        tables.append((second_rows[level, :row_out, None] == columns).astype(jnp.bfloat16))
        tables.append(shifts[level, :row_out, None])
    buf_rows = max(p[1] * p[2] for p in plan)
    depth_most = max(p[3] for p in plan)
    vmem = pl.BlockSpec(memory_space=pltpu.VMEM)
    return pl.pallas_call(
        functools.partial(matmul_kernel, plan),
        out_shape=jax.ShapeDtypeStruct((plan[-1][1] * plan[-1][2], width), jnp.float32),
        in_specs=[vmem] * (1 + len(tables)),
        out_specs=vmem,
        scratch_shapes=[
            pltpu.VMEM((buf_rows, width), jnp.float32),
            pltpu.VMEM((buf_rows, width), jnp.float32),
            pltpu.VMEM((2, 3, depth_most, 2 * width), jnp.bfloat16),
        ],
        compiler_params=pltpu.CompilerParams(vmem_limit_bytes=60 * 1024 * 1024),
    )(state, *tables)


def spectra(series, harmonic_bins):
    count = series.shape[0]
    total = series.shape[1]
    outer = DFT_OUTER
    inner = total // outer
    half_inner = inner // 2
    highest = lax.Precision.HIGHEST
    grid = series.reshape(count, outer, inner)
    outer_index = jnp.arange(outer, dtype=jnp.int32)
    inner_index = jnp.arange(inner, dtype=jnp.int32)
    half_index = jnp.arange(half_inner, dtype=jnp.int32)
    angle_outer = (
        2.0
        * math.pi
        / outer
        * (outer_index[:, None] * outer_index[None, :] % outer).astype(jnp.float32)
    )
    outer_table = jnp.concatenate([jnp.cos(angle_outer), jnp.sin(angle_outer)], axis=1)
    section_one = jnp.einsum("npq,pk->nkq", grid, outer_table, precision=highest)
    section_re = section_one[:, :outer]
    section_im = -section_one[:, outer:]
    angle_twist = (
        2.0
        * math.pi
        / total
        * (outer_index[:, None] * inner_index[None, :] % total).astype(jnp.float32)
    )
    twist_cos = jnp.cos(angle_twist)
    twist_sin = jnp.sin(angle_twist)
    rotated = jnp.stack(
        [
            section_re * twist_cos + section_im * twist_sin,
            section_im * twist_cos - section_re * twist_sin,
        ]
    )
    angle_inner = (
        2.0
        * math.pi
        / inner
        * (inner_index[:, None] * half_index[None, :] % inner).astype(jnp.float32)
    )
    inner_table = jnp.concatenate([jnp.cos(angle_inner), jnp.sin(angle_inner)], axis=1)
    section_two = jnp.einsum("snkq,qm->snkm", rotated, inner_table, precision=highest)
    final_re = section_two[0, :, :, :half_inner] + section_two[1, :, :, half_inner:]
    final_im = section_two[1, :, :, :half_inner] - section_two[0, :, :, half_inner:]
    spectrum_power = (final_re * final_re + final_im * final_im) / (C * total)
    spectrum_power = jnp.transpose(spectrum_power, (0, 2, 1)).reshape(count, total // 2)
    harmonic = jnp.sum(jnp.take(spectrum_power, harmonic_bins, axis=1), axis=1) / HARM
    return spectrum_power, harmonic


def on_device(filterbank, first_rows, second_rows, shifts, harmonic_bins):
    channels = filterbank.shape[0]
    samples = filterbank.shape[1]
    local_levels = channels.bit_length() - 1
    chan_count = lax.axis_size("chan")
    tm_count = lax.axis_size("tm")
    cross_levels = chan_count.bit_length() - 1
    levels = local_levels + cross_levels
    rim = lax.ppermute(
        filterbank[:, samples - RAW_HALO :],
        "tm",
        [(source, source + 1) for source in range(tm_count - 1)],
    )
    widened = jnp.concatenate([rim, filterbank], axis=1)
    local_plan = [(2**level, 2 ** (level + 1), channels) for level in range(local_levels)]
    band = run_levels(
        widened.astype(jnp.float32),
        first_rows[:local_levels, :channels],
        second_rows[:local_levels, :channels],
        shifts[:local_levels, :channels],
        local_plan,
    )
    sub = samples // chan_count
    window = sub + SUB_HALO
    base = RAW_HALO - SUB_HALO
    pieces = jnp.stack(
        [band[:, base + sub * dest : base + sub * dest + window] for dest in range(chan_count)]
    )
    layers = lax.all_to_all(pieces, "chan", split_axis=0, concat_axis=0, tiled=True)
    cross_plan = []
    bands = chan_count
    for level in range(local_levels, levels):
        bands //= 2
        rows_in = min(2**level, NDM)
        cross_plan.append((rows_in, min(2 ** (level + 1), NDM), bands, min(rows_in, NDM // 2)))
    plane = run_matmul_levels(
        layers.reshape(chan_count * channels, window),
        first_rows,
        second_rows,
        shifts,
        list(range(local_levels, levels)),
        cross_plan,
    )[:, SUB_HALO:]
    groups = chan_count * tm_count
    share = NDM // groups
    outgoing = plane.reshape(groups, share, sub)
    incoming = lax.all_to_all(outgoing, ("chan", "tm"), split_axis=0, concat_axis=0, tiled=True)
    series = (
        incoming.reshape(chan_count, tm_count, share, sub)
        .transpose(2, 1, 0, 3)
        .reshape(share, tm_count * samples)
    )
    return spectra(series, harmonic_bins)


def solution(mesh):
    in_specs = (P("chan", "tm"), P(), P(), P(), P())
    out_specs = (P(("chan", "tm"), None), P(("chan", "tm"), None))
    return jax.shard_map(
        on_device, mesh=mesh, in_specs=in_specs, out_specs=out_specs, check_vma=False
    )
```

```python
import functools
import math

import jax
import jax.numpy as jnp
from jax import lax
from jax.experimental import pallas as pl
from jax.experimental.pallas import tpu as pltpu
from jax.sharding import PartitionSpec as P

C = 4096
NDM = 2048
SHIFT = 16
DFT_OUTER = 64
HARM = 8
RAW_HALO = 256
SUB_HALO = 64
TILE = 256


def shift_right(value, amount):
    width = value.shape[-1]
    pad = [(0, 0)] * (value.ndim - 1) + [(amount, 0)]
    return jnp.pad(value, pad)[..., :width]


def merge_level(paired, rows_first, rows_second, delays):
    lower_bands = jnp.take(paired[0::2], rows_first, axis=1)
    upper_bands = jnp.take(paired[1::2], rows_second, axis=1)
    delay_col = delays[None, :, None]
    shifted = upper_bands
    for bit in (1, 2, 4, 8):
        shifted = jnp.where((delay_col & bit) != 0, shift_right(shifted, bit), shifted)
    return lower_bands + shifted


def level_merge(layers, first_rows, second_rows, shifts, level):
    count = min(2 ** (level + 1), NDM)
    return merge_level(
        layers, first_rows[level, :count], second_rows[level, :count], shifts[level, :count]
    )


def levels_kernel(plan, first_ref, second_ref, shift_ref, x_ref, out_ref, buf_a, buf_b):
    source = x_ref
    for step, (row_in, row_out, rows_total) in enumerate(plan):
        target = out_ref if step == len(plan) - 1 else (buf_a, buf_b)[step % 2]
        log_out = row_out.bit_length() - 1

        def body(out_row, carry, source=source, target=target, step=step,
                 row_in=row_in, row_out=row_out, log_out=log_out):
            band = lax.shift_right_logical(out_row, log_out)
            row = lax.bitwise_and(out_row, row_out - 1)
            low = 2 * band * row_in + first_ref[step, row]
            high = (2 * band + 1) * row_in + second_ref[step, row]
            amount = shift_ref[step, row]
            lower = source[pl.ds(low, 1), :]
            upper = source[pl.ds(high, 1), :]
            target[pl.ds(out_row, 1), :] = lower + pltpu.roll(upper, amount, 1)
            return carry

        lax.fori_loop(0, rows_total, body, 0, unroll=8)
        source = target


def run_levels(state, first_rows, second_rows, shifts, plan):
    rows, width = state.shape
    out_rows = plan[-1][2]
    buf_rows = max(p[2] for p in plan)
    smem = pl.BlockSpec(memory_space=pltpu.SMEM)
    vmem = pl.BlockSpec(memory_space=pltpu.VMEM)
    return pl.pallas_call(
        functools.partial(levels_kernel, plan),
        out_shape=jax.ShapeDtypeStruct((out_rows, width), jnp.float32),
        in_specs=[smem, smem, smem, vmem],
        out_specs=vmem,
        scratch_shapes=[pltpu.VMEM((buf_rows, width), jnp.float32)] * 2,
        compiler_params=pltpu.CompilerParams(vmem_limit_bytes=48 * 1024 * 1024),
    )(first_rows, second_rows, shifts, state)


def split_three(block):
    high = block.astype(jnp.bfloat16)
    rest = block - high.astype(jnp.float32)
    middle = rest.astype(jnp.bfloat16)
    low = (rest - middle.astype(jnp.float32)).astype(jnp.bfloat16)
    return high, middle, low


def matmul_kernel(plan, x_ref, *refs):
    count = len(plan)
    tables = refs[: 3 * count]
    out_ref, buf_a, buf_b, parts = refs[3 * count :]
    width = x_ref.shape[1]
    source = x_ref
    for step, (row_in, row_out, bands_out, depth) in enumerate(plan):
        pick_low, pick_high, delay = tables[3 * step : 3 * step + 3]
        target = out_ref if step == count - 1 else (buf_a, buf_b)[step % 2]
        group = 2 if bands_out >= 2 else 1
        lanes = group * width
        for first_band in range(0, bands_out, group):
            for member in range(group):
                band = first_band + member
                for side in range(2):
                    block = source[pl.ds((2 * band + side) * row_in, depth), :]
                    for piece, value in enumerate(split_three(block)):
                        parts[side, piece, pl.ds(0, depth), pl.ds(member * width, width)] = value

            def tile(index, carry, target=target, first_band=first_band, depth=depth,
                     row_out=row_out, group=group, lanes=lanes,
                     pick_low=pick_low, pick_high=pick_high, delay=delay):
                rows = pl.ds(pl.multiple_of(index * TILE, TILE), TILE)
                low_sel = pick_low[rows, :]
                high_sel = pick_high[rows, :]
                lower = None
                upper = None
                for piece in range(3):
                    term = jnp.dot(low_sel, parts[0, piece, pl.ds(0, depth), pl.ds(0, lanes)],
                                   preferred_element_type=jnp.float32)
                    lower = term if lower is None else lower + term
                    term = jnp.dot(high_sel, parts[1, piece, pl.ds(0, depth), pl.ds(0, lanes)],
                                   preferred_element_type=jnp.float32)
                    upper = term if upper is None else upper + term
                amount = delay[rows, :]
                for bit in (1, 2, 4, 8):
                    upper = jnp.where((amount & bit) != 0, pltpu.roll(upper, bit, 1), upper)
                merged = lower + upper
                for member in range(group):
                    start = pl.multiple_of((first_band + member) * row_out + index * TILE, TILE)
                    target[pl.ds(start, TILE), :] = merged[:, member * width : (member + 1) * width]
                return carry

            lax.fori_loop(0, row_out // TILE, tile, 0)
        source = target


def run_matmul_levels(state, first_rows, second_rows, shifts, levels, plan):
    width = state.shape[1]
    tables = []
    for level, (row_in, row_out, bands_out, depth) in zip(levels, plan):
        columns = jnp.arange(depth, dtype=jnp.int32)[None, :]
        tables.append((first_rows[level, :row_out, None] == columns).astype(jnp.bfloat16))
        tables.append((second_rows[level, :row_out, None] == columns).astype(jnp.bfloat16))
        tables.append(shifts[level, :row_out, None])
    buf_rows = max(p[1] * p[2] for p in plan)
    depth_most = max(p[3] for p in plan)
    vmem = pl.BlockSpec(memory_space=pltpu.VMEM)
    return pl.pallas_call(
        functools.partial(matmul_kernel, plan),
        out_shape=jax.ShapeDtypeStruct((plan[-1][1] * plan[-1][2], width), jnp.float32),
        in_specs=[vmem] * (1 + len(tables)),
        out_specs=vmem,
        scratch_shapes=[
            pltpu.VMEM((buf_rows, width), jnp.float32),
            pltpu.VMEM((buf_rows, width), jnp.float32),
            pltpu.VMEM((2, 3, depth_most, 2 * width), jnp.bfloat16),
        ],
        compiler_params=pltpu.CompilerParams(vmem_limit_bytes=60 * 1024 * 1024),
    )(state, *tables)


def spectra(series, harmonic_bins):
    count = series.shape[0]
    total = series.shape[1]
    outer = DFT_OUTER
    inner = total // outer
    half_inner = inner // 2
    highest = lax.Precision.HIGHEST
    grid = series.reshape(count, outer, inner)
    outer_index = jnp.arange(outer, dtype=jnp.int32)
    inner_index = jnp.arange(inner, dtype=jnp.int32)
    half_index = jnp.arange(half_inner, dtype=jnp.int32)
    angle_outer = (
        2.0
        * math.pi
        / outer
        * (outer_index[:, None] * outer_index[None, :] % outer).astype(jnp.float32)
    )
    outer_table = jnp.concatenate([jnp.cos(angle_outer), jnp.sin(angle_outer)], axis=1)
    section_one = jnp.einsum("npq,pk->nkq", grid, outer_table, precision=highest)
    section_re = section_one[:, :outer]
    section_im = -section_one[:, outer:]
    angle_twist = (
        2.0
        * math.pi
        / total
        * (outer_index[:, None] * inner_index[None, :] % total).astype(jnp.float32)
    )
    twist_cos = jnp.cos(angle_twist)
    twist_sin = jnp.sin(angle_twist)
    rotated = jnp.stack(
        [
            section_re * twist_cos + section_im * twist_sin,
            section_im * twist_cos - section_re * twist_sin,
        ]
    )
    angle_inner = (
        2.0
        * math.pi
        / inner
        * (inner_index[:, None] * half_index[None, :] % inner).astype(jnp.float32)
    )
    inner_table = jnp.concatenate([jnp.cos(angle_inner), jnp.sin(angle_inner)], axis=1)
    section_two = jnp.einsum("snkq,qm->snkm", rotated, inner_table, precision=highest)
    final_re = section_two[0, :, :, :half_inner] + section_two[1, :, :, half_inner:]
    final_im = section_two[1, :, :, :half_inner] - section_two[0, :, :, half_inner:]
    spectrum_power = (final_re * final_re + final_im * final_im) / (C * total)
    spectrum_power = jnp.transpose(spectrum_power, (0, 2, 1)).reshape(count, total // 2)
    power_t = jnp.transpose(spectrum_power)
    fundamentals = harmonic_bins.shape[1]
    fundamental = jnp.arange(fundamentals, dtype=jnp.int32)
    total_t = None
    for order in range(HARM):
        stride = order + 1
        offset = (harmonic_bins[order] - stride * fundamental)[:, None]
        for phase in range(stride):
            picked = lax.slice(
                power_t, (phase, 0), (phase + stride * (fundamentals - 1) + 1, count), (stride, 1)
            )
            term = jnp.where(offset == phase, picked, 0.0)
            total_t = term if total_t is None else total_t + term
    harmonic = jnp.transpose(total_t) / HARM
    return spectrum_power, harmonic


def on_device(filterbank, first_rows, second_rows, shifts, harmonic_bins):
    channels = filterbank.shape[0]
    samples = filterbank.shape[1]
    local_levels = channels.bit_length() - 1
    chan_count = lax.axis_size("chan")
    tm_count = lax.axis_size("tm")
    cross_levels = chan_count.bit_length() - 1
    levels = local_levels + cross_levels
    rim = lax.ppermute(
        filterbank[:, samples - RAW_HALO :],
        "tm",
        [(source, source + 1) for source in range(tm_count - 1)],
    )
    widened = jnp.concatenate([rim, filterbank], axis=1)
    local_plan = [(2**level, 2 ** (level + 1), channels) for level in range(local_levels)]
    band = run_levels(widened.astype(jnp.float32), first_rows, second_rows, shifts, local_plan)
    band, first_rows, second_rows, shifts = lax.optimization_barrier(
        (band, first_rows, second_rows, shifts)
    )
    sub = samples // chan_count
    window = sub + SUB_HALO
    base = RAW_HALO - SUB_HALO
    pieces = jnp.stack(
        [band[:, base + sub * dest : base + sub * dest + window] for dest in range(chan_count)]
    )
    layers = lax.all_to_all(pieces, "chan", split_axis=0, concat_axis=0, tiled=True)
    cross_plan = []
    bands = chan_count
    for level in range(local_levels, levels):
        bands //= 2
        rows_in = min(2**level, NDM)
        cross_plan.append((rows_in, min(2 ** (level + 1), NDM), bands, min(rows_in, NDM // 2)))
    plane = run_matmul_levels(
        layers.reshape(chan_count * channels, window),
        first_rows,
        second_rows,
        shifts,
        list(range(local_levels, levels)),
        cross_plan,
    )[:, SUB_HALO:]
    groups = chan_count * tm_count
    share = NDM // groups
    outgoing = plane.reshape(groups, share, sub)
    incoming = lax.all_to_all(outgoing, ("chan", "tm"), split_axis=0, concat_axis=0, tiled=True)
    series = (
        incoming.reshape(chan_count, tm_count, share, sub)
        .transpose(2, 1, 0, 3)
        .reshape(share, tm_count * samples)
    )
    return spectra(series, harmonic_bins)


def solution(mesh):
    in_specs = (P("chan", "tm"), P(), P(), P(), P())
    out_specs = (P(("chan", "tm"), None), P(("chan", "tm"), None))
    return jax.shard_map(
        on_device, mesh=mesh, in_specs=in_specs, out_specs=out_specs, check_vma=False
    )
```

```python
import functools
import math

import jax
import jax.numpy as jnp
from jax import lax
from jax.experimental import pallas as pl
from jax.experimental.pallas import tpu as pltpu
from jax.sharding import PartitionSpec as P

C = 4096
NDM = 2048
SHIFT = 16
DFT_OUTER = 64
HARM = 8
RAW_HALO = 256
SUB_HALO = 64
TILE = 256


def shift_right(value, amount):
    width = value.shape[-1]
    pad = [(0, 0)] * (value.ndim - 1) + [(amount, 0)]
    return jnp.pad(value, pad)[..., :width]


def merge_level(paired, rows_first, rows_second, delays):
    lower_bands = jnp.take(paired[0::2], rows_first, axis=1)
    upper_bands = jnp.take(paired[1::2], rows_second, axis=1)
    delay_col = delays[None, :, None]
    shifted = upper_bands
    for bit in (1, 2, 4, 8):
        shifted = jnp.where((delay_col & bit) != 0, shift_right(shifted, bit), shifted)
    return lower_bands + shifted


def level_merge(layers, first_rows, second_rows, shifts, level):
    count = min(2 ** (level + 1), NDM)
    return merge_level(
        layers, first_rows[level, :count], second_rows[level, :count], shifts[level, :count]
    )


def levels_kernel(plan, first_ref, second_ref, shift_ref, x_ref, out_ref, buf_a, buf_b):
    source = x_ref
    for step, (row_in, row_out, rows_total) in enumerate(plan):
        target = out_ref if step == len(plan) - 1 else (buf_a, buf_b)[step % 2]
        log_out = row_out.bit_length() - 1

        def body(out_row, carry, source=source, target=target, step=step,
                 row_in=row_in, row_out=row_out, log_out=log_out):
            band = lax.shift_right_logical(out_row, log_out)
            row = lax.bitwise_and(out_row, row_out - 1)
            low = 2 * band * row_in + first_ref[step, row]
            high = (2 * band + 1) * row_in + second_ref[step, row]
            amount = shift_ref[step, row]
            lower = source[pl.ds(low, 1), :]
            upper = source[pl.ds(high, 1), :]
            target[pl.ds(out_row, 1), :] = lower + pltpu.roll(upper, amount, 1)
            return carry

        lax.fori_loop(0, rows_total, body, 0, unroll=8)
        source = target


def run_levels(state, first_rows, second_rows, shifts, plan):
    rows, width = state.shape
    out_rows = plan[-1][2]
    buf_rows = max(p[2] for p in plan)
    smem = pl.BlockSpec(memory_space=pltpu.SMEM)
    vmem = pl.BlockSpec(memory_space=pltpu.VMEM)
    return pl.pallas_call(
        functools.partial(levels_kernel, plan),
        out_shape=jax.ShapeDtypeStruct((out_rows, width), jnp.float32),
        in_specs=[smem, smem, smem, vmem],
        out_specs=vmem,
        scratch_shapes=[pltpu.VMEM((buf_rows, width), jnp.float32)] * 2,
        compiler_params=pltpu.CompilerParams(vmem_limit_bytes=48 * 1024 * 1024),
    )(first_rows, second_rows, shifts, state)


def split_three(block):
    high = block.astype(jnp.bfloat16)
    rest = block - high.astype(jnp.float32)
    middle = rest.astype(jnp.bfloat16)
    low = (rest - middle.astype(jnp.float32)).astype(jnp.bfloat16)
    return high, middle, low


def matmul_kernel(plan, x_ref, *refs):
    count = len(plan)
    tables = refs[: 3 * count]
    out_ref, buf_a, buf_b, parts = refs[3 * count :]
    width = x_ref.shape[1]
    source = x_ref
    for step, (row_in, row_out, bands_out, depth) in enumerate(plan):
        pick_low, pick_high, delay = tables[3 * step : 3 * step + 3]
        target = out_ref if step == count - 1 else (buf_a, buf_b)[step % 2]
        group = 2 if bands_out >= 2 else 1
        lanes = group * width
        for first_band in range(0, bands_out, group):
            for member in range(group):
                band = first_band + member
                for side in range(2):
                    block = source[pl.ds((2 * band + side) * row_in, depth), :]
                    for piece, value in enumerate(split_three(block)):
                        parts[side, piece, pl.ds(0, depth), pl.ds(member * width, width)] = value

            def tile(index, carry, target=target, first_band=first_band, depth=depth,
                     row_out=row_out, group=group, lanes=lanes,
                     pick_low=pick_low, pick_high=pick_high, delay=delay):
                rows = pl.ds(pl.multiple_of(index * TILE, TILE), TILE)
                low_sel = pick_low[rows, :]
                high_sel = pick_high[rows, :]
                lower = None
                upper = None
                for piece in range(3):
                    term = jnp.dot(low_sel, parts[0, piece, pl.ds(0, depth), pl.ds(0, lanes)],
                                   preferred_element_type=jnp.float32)
                    lower = term if lower is None else lower + term
                    term = jnp.dot(high_sel, parts[1, piece, pl.ds(0, depth), pl.ds(0, lanes)],
                                   preferred_element_type=jnp.float32)
                    upper = term if upper is None else upper + term
                amount = delay[rows, :]
                for bit in (1, 2, 4, 8):
                    upper = jnp.where((amount & bit) != 0, pltpu.roll(upper, bit, 1), upper)
                merged = lower + upper
                for member in range(group):
                    start = pl.multiple_of((first_band + member) * row_out + index * TILE, TILE)
                    target[pl.ds(start, TILE), :] = merged[:, member * width : (member + 1) * width]
                return carry

            lax.fori_loop(0, row_out // TILE, tile, 0)
        source = target


def run_matmul_levels(state, first_rows, second_rows, shifts, levels, plan):
    width = state.shape[1]
    tables = []
    for level, (row_in, row_out, bands_out, depth) in zip(levels, plan):
        columns = jnp.arange(depth, dtype=jnp.int32)[None, :]
        tables.append((first_rows[level, :row_out, None] == columns).astype(jnp.bfloat16))
        tables.append((second_rows[level, :row_out, None] == columns).astype(jnp.bfloat16))
        tables.append(shifts[level, :row_out, None])
    buf_rows = max(p[1] * p[2] for p in plan)
    depth_most = max(p[3] for p in plan)
    vmem = pl.BlockSpec(memory_space=pltpu.VMEM)
    return pl.pallas_call(
        functools.partial(matmul_kernel, plan),
        out_shape=jax.ShapeDtypeStruct((plan[-1][1] * plan[-1][2], width), jnp.float32),
        in_specs=[vmem] * (1 + len(tables)),
        out_specs=vmem,
        scratch_shapes=[
            pltpu.VMEM((buf_rows, width), jnp.float32),
            pltpu.VMEM((buf_rows, width), jnp.float32),
            pltpu.VMEM((2, 3, depth_most, 2 * width), jnp.bfloat16),
        ],
        compiler_params=pltpu.CompilerParams(vmem_limit_bytes=60 * 1024 * 1024),
    )(state, *tables)


def harmonic_kernel(power_ref, offset_ref, out_ref):
    fundamentals = out_ref.shape[0]
    total = None
    for order in range(HARM):
        stride = order + 1
        offset = offset_ref[order]
        for phase in range(stride):
            picked = power_ref[pl.ds(phase, fundamentals, stride=stride), :]
            term = jnp.where(offset == phase, picked, 0.0)
            total = term if total is None else total + term
    out_ref[...] = total * (1.0 / HARM)


def spectra(series, harmonic_bins):
    count = series.shape[0]
    total = series.shape[1]
    outer = DFT_OUTER
    inner = total // outer
    half_inner = inner // 2
    highest = lax.Precision.HIGHEST
    grid = series.reshape(count, outer, inner)
    outer_index = jnp.arange(outer, dtype=jnp.int32)
    inner_index = jnp.arange(inner, dtype=jnp.int32)
    half_index = jnp.arange(half_inner, dtype=jnp.int32)
    angle_outer = (
        2.0
        * math.pi
        / outer
        * (outer_index[:, None] * outer_index[None, :] % outer).astype(jnp.float32)
    )
    outer_table = jnp.concatenate([jnp.cos(angle_outer), jnp.sin(angle_outer)], axis=1)
    section_one = jnp.einsum("npq,pk->nkq", grid, outer_table, precision=highest)
    section_re = section_one[:, :outer]
    section_im = -section_one[:, outer:]
    angle_twist = (
        2.0
        * math.pi
        / total
        * (outer_index[:, None] * inner_index[None, :] % total).astype(jnp.float32)
    )
    twist_cos = jnp.cos(angle_twist)
    twist_sin = jnp.sin(angle_twist)
    rotated = jnp.stack(
        [
            section_re * twist_cos + section_im * twist_sin,
            section_im * twist_cos - section_re * twist_sin,
        ]
    )
    angle_inner = (
        2.0
        * math.pi
        / inner
        * (inner_index[:, None] * half_index[None, :] % inner).astype(jnp.float32)
    )
    inner_table = jnp.concatenate([jnp.cos(angle_inner), jnp.sin(angle_inner)], axis=1)
    section_two = jnp.einsum("snkq,qm->snkm", rotated, inner_table, precision=highest)
    final_re = section_two[0, :, :, :half_inner] + section_two[1, :, :, half_inner:]
    final_im = section_two[1, :, :, :half_inner] - section_two[0, :, :, half_inner:]
    spectrum_power = (final_re * final_re + final_im * final_im) / (C * total)
    spectrum_power = jnp.transpose(spectrum_power, (0, 2, 1)).reshape(count, total // 2)
    fundamentals = harmonic_bins.shape[1]
    fundamental = jnp.arange(fundamentals, dtype=jnp.int32)
    stride = jnp.arange(1, HARM + 1, dtype=jnp.int32)[:, None]
    offsets = (harmonic_bins - stride * fundamental[None, :])[:, :, None]
    vmem = pl.BlockSpec(memory_space=pltpu.VMEM)
    harmonic_t = pl.pallas_call(
        harmonic_kernel,
        out_shape=jax.ShapeDtypeStruct((fundamentals, count), jnp.float32),
        in_specs=[vmem, vmem],
        out_specs=vmem,
    )(jnp.transpose(spectrum_power), offsets)
    harmonic = jnp.transpose(harmonic_t)
    return spectrum_power, harmonic


def on_device(filterbank, first_rows, second_rows, shifts, harmonic_bins):
    channels = filterbank.shape[0]
    samples = filterbank.shape[1]
    local_levels = channels.bit_length() - 1
    chan_count = lax.axis_size("chan")
    tm_count = lax.axis_size("tm")
    cross_levels = chan_count.bit_length() - 1
    levels = local_levels + cross_levels
    rim = lax.ppermute(
        filterbank[:, samples - RAW_HALO :],
        "tm",
        [(source, source + 1) for source in range(tm_count - 1)],
    )
    widened = jnp.concatenate([rim, filterbank], axis=1)
    local_plan = [(2**level, 2 ** (level + 1), channels) for level in range(local_levels)]
    band = run_levels(
        widened.astype(jnp.float32),
        first_rows[:local_levels, :channels],
        second_rows[:local_levels, :channels],
        shifts[:local_levels, :channels],
        local_plan,
    )
    band, first_rows, second_rows, shifts = lax.optimization_barrier(
        (band, first_rows, second_rows, shifts)
    )
    sub = samples // chan_count
    window = sub + SUB_HALO
    base = RAW_HALO - SUB_HALO
    pieces = jnp.stack(
        [band[:, base + sub * dest : base + sub * dest + window] for dest in range(chan_count)]
    )
    layers = lax.all_to_all(pieces, "chan", split_axis=0, concat_axis=0, tiled=True)
    cross_plan = []
    bands = chan_count
    for level in range(local_levels, levels):
        bands //= 2
        rows_in = min(2**level, NDM)
        cross_plan.append((rows_in, min(2 ** (level + 1), NDM), bands, min(rows_in, NDM // 2)))
    plane = run_matmul_levels(
        layers.reshape(chan_count * channels, window),
        first_rows,
        second_rows,
        shifts,
        list(range(local_levels, levels)),
        cross_plan,
    )[:, SUB_HALO:]
    groups = chan_count * tm_count
    share = NDM // groups
    outgoing = plane.reshape(groups, share, sub)
    incoming = lax.all_to_all(outgoing, ("chan", "tm"), split_axis=0, concat_axis=0, tiled=True)
    series = (
        incoming.reshape(chan_count, tm_count, share, sub)
        .transpose(2, 1, 0, 3)
        .reshape(share, tm_count * samples)
    )
    return spectra(series, harmonic_bins)


def solution(mesh):
    in_specs = (P("chan", "tm"), P(), P(), P(), P())
    out_specs = (P(("chan", "tm"), None), P(("chan", "tm"), None))
    return jax.shard_map(
        on_device, mesh=mesh, in_specs=in_specs, out_specs=out_specs, check_vma=False
    )
```

```python
import functools
import math

import jax
import jax.numpy as jnp
from jax import lax
from jax.experimental import pallas as pl
from jax.experimental.pallas import tpu as pltpu
from jax.sharding import PartitionSpec as P

C = 4096
NDM = 2048
SHIFT = 16
DFT_OUTER = 64
HARM = 8
RAW_HALO = 256
SUB_HALO = 64
TILE = 256
LANES = 128


def shift_right(value, amount):
    width = value.shape[-1]
    pad = [(0, 0)] * (value.ndim - 1) + [(amount, 0)]
    return jnp.pad(value, pad)[..., :width]


def merge_level(paired, rows_first, rows_second, delays):
    lower_bands = jnp.take(paired[0::2], rows_first, axis=1)
    upper_bands = jnp.take(paired[1::2], rows_second, axis=1)
    delay_col = delays[None, :, None]
    shifted = upper_bands
    for bit in (1, 2, 4, 8):
        shifted = jnp.where((delay_col & bit) != 0, shift_right(shifted, bit), shifted)
    return lower_bands + shifted


def level_merge(layers, first_rows, second_rows, shifts, level):
    count = min(2 ** (level + 1), NDM)
    return merge_level(
        layers, first_rows[level, :count], second_rows[level, :count], shifts[level, :count]
    )


def split_three(block):
    high = block.astype(jnp.bfloat16)
    rest = block - high.astype(jnp.float32)
    middle = rest.astype(jnp.bfloat16)
    low = (rest - middle.astype(jnp.float32)).astype(jnp.bfloat16)
    return high, middle, low


def matmul_kernel(plan, x_ref, *refs):
    count = len(plan)
    tables = refs[: 3 * count]
    out_ref, buf_a, buf_b, parts = refs[3 * count :]
    width = x_ref.shape[1]
    source = x_ref
    for step, (row_in, row_out, bands_out, depth) in enumerate(plan):
        pick_low, pick_high, delay = tables[3 * step : 3 * step + 3]
        target = out_ref if step == count - 1 else (buf_a, buf_b)[step % 2]
        group = 2 if bands_out >= 2 else 1
        lanes = group * width
        for first_band in range(0, bands_out, group):
            for member in range(group):
                band = first_band + member
                for side in range(2):
                    block = source[pl.ds((2 * band + side) * row_in, depth), :]
                    for piece, value in enumerate(split_three(block)):
                        parts[side, piece, pl.ds(0, depth), pl.ds(member * width, width)] = value

            def tile(index, carry, target=target, first_band=first_band, depth=depth,
                     row_out=row_out, group=group, lanes=lanes,
                     pick_low=pick_low, pick_high=pick_high, delay=delay):
                rows = pl.ds(pl.multiple_of(index * TILE, TILE), TILE)
                low_sel = pick_low[rows, :]
                high_sel = pick_high[rows, :]
                lower = None
                upper = None
                for piece in range(3):
                    term = jnp.dot(low_sel, parts[0, piece, pl.ds(0, depth), pl.ds(0, lanes)],
                                   preferred_element_type=jnp.float32)
                    lower = term if lower is None else lower + term
                    term = jnp.dot(high_sel, parts[1, piece, pl.ds(0, depth), pl.ds(0, lanes)],
                                   preferred_element_type=jnp.float32)
                    upper = term if upper is None else upper + term
                amount = delay[rows, :]
                for bit in (1, 2, 4, 8):
                    upper = jnp.where((amount & bit) != 0, pltpu.roll(upper, bit, 1), upper)
                merged = lower + upper
                for member in range(group):
                    start = pl.multiple_of((first_band + member) * row_out + index * TILE, TILE)
                    target[pl.ds(start, TILE), :] = merged[:, member * width : (member + 1) * width]
                return carry

            lax.fori_loop(0, row_out // TILE, tile, 0)
        source = target


def run_matmul_levels(state, first_rows, second_rows, shifts, levels, plan):
    width = state.shape[1]
    tables = []
    for level, (row_in, row_out, bands_out, depth) in zip(levels, plan):
        columns = jnp.arange(depth, dtype=jnp.int32)[None, :]
        tables.append((first_rows[level, :row_out, None] == columns).astype(jnp.bfloat16))
        tables.append((second_rows[level, :row_out, None] == columns).astype(jnp.bfloat16))
        tables.append(shifts[level, :row_out, None])
    buf_rows = max(p[1] * p[2] for p in plan)
    depth_most = max(p[3] for p in plan)
    vmem = pl.BlockSpec(memory_space=pltpu.VMEM)
    return pl.pallas_call(
        functools.partial(matmul_kernel, plan),
        out_shape=jax.ShapeDtypeStruct((plan[-1][1] * plan[-1][2], width), jnp.float32),
        in_specs=[vmem] * (1 + len(tables)),
        out_specs=vmem,
        scratch_shapes=[
            pltpu.VMEM((buf_rows, width), jnp.float32),
            pltpu.VMEM((buf_rows, width), jnp.float32),
            pltpu.VMEM((2, 3, depth_most, 2 * width), jnp.bfloat16),
        ],
        compiler_params=pltpu.CompilerParams(vmem_limit_bytes=60 * 1024 * 1024),
    )(state, *tables)


def harmonic_kernel(power_ref, offset_ref, out_ref):
    fundamentals = out_ref.shape[0]
    total = None
    for order in range(HARM):
        stride = order + 1
        offset = offset_ref[order]
        for phase in range(stride):
            picked = power_ref[pl.ds(phase, fundamentals, stride=stride), :]
            term = jnp.where(offset == phase, picked, 0.0)
            total = term if total is None else total + term
    out_ref[...] = total * (1.0 / HARM)


def delayed(value, amount):
    rolled = pltpu.roll(value, amount, 2)
    previous = jnp.concatenate([rolled[-1:], rolled[:-1]], axis=0)
    lane = lax.broadcasted_iota(jnp.int32, value.shape, 2)
    return jnp.where(lane < amount, previous, rolled)


def local_kernel(plan, sub, base, first_ref, second_ref, shift_ref, x_ref, out_ref, *bufs):
    count = len(plan)
    final = bufs[-1]
    source = x_ref
    for step, (row_in, row_out, bands_out) in enumerate(plan):
        target = final if step == count - 1 else bufs[step]

        def body(row, carry, source=source, target=target, step=step,
                 bands_out=bands_out, last=step == count - 1):
            lower = source[first_ref[step, row], :, pl.ds(0, bands_out, stride=2), :]
            upper = source[second_ref[step, row], :, pl.ds(1, bands_out, stride=2), :]
            merged = lower + delayed(upper, shift_ref[step, row])
            if last:
                target[:, pl.ds(row, 1), :] = merged
            else:
                target[row] = merged
            return carry

        lax.fori_loop(0, row_out, body, 0, unroll=min(row_out, 8))
        source = target
    for dest in range(out_ref.shape[0]):
        start = base + sub * dest
        slab, offset = start // LANES, start % LANES
        if offset == 0:
            out_ref[dest] = final[slab]
        else:
            lane = lax.broadcasted_iota(jnp.int32, final.shape[1:], 1)
            head = pltpu.roll(final[slab], LANES - offset, 1)
            tail = pltpu.roll(final[slab + 1], LANES - offset, 1)
            out_ref[dest] = jnp.where(lane < LANES - offset, head, tail)


def run_local(state, first_rows, second_rows, shifts, plan, parts, sub, base):
    slabs = state.shape[1]
    rows_last = plan[-1][1]
    smem = pl.BlockSpec(memory_space=pltpu.SMEM)
    vmem = pl.BlockSpec(memory_space=pltpu.VMEM)
    scratch = [pltpu.VMEM((p[1], slabs, p[2], LANES), jnp.float32) for p in plan[:-1]]
    scratch.append(pltpu.VMEM((slabs, rows_last, LANES), jnp.float32))
    return pl.pallas_call(
        functools.partial(local_kernel, plan, sub, base),
        out_shape=jax.ShapeDtypeStruct((parts, rows_last, sub + SUB_HALO), jnp.float32),
        in_specs=[smem, smem, smem, vmem],
        out_specs=vmem,
        scratch_shapes=scratch,
        compiler_params=pltpu.CompilerParams(vmem_limit_bytes=56 * 1024 * 1024),
    )(first_rows, second_rows, shifts, state)


def spectra(series, harmonic_bins):
    count = series.shape[0]
    total = series.shape[1]
    outer = DFT_OUTER
    inner = total // outer
    half_inner = inner // 2
    highest = lax.Precision.HIGHEST
    grid = series.reshape(count, outer, inner)
    outer_index = jnp.arange(outer, dtype=jnp.int32)
    inner_index = jnp.arange(inner, dtype=jnp.int32)
    half_index = jnp.arange(half_inner, dtype=jnp.int32)
    angle_outer = (
        2.0
        * math.pi
        / outer
        * (outer_index[:, None] * outer_index[None, :] % outer).astype(jnp.float32)
    )
    outer_table = jnp.concatenate([jnp.cos(angle_outer), jnp.sin(angle_outer)], axis=1)
    section_one = jnp.einsum("npq,pk->nkq", grid, outer_table, precision=highest)
    section_re = section_one[:, :outer]
    section_im = -section_one[:, outer:]
    angle_twist = (
        2.0
        * math.pi
        / total
        * (outer_index[:, None] * inner_index[None, :] % total).astype(jnp.float32)
    )
    twist_cos = jnp.cos(angle_twist)
    twist_sin = jnp.sin(angle_twist)
    rotated = jnp.stack(
        [
            section_re * twist_cos + section_im * twist_sin,
            section_im * twist_cos - section_re * twist_sin,
        ]
    )
    angle_inner = (
        2.0
        * math.pi
        / inner
        * (inner_index[:, None] * half_index[None, :] % inner).astype(jnp.float32)
    )
    inner_table = jnp.concatenate([jnp.cos(angle_inner), jnp.sin(angle_inner)], axis=1)
    section_two = jnp.einsum("snkq,qm->snkm", rotated, inner_table, precision=highest)
    final_re = section_two[0, :, :, :half_inner] + section_two[1, :, :, half_inner:]
    final_im = section_two[1, :, :, :half_inner] - section_two[0, :, :, half_inner:]
    spectrum_power = (final_re * final_re + final_im * final_im) / (C * total)
    spectrum_power = jnp.transpose(spectrum_power, (0, 2, 1)).reshape(count, total // 2)
    fundamentals = harmonic_bins.shape[1]
    fundamental = jnp.arange(fundamentals, dtype=jnp.int32)
    stride = jnp.arange(1, HARM + 1, dtype=jnp.int32)[:, None]
    offsets = (harmonic_bins - stride * fundamental[None, :])[:, :, None]
    vmem = pl.BlockSpec(memory_space=pltpu.VMEM)
    harmonic_t = pl.pallas_call(
        harmonic_kernel,
        out_shape=jax.ShapeDtypeStruct((fundamentals, count), jnp.float32),
        in_specs=[vmem, vmem],
        out_specs=vmem,
    )(jnp.transpose(spectrum_power), offsets)
    harmonic = jnp.transpose(harmonic_t)
    return spectrum_power, harmonic


def on_device(filterbank, first_rows, second_rows, shifts, harmonic_bins):
    channels = filterbank.shape[0]
    samples = filterbank.shape[1]
    local_levels = channels.bit_length() - 1
    chan_count = lax.axis_size("chan")
    tm_count = lax.axis_size("tm")
    cross_levels = chan_count.bit_length() - 1
    levels = local_levels + cross_levels
    rim = lax.ppermute(
        filterbank[:, samples - RAW_HALO :],
        "tm",
        [(source, source + 1) for source in range(tm_count - 1)],
    )
    widened = jnp.concatenate([rim, filterbank], axis=1)
    local_plan = [
        (2**level, 2 ** (level + 1), channels >> (level + 1)) for level in range(local_levels)
    ]
    sub = samples // chan_count
    pieces = run_local(
        widened.astype(jnp.float32).reshape(channels, -1, LANES).transpose(1, 0, 2)[None],
        first_rows[:local_levels, :channels],
        second_rows[:local_levels, :channels],
        shifts[:local_levels, :channels],
        local_plan,
        chan_count,
        sub,
        RAW_HALO - SUB_HALO,
    )
    pieces, first_rows, second_rows, shifts = lax.optimization_barrier(
        (pieces, first_rows, second_rows, shifts)
    )
    window = sub + SUB_HALO
    layers = lax.all_to_all(pieces, "chan", split_axis=0, concat_axis=0, tiled=True)
    cross_plan = []
    bands = chan_count
    for level in range(local_levels, levels):
        bands //= 2
        rows_in = min(2**level, NDM)
        cross_plan.append((rows_in, min(2 ** (level + 1), NDM), bands, min(rows_in, NDM // 2)))
    plane = run_matmul_levels(
        layers.reshape(chan_count * channels, window),
        first_rows,
        second_rows,
        shifts,
        list(range(local_levels, levels)),
        cross_plan,
    )[:, SUB_HALO:]
    groups = chan_count * tm_count
    share = NDM // groups
    outgoing = plane.reshape(groups, share, sub)
    incoming = lax.all_to_all(outgoing, ("chan", "tm"), split_axis=0, concat_axis=0, tiled=True)
    series = (
        incoming.reshape(chan_count, tm_count, share, sub)
        .transpose(2, 1, 0, 3)
        .reshape(share, tm_count * samples)
    )
    return spectra(series, harmonic_bins)


def solution(mesh):
    in_specs = (P("chan", "tm"), P(), P(), P(), P())
    out_specs = (P(("chan", "tm"), None), P(("chan", "tm"), None))
    return jax.shard_map(
        on_device, mesh=mesh, in_specs=in_specs, out_specs=out_specs, check_vma=False
    )
```

```python
import functools
import math

import jax
import jax.numpy as jnp
from jax import lax
from jax.experimental import pallas as pl
from jax.experimental.pallas import tpu as pltpu
from jax.sharding import PartitionSpec as P

C = 4096
NDM = 2048
SHIFT = 16
DFT_OUTER = 64
HARM = 8
RAW_HALO = 256
SUB_HALO = 64
TILE = 256
LANES = 128
PIECES = 2


def shift_right(value, amount):
    width = value.shape[-1]
    pad = [(0, 0)] * (value.ndim - 1) + [(amount, 0)]
    return jnp.pad(value, pad)[..., :width]


def merge_level(paired, rows_first, rows_second, delays):
    lower_bands = jnp.take(paired[0::2], rows_first, axis=1)
    upper_bands = jnp.take(paired[1::2], rows_second, axis=1)
    delay_col = delays[None, :, None]
    shifted = upper_bands
    for bit in (1, 2, 4, 8):
        shifted = jnp.where((delay_col & bit) != 0, shift_right(shifted, bit), shifted)
    return lower_bands + shifted


def level_merge(layers, first_rows, second_rows, shifts, level):
    count = min(2 ** (level + 1), NDM)
    return merge_level(
        layers, first_rows[level, :count], second_rows[level, :count], shifts[level, :count]
    )


def split_pieces(block):
    high = block.astype(jnp.bfloat16)
    low = (block - high.astype(jnp.float32)).astype(jnp.bfloat16)
    return high, low


def matmul_kernel(plan, x_ref, *refs):
    count = len(plan)
    tables = refs[: 3 * count]
    out_ref, buf_a, buf_b, parts = refs[3 * count :]
    width = x_ref.shape[1]
    source = x_ref
    for step, (row_in, row_out, bands_out, depth) in enumerate(plan):
        pick_low, pick_high, delay = tables[3 * step : 3 * step + 3]
        target = out_ref if step == count - 1 else (buf_a, buf_b)[step % 2]
        group = 2 if bands_out >= 2 else 1
        lanes = group * width
        for first_band in range(0, bands_out, group):
            for member in range(group):
                band = first_band + member
                for side in range(2):
                    block = source[pl.ds((2 * band + side) * row_in, depth), :]
                    for piece, value in enumerate(split_pieces(block)):
                        parts[side, piece, pl.ds(0, depth), pl.ds(member * width, width)] = value

            def tile(index, carry, target=target, first_band=first_band, depth=depth,
                     row_out=row_out, group=group, lanes=lanes,
                     pick_low=pick_low, pick_high=pick_high, delay=delay):
                rows = pl.ds(pl.multiple_of(index * TILE, TILE), TILE)
                low_sel = pick_low[rows, :]
                high_sel = pick_high[rows, :]
                lower = None
                upper = None
                for piece in range(PIECES):
                    term = jnp.dot(low_sel, parts[0, piece, pl.ds(0, depth), pl.ds(0, lanes)],
                                   preferred_element_type=jnp.float32)
                    lower = term if lower is None else lower + term
                    term = jnp.dot(high_sel, parts[1, piece, pl.ds(0, depth), pl.ds(0, lanes)],
                                   preferred_element_type=jnp.float32)
                    upper = term if upper is None else upper + term
                amount = delay[rows, :]
                for bit in (1, 2, 4, 8):
                    upper = jnp.where((amount & bit) != 0, pltpu.roll(upper, bit, 1), upper)
                merged = lower + upper
                for member in range(group):
                    start = pl.multiple_of((first_band + member) * row_out + index * TILE, TILE)
                    target[pl.ds(start, TILE), :] = merged[:, member * width : (member + 1) * width]
                return carry

            lax.fori_loop(0, row_out // TILE, tile, 0)
        source = target


def run_matmul_levels(state, first_rows, second_rows, shifts, levels, plan):
    width = state.shape[1]
    tables = []
    for level, (row_in, row_out, bands_out, depth) in zip(levels, plan):
        columns = jnp.arange(depth, dtype=jnp.int32)[None, :]
        tables.append((first_rows[level, :row_out, None] == columns).astype(jnp.bfloat16))
        tables.append((second_rows[level, :row_out, None] == columns).astype(jnp.bfloat16))
        tables.append(shifts[level, :row_out, None])
    buf_rows = max(p[1] * p[2] for p in plan)
    depth_most = max(p[3] for p in plan)
    vmem = pl.BlockSpec(memory_space=pltpu.VMEM)
    return pl.pallas_call(
        functools.partial(matmul_kernel, plan),
        out_shape=jax.ShapeDtypeStruct((plan[-1][1] * plan[-1][2], width), jnp.float32),
        in_specs=[vmem] * (1 + len(tables)),
        out_specs=vmem,
        scratch_shapes=[
            pltpu.VMEM((buf_rows, width), jnp.float32),
            pltpu.VMEM((buf_rows, width), jnp.float32),
            pltpu.VMEM((2, PIECES, depth_most, 2 * width), jnp.bfloat16),
        ],
        compiler_params=pltpu.CompilerParams(vmem_limit_bytes=60 * 1024 * 1024),
    )(state, *tables)


def harmonic_kernel(power_ref, offset_ref, out_ref):
    fundamentals = out_ref.shape[0]
    total = None
    for order in range(HARM):
        stride = order + 1
        offset = offset_ref[order]
        for phase in range(stride):
            picked = power_ref[pl.ds(phase, fundamentals, stride=stride), :]
            term = jnp.where(offset == phase, picked, 0.0)
            total = term if total is None else total + term
    out_ref[...] = total * (1.0 / HARM)


def delayed(value, amount):
    rolled = pltpu.roll(value, amount, 2)
    previous = jnp.concatenate([rolled[-1:], rolled[:-1]], axis=0)
    lane = lax.broadcasted_iota(jnp.int32, value.shape, 2)
    return jnp.where(lane < amount, previous, rolled)


def local_kernel(plan, sub, base, first_ref, second_ref, shift_ref, x_ref, out_ref, *bufs):
    count = len(plan)
    final = bufs[-1]
    source = x_ref
    for step, (row_in, row_out, bands_out) in enumerate(plan):
        target = final if step == count - 1 else bufs[step]

        def body(row, carry, source=source, target=target, step=step,
                 bands_out=bands_out, last=step == count - 1):
            lower = source[first_ref[step, row], :, pl.ds(0, bands_out, stride=2), :]
            upper = source[second_ref[step, row], :, pl.ds(1, bands_out, stride=2), :]
            merged = lower + delayed(upper, shift_ref[step, row])
            if last:
                target[:, pl.ds(row, 1), :] = merged
            else:
                target[row] = merged
            return carry

        lax.fori_loop(0, row_out, body, 0, unroll=min(row_out, 8))
        source = target
    for dest in range(out_ref.shape[0]):
        start = base + sub * dest
        slab, offset = start // LANES, start % LANES
        if offset == 0:
            out_ref[dest] = final[slab]
        else:
            lane = lax.broadcasted_iota(jnp.int32, final.shape[1:], 1)
            head = pltpu.roll(final[slab], LANES - offset, 1)
            tail = pltpu.roll(final[slab + 1], LANES - offset, 1)
            out_ref[dest] = jnp.where(lane < LANES - offset, head, tail)


def run_local(state, first_rows, second_rows, shifts, plan, parts, sub, base):
    slabs = state.shape[1]
    rows_last = plan[-1][1]
    smem = pl.BlockSpec(memory_space=pltpu.SMEM)
    vmem = pl.BlockSpec(memory_space=pltpu.VMEM)
    scratch = [pltpu.VMEM((p[1], slabs, p[2], LANES), jnp.float32) for p in plan[:-1]]
    scratch.append(pltpu.VMEM((slabs, rows_last, LANES), jnp.float32))
    return pl.pallas_call(
        functools.partial(local_kernel, plan, sub, base),
        out_shape=jax.ShapeDtypeStruct((parts, rows_last, sub + SUB_HALO), jnp.float32),
        in_specs=[smem, smem, smem, vmem],
        out_specs=vmem,
        scratch_shapes=scratch,
        compiler_params=pltpu.CompilerParams(vmem_limit_bytes=56 * 1024 * 1024),
    )(first_rows, second_rows, shifts, state)


def spectra(series, harmonic_bins):
    count = series.shape[0]
    total = series.shape[1]
    outer = DFT_OUTER
    inner = total // outer
    half_inner = inner // 2
    highest = lax.Precision.HIGHEST
    grid = series.reshape(count, outer, inner)
    outer_index = jnp.arange(outer, dtype=jnp.int32)
    inner_index = jnp.arange(inner, dtype=jnp.int32)
    half_index = jnp.arange(half_inner, dtype=jnp.int32)
    angle_outer = (
        2.0
        * math.pi
        / outer
        * (outer_index[:, None] * outer_index[None, :] % outer).astype(jnp.float32)
    )
    outer_table = jnp.concatenate([jnp.cos(angle_outer), jnp.sin(angle_outer)], axis=1)
    section_one = jnp.einsum("npq,pk->nkq", grid, outer_table, precision=highest)
    section_re = section_one[:, :outer]
    section_im = -section_one[:, outer:]
    angle_twist = (
        2.0
        * math.pi
        / total
        * (outer_index[:, None] * inner_index[None, :] % total).astype(jnp.float32)
    )
    twist_cos = jnp.cos(angle_twist)
    twist_sin = jnp.sin(angle_twist)
    rotated = jnp.stack(
        [
            section_re * twist_cos + section_im * twist_sin,
            section_im * twist_cos - section_re * twist_sin,
        ]
    )
    angle_inner = (
        2.0
        * math.pi
        / inner
        * (inner_index[:, None] * half_index[None, :] % inner).astype(jnp.float32)
    )
    inner_table = jnp.concatenate([jnp.cos(angle_inner), jnp.sin(angle_inner)], axis=1)
    section_two = jnp.einsum("snkq,qm->snkm", rotated, inner_table, precision=highest)
    final_re = section_two[0, :, :, :half_inner] + section_two[1, :, :, half_inner:]
    final_im = section_two[1, :, :, :half_inner] - section_two[0, :, :, half_inner:]
    spectrum_power = (final_re * final_re + final_im * final_im) / (C * total)
    spectrum_power = jnp.transpose(spectrum_power, (0, 2, 1)).reshape(count, total // 2)
    fundamentals = harmonic_bins.shape[1]
    fundamental = jnp.arange(fundamentals, dtype=jnp.int32)
    stride = jnp.arange(1, HARM + 1, dtype=jnp.int32)[:, None]
    offsets = (harmonic_bins - stride * fundamental[None, :])[:, :, None]
    vmem = pl.BlockSpec(memory_space=pltpu.VMEM)
    harmonic_t = pl.pallas_call(
        harmonic_kernel,
        out_shape=jax.ShapeDtypeStruct((fundamentals, count), jnp.float32),
        in_specs=[vmem, vmem],
        out_specs=vmem,
    )(jnp.transpose(spectrum_power), offsets)
    harmonic = jnp.transpose(harmonic_t)
    return spectrum_power, harmonic


def on_device(filterbank, first_rows, second_rows, shifts, harmonic_bins):
    channels = filterbank.shape[0]
    samples = filterbank.shape[1]
    local_levels = channels.bit_length() - 1
    chan_count = lax.axis_size("chan")
    tm_count = lax.axis_size("tm")
    cross_levels = chan_count.bit_length() - 1
    levels = local_levels + cross_levels
    rim = lax.ppermute(
        filterbank[:, samples - RAW_HALO :],
        "tm",
        [(source, source + 1) for source in range(tm_count - 1)],
    )
    widened = jnp.concatenate([rim, filterbank], axis=1)
    local_plan = [
        (2**level, 2 ** (level + 1), channels >> (level + 1)) for level in range(local_levels)
    ]
    sub = samples // chan_count
    pieces = run_local(
        widened.astype(jnp.float32).reshape(channels, -1, LANES).transpose(1, 0, 2)[None],
        first_rows[:local_levels, :channels],
        second_rows[:local_levels, :channels],
        shifts[:local_levels, :channels],
        local_plan,
        chan_count,
        sub,
        RAW_HALO - SUB_HALO,
    )
    pieces, first_rows, second_rows, shifts = lax.optimization_barrier(
        (pieces, first_rows, second_rows, shifts)
    )
    window = sub + SUB_HALO
    layers = lax.all_to_all(pieces, "chan", split_axis=0, concat_axis=0, tiled=True)
    cross_plan = []
    bands = chan_count
    for level in range(local_levels, levels):
        bands //= 2
        rows_in = min(2**level, NDM)
        cross_plan.append((rows_in, min(2 ** (level + 1), NDM), bands, min(rows_in, NDM // 2)))
    plane = run_matmul_levels(
        layers.reshape(chan_count * channels, window),
        first_rows,
        second_rows,
        shifts,
        list(range(local_levels, levels)),
        cross_plan,
    )[:, SUB_HALO:]
    groups = chan_count * tm_count
    share = NDM // groups
    outgoing = plane.reshape(groups, share, sub)
    incoming = lax.all_to_all(outgoing, ("chan", "tm"), split_axis=0, concat_axis=0, tiled=True)
    series = (
        incoming.reshape(chan_count, tm_count, share, sub)
        .transpose(2, 1, 0, 3)
        .reshape(share, tm_count * samples)
    )
    return spectra(series, harmonic_bins)


def solution(mesh):
    in_specs = (P("chan", "tm"), P(), P(), P(), P())
    out_specs = (P(("chan", "tm"), None), P(("chan", "tm"), None))
    return jax.shard_map(
        on_device, mesh=mesh, in_specs=in_specs, out_specs=out_specs, check_vma=False
    )
```

```python
import functools
import math

import jax
import jax.numpy as jnp
from jax import lax
from jax.experimental import pallas as pl
from jax.experimental.pallas import tpu as pltpu
from jax.sharding import PartitionSpec as P

C = 4096
NDM = 2048
SHIFT = 16
DFT_OUTER = 64
HARM = 8
RAW_HALO = 256
SUB_HALO = 64
TILE = 512
LANES = 128
PIECES = 2


def shift_right(value, amount):
    width = value.shape[-1]
    pad = [(0, 0)] * (value.ndim - 1) + [(amount, 0)]
    return jnp.pad(value, pad)[..., :width]


def merge_level(paired, rows_first, rows_second, delays):
    lower_bands = jnp.take(paired[0::2], rows_first, axis=1)
    upper_bands = jnp.take(paired[1::2], rows_second, axis=1)
    delay_col = delays[None, :, None]
    shifted = upper_bands
    for bit in (1, 2, 4, 8):
        shifted = jnp.where((delay_col & bit) != 0, shift_right(shifted, bit), shifted)
    return lower_bands + shifted


def level_merge(layers, first_rows, second_rows, shifts, level):
    count = min(2 ** (level + 1), NDM)
    return merge_level(
        layers, first_rows[level, :count], second_rows[level, :count], shifts[level, :count]
    )


def split_pieces(block):
    high = block.astype(jnp.bfloat16)
    low = (block - high.astype(jnp.float32)).astype(jnp.bfloat16)
    return high, low


def matmul_kernel(plan, x_ref, *refs):
    count = len(plan)
    tables = refs[: 3 * count]
    out_ref, buf_a, buf_b, parts = refs[3 * count :]
    width = x_ref.shape[1]
    source = x_ref
    for step, (row_in, row_out, bands_out, depth) in enumerate(plan):
        pick_low, pick_high, delay = tables[3 * step : 3 * step + 3]
        target = out_ref if step == count - 1 else (buf_a, buf_b)[step % 2]
        group = 2 if bands_out >= 2 else 1
        lanes = group * width
        for first_band in range(0, bands_out, group):
            for member in range(group):
                band = first_band + member
                for side in range(2):
                    block = source[pl.ds((2 * band + side) * row_in, depth), :]
                    for piece, value in enumerate(split_pieces(block)):
                        parts[side, piece, pl.ds(0, depth), pl.ds(member * width, width)] = value

            def tile(index, carry, target=target, first_band=first_band, depth=depth,
                     row_out=row_out, group=group, lanes=lanes,
                     pick_low=pick_low, pick_high=pick_high, delay=delay):
                rows = pl.ds(pl.multiple_of(index * TILE, TILE), TILE)
                low_sel = pick_low[rows, :]
                high_sel = pick_high[rows, :]
                lower = None
                upper = None
                for piece in range(PIECES):
                    term = jnp.dot(low_sel, parts[0, piece, pl.ds(0, depth), pl.ds(0, lanes)],
                                   preferred_element_type=jnp.float32)
                    lower = term if lower is None else lower + term
                    term = jnp.dot(high_sel, parts[1, piece, pl.ds(0, depth), pl.ds(0, lanes)],
                                   preferred_element_type=jnp.float32)
                    upper = term if upper is None else upper + term
                amount = delay[rows, :]
                for bit in (1, 2, 4, 8):
                    upper = jnp.where((amount & bit) != 0, pltpu.roll(upper, bit, 1), upper)
                merged = lower + upper
                for member in range(group):
                    start = pl.multiple_of((first_band + member) * row_out + index * TILE, TILE)
                    target[pl.ds(start, TILE), :] = merged[:, member * width : (member + 1) * width]
                return carry

            lax.fori_loop(0, row_out // TILE, tile, 0)
        source = target


def run_matmul_levels(state, first_rows, second_rows, shifts, levels, plan):
    width = state.shape[1]
    tables = []
    for level, (row_in, row_out, bands_out, depth) in zip(levels, plan):
        columns = jnp.arange(depth, dtype=jnp.int32)[None, :]
        tables.append((first_rows[level, :row_out, None] == columns).astype(jnp.bfloat16))
        tables.append((second_rows[level, :row_out, None] == columns).astype(jnp.bfloat16))
        tables.append(shifts[level, :row_out, None])
    buf_rows = max(p[1] * p[2] for p in plan)
    depth_most = max(p[3] for p in plan)
    vmem = pl.BlockSpec(memory_space=pltpu.VMEM)
    return pl.pallas_call(
        functools.partial(matmul_kernel, plan),
        out_shape=jax.ShapeDtypeStruct((plan[-1][1] * plan[-1][2], width), jnp.float32),
        in_specs=[vmem] * (1 + len(tables)),
        out_specs=vmem,
        scratch_shapes=[
            pltpu.VMEM((buf_rows, width), jnp.float32),
            pltpu.VMEM((buf_rows, width), jnp.float32),
            pltpu.VMEM((2, PIECES, depth_most, 2 * width), jnp.bfloat16),
        ],
        compiler_params=pltpu.CompilerParams(vmem_limit_bytes=60 * 1024 * 1024),
    )(state, *tables)


def harmonic_kernel(power_ref, offset_ref, out_ref):
    fundamentals = out_ref.shape[0]
    total = None
    for order in range(HARM):
        stride = order + 1
        offset = offset_ref[order]
        for phase in range(stride):
            picked = power_ref[pl.ds(phase, fundamentals, stride=stride), :]
            term = jnp.where(offset == phase, picked, 0.0)
            total = term if total is None else total + term
    out_ref[...] = total * (1.0 / HARM)


def delayed(value, amount):
    rolled = pltpu.roll(value, amount, 2)
    previous = jnp.concatenate([rolled[-1:], rolled[:-1]], axis=0)
    lane = lax.broadcasted_iota(jnp.int32, value.shape, 2)
    return jnp.where(lane < amount, previous, rolled)


def local_kernel(plan, sub, base, table_ref, x_ref, out_ref, *bufs):
    count = len(plan)
    final = bufs[-1]
    source = x_ref
    for step, (row_in, row_out, bands_out) in enumerate(plan):
        target = final if step == count - 1 else bufs[step]

        def body(row, carry, source=source, target=target, step=step,
                 bands_out=bands_out, last=step == count - 1):
            lower = source[table_ref[0, step, row], :, pl.ds(0, bands_out, stride=2), :]
            upper = source[table_ref[1, step, row], :, pl.ds(1, bands_out, stride=2), :]
            merged = lower + delayed(upper, table_ref[2, step, row])
            if last:
                target[:, pl.ds(row, 1), :] = merged
            else:
                target[row] = merged
            return carry

        lax.fori_loop(0, row_out, body, 0, unroll=min(row_out, 8))
        source = target
    for dest in range(out_ref.shape[0]):
        start = base + sub * dest
        slab, offset = start // LANES, start % LANES
        if offset == 0:
            out_ref[dest] = final[slab]
        else:
            lane = lax.broadcasted_iota(jnp.int32, final.shape[1:], 1)
            head = pltpu.roll(final[slab], LANES - offset, 1)
            tail = pltpu.roll(final[slab + 1], LANES - offset, 1)
            out_ref[dest] = jnp.where(lane < LANES - offset, head, tail)


def run_local(state, tables, plan, parts, sub, base):
    slabs = state.shape[1]
    rows_last = plan[-1][1]
    smem = pl.BlockSpec(memory_space=pltpu.SMEM)
    vmem = pl.BlockSpec(memory_space=pltpu.VMEM)
    scratch = [pltpu.VMEM((p[1], slabs, p[2], LANES), jnp.float32) for p in plan[:-1]]
    scratch.append(pltpu.VMEM((slabs, rows_last, LANES), jnp.float32))
    return pl.pallas_call(
        functools.partial(local_kernel, plan, sub, base),
        out_shape=jax.ShapeDtypeStruct((parts, rows_last, sub + SUB_HALO), jnp.float32),
        in_specs=[smem, vmem],
        out_specs=vmem,
        scratch_shapes=scratch,
        compiler_params=pltpu.CompilerParams(vmem_limit_bytes=56 * 1024 * 1024),
    )(tables, state)


def spectra(series, harmonic_bins):
    count = series.shape[0]
    total = series.shape[1]
    outer = DFT_OUTER
    inner = total // outer
    half_inner = inner // 2
    highest = lax.Precision.HIGHEST
    grid = series.reshape(count, outer, inner)
    outer_index = jnp.arange(outer, dtype=jnp.int32)
    inner_index = jnp.arange(inner, dtype=jnp.int32)
    half_index = jnp.arange(half_inner, dtype=jnp.int32)
    angle_outer = (
        2.0
        * math.pi
        / outer
        * (outer_index[:, None] * outer_index[None, :] % outer).astype(jnp.float32)
    )
    outer_table = jnp.concatenate([jnp.cos(angle_outer), jnp.sin(angle_outer)], axis=1)
    section_one = jnp.einsum("npq,pk->nkq", grid, outer_table, precision=highest)
    section_re = section_one[:, :outer]
    section_im = -section_one[:, outer:]
    angle_twist = (
        2.0
        * math.pi
        / total
        * (outer_index[:, None] * inner_index[None, :] % total).astype(jnp.float32)
    )
    twist_cos = jnp.cos(angle_twist)
    twist_sin = jnp.sin(angle_twist)
    rotated = jnp.stack(
        [
            section_re * twist_cos + section_im * twist_sin,
            section_im * twist_cos - section_re * twist_sin,
        ]
    )
    angle_inner = (
        2.0
        * math.pi
        / inner
        * (inner_index[:, None] * half_index[None, :] % inner).astype(jnp.float32)
    )
    inner_table = jnp.concatenate([jnp.cos(angle_inner), jnp.sin(angle_inner)], axis=1)
    section_two = jnp.einsum("snkq,qm->snkm", rotated, inner_table, precision=highest)
    final_re = section_two[0, :, :, :half_inner] + section_two[1, :, :, half_inner:]
    final_im = section_two[1, :, :, :half_inner] - section_two[0, :, :, half_inner:]
    spectrum_power = (final_re * final_re + final_im * final_im) / (C * total)
    spectrum_power = jnp.transpose(spectrum_power, (0, 2, 1)).reshape(count, total // 2)
    fundamentals = harmonic_bins.shape[1]
    fundamental = jnp.arange(fundamentals, dtype=jnp.int32)
    stride = jnp.arange(1, HARM + 1, dtype=jnp.int32)[:, None]
    offsets = (harmonic_bins - stride * fundamental[None, :])[:, :, None]
    vmem = pl.BlockSpec(memory_space=pltpu.VMEM)
    harmonic_t = pl.pallas_call(
        harmonic_kernel,
        out_shape=jax.ShapeDtypeStruct((fundamentals, count), jnp.float32),
        in_specs=[vmem, vmem],
        out_specs=vmem,
    )(jnp.transpose(spectrum_power), offsets)
    harmonic = jnp.transpose(harmonic_t)
    return spectrum_power, harmonic


def on_device(filterbank, first_rows, second_rows, shifts, harmonic_bins):
    channels = filterbank.shape[0]
    samples = filterbank.shape[1]
    local_levels = channels.bit_length() - 1
    chan_count = lax.axis_size("chan")
    tm_count = lax.axis_size("tm")
    cross_levels = chan_count.bit_length() - 1
    levels = local_levels + cross_levels
    rim = lax.ppermute(
        filterbank[:, samples - RAW_HALO :],
        "tm",
        [(source, source + 1) for source in range(tm_count - 1)],
    )
    widened = jnp.concatenate([rim, filterbank], axis=1)
    local_plan = [
        (2**level, 2 ** (level + 1), channels >> (level + 1)) for level in range(local_levels)
    ]
    sub = samples // chan_count
    pieces = run_local(
        widened.astype(jnp.float32).reshape(channels, -1, LANES).transpose(1, 0, 2)[None],
        jnp.stack([first_rows, second_rows, shifts])[:, :local_levels, :channels],
        local_plan,
        chan_count,
        sub,
        RAW_HALO - SUB_HALO,
    )
    pieces, first_rows, second_rows, shifts = lax.optimization_barrier(
        (pieces, first_rows, second_rows, shifts)
    )
    window = sub + SUB_HALO
    layers = lax.all_to_all(pieces, "chan", split_axis=0, concat_axis=0, tiled=True)
    cross_plan = []
    bands = chan_count
    for level in range(local_levels, levels):
        bands //= 2
        rows_in = min(2**level, NDM)
        cross_plan.append((rows_in, min(2 ** (level + 1), NDM), bands, min(rows_in, NDM // 2)))
    plane = run_matmul_levels(
        layers.reshape(chan_count * channels, window),
        first_rows,
        second_rows,
        shifts,
        list(range(local_levels, levels)),
        cross_plan,
    )[:, SUB_HALO:]
    groups = chan_count * tm_count
    share = NDM // groups
    outgoing = plane.reshape(groups, share, sub)
    incoming = lax.all_to_all(outgoing, ("chan", "tm"), split_axis=0, concat_axis=0, tiled=True)
    series = (
        incoming.reshape(chan_count, tm_count, share, sub)
        .transpose(2, 1, 0, 3)
        .reshape(share, tm_count * samples)
    )
    return spectra(series, harmonic_bins)


def solution(mesh):
    in_specs = (P("chan", "tm"), P(), P(), P(), P())
    out_specs = (P(("chan", "tm"), None), P(("chan", "tm"), None))
    return jax.shard_map(
        on_device, mesh=mesh, in_specs=in_specs, out_specs=out_specs, check_vma=False
    )
```

```python
import functools
import math

import jax
import jax.numpy as jnp
from jax import lax
from jax.experimental import pallas as pl
from jax.experimental.pallas import tpu as pltpu
from jax.sharding import PartitionSpec as P

C = 4096
NDM = 2048
SHIFT = 16
DFT_OUTER = 64
HARM = 8
RAW_HALO = 256
SUB_HALO = 64
TILE = 512
LANES = 128
PIECES = 2


def shift_right(value, amount):
    width = value.shape[-1]
    pad = [(0, 0)] * (value.ndim - 1) + [(amount, 0)]
    return jnp.pad(value, pad)[..., :width]


def merge_level(paired, rows_first, rows_second, delays):
    lower_bands = jnp.take(paired[0::2], rows_first, axis=1)
    upper_bands = jnp.take(paired[1::2], rows_second, axis=1)
    delay_col = delays[None, :, None]
    shifted = upper_bands
    for bit in (1, 2, 4, 8):
        shifted = jnp.where((delay_col & bit) != 0, shift_right(shifted, bit), shifted)
    return lower_bands + shifted


def level_merge(layers, first_rows, second_rows, shifts, level):
    count = min(2 ** (level + 1), NDM)
    return merge_level(
        layers, first_rows[level, :count], second_rows[level, :count], shifts[level, :count]
    )


def split_pieces(block):
    high = block.astype(jnp.bfloat16)
    low = (block - high.astype(jnp.float32)).astype(jnp.bfloat16)
    return high, low


def matmul_kernel(plan, x_ref, *refs):
    count = len(plan)
    tables = refs[: 3 * count]
    out_ref, buf_a, buf_b, parts = refs[3 * count :]
    width = x_ref.shape[1]
    source = x_ref
    for step, (row_in, row_out, bands_out, depth) in enumerate(plan):
        pick_low, pick_high, delay = tables[3 * step : 3 * step + 3]
        target = out_ref if step == count - 1 else (buf_a, buf_b)[step % 2]
        group = 2 if bands_out >= 2 else 1
        lanes = group * width
        for first_band in range(0, bands_out, group):
            for member in range(group):
                band = first_band + member
                for side in range(2):
                    block = source[pl.ds((2 * band + side) * row_in, depth), :]
                    for piece, value in enumerate(split_pieces(block)):
                        parts[side, piece, pl.ds(0, depth), pl.ds(member * width, width)] = value

            def tile(index, carry, target=target, first_band=first_band, depth=depth,
                     row_out=row_out, group=group, lanes=lanes,
                     pick_low=pick_low, pick_high=pick_high, delay=delay):
                rows = pl.ds(pl.multiple_of(index * TILE, TILE), TILE)
                low_sel = pick_low[rows, :]
                high_sel = pick_high[rows, :]
                lower = None
                upper = None
                for piece in range(PIECES):
                    term = jnp.dot(low_sel, parts[0, piece, pl.ds(0, depth), pl.ds(0, lanes)],
                                   preferred_element_type=jnp.float32)
                    lower = term if lower is None else lower + term
                    term = jnp.dot(high_sel, parts[1, piece, pl.ds(0, depth), pl.ds(0, lanes)],
                                   preferred_element_type=jnp.float32)
                    upper = term if upper is None else upper + term
                amount = delay[rows, :]
                for bit in (1, 2, 4, 8):
                    upper = jnp.where((amount & bit) != 0, pltpu.roll(upper, bit, 1), upper)
                merged = lower + upper
                skip = SUB_HALO if target is out_ref else 0
                for member in range(group):
                    start = pl.multiple_of((first_band + member) * row_out + index * TILE, TILE)
                    target[pl.ds(start, TILE), :] = merged[
                        :, member * width + skip : (member + 1) * width
                    ]
                return carry

            lax.fori_loop(0, row_out // TILE, tile, 0)
        source = target


def run_matmul_levels(state, first_rows, second_rows, shifts, levels, plan):
    width = state.shape[1]
    tables = []
    for level, (row_in, row_out, bands_out, depth) in zip(levels, plan):
        columns = jnp.arange(depth, dtype=jnp.int32)[None, :]
        tables.append((first_rows[level, :row_out, None] == columns).astype(jnp.bfloat16))
        tables.append((second_rows[level, :row_out, None] == columns).astype(jnp.bfloat16))
        tables.append(shifts[level, :row_out, None])
    buf_rows = max(p[1] * p[2] for p in plan)
    depth_most = max(p[3] for p in plan)
    vmem = pl.BlockSpec(memory_space=pltpu.VMEM)
    return pl.pallas_call(
        functools.partial(matmul_kernel, plan),
        out_shape=jax.ShapeDtypeStruct((plan[-1][1] * plan[-1][2], width - SUB_HALO), jnp.float32),
        in_specs=[vmem] * (1 + len(tables)),
        out_specs=vmem,
        scratch_shapes=[
            pltpu.VMEM((buf_rows, width), jnp.float32),
            pltpu.VMEM((buf_rows, width), jnp.float32),
            pltpu.VMEM((2, PIECES, depth_most, 2 * width), jnp.bfloat16),
        ],
        compiler_params=pltpu.CompilerParams(vmem_limit_bytes=60 * 1024 * 1024),
    )(state, *tables)


def harmonic_kernel(power_ref, offset_ref, out_ref):
    fundamentals = out_ref.shape[1]
    total = None
    for order in range(HARM):
        stride = order + 1
        offset = offset_ref[order]
        for phase in range(stride):
            picked = power_ref[pl.ds(phase, fundamentals, stride=stride), :]
            term = jnp.where(offset == phase, picked, 0.0)
            total = term if total is None else total + term
    out_ref[...] = jnp.transpose(total * (1.0 / HARM))


def delayed(value, amount):
    rolled = pltpu.roll(value, amount, 2)
    previous = jnp.concatenate([rolled[-1:], rolled[:-1]], axis=0)
    lane = lax.broadcasted_iota(jnp.int32, value.shape, 2)
    return jnp.where(lane < amount, previous, rolled)


def local_kernel(plan, sub, base, table_ref, x_ref, out_ref, *bufs):
    count = len(plan)
    final = bufs[-1]
    source = x_ref
    for step, (row_in, row_out, bands_out) in enumerate(plan):
        target = final if step == count - 1 else bufs[step]

        def body(row, carry, source=source, target=target, step=step,
                 bands_out=bands_out, last=step == count - 1):
            lower = source[table_ref[0, step, row], :, pl.ds(0, bands_out, stride=2), :]
            upper = source[table_ref[1, step, row], :, pl.ds(1, bands_out, stride=2), :]
            merged = lower + delayed(upper, table_ref[2, step, row])
            if last:
                target[:, pl.ds(row, 1), :] = merged
            else:
                target[row] = merged
            return carry

        lax.fori_loop(0, row_out, body, 0, unroll=min(row_out, 8))
        source = target
    for dest in range(out_ref.shape[0]):
        start = base + sub * dest
        slab, offset = start // LANES, start % LANES
        if offset == 0:
            out_ref[dest] = final[slab]
        else:
            lane = lax.broadcasted_iota(jnp.int32, final.shape[1:], 1)
            head = pltpu.roll(final[slab], LANES - offset, 1)
            tail = pltpu.roll(final[slab + 1], LANES - offset, 1)
            out_ref[dest] = jnp.where(lane < LANES - offset, head, tail)


def run_local(state, tables, plan, parts, sub, base):
    slabs = state.shape[1]
    rows_last = plan[-1][1]
    smem = pl.BlockSpec(memory_space=pltpu.SMEM)
    vmem = pl.BlockSpec(memory_space=pltpu.VMEM)
    scratch = [pltpu.VMEM((p[1], slabs, p[2], LANES), jnp.float32) for p in plan[:-1]]
    scratch.append(pltpu.VMEM((slabs, rows_last, LANES), jnp.float32))
    return pl.pallas_call(
        functools.partial(local_kernel, plan, sub, base),
        out_shape=jax.ShapeDtypeStruct((parts, rows_last, sub + SUB_HALO), jnp.float32),
        in_specs=[smem, vmem],
        out_specs=vmem,
        scratch_shapes=scratch,
        compiler_params=pltpu.CompilerParams(vmem_limit_bytes=56 * 1024 * 1024),
    )(tables, state)


def spectra(series, harmonic_bins):
    count = series.shape[0]
    total = series.shape[1]
    outer = DFT_OUTER
    inner = total // outer
    half_inner = inner // 2
    highest = lax.Precision.HIGHEST
    grid = series.reshape(count, outer, inner)
    outer_index = jnp.arange(outer, dtype=jnp.int32)
    inner_index = jnp.arange(inner, dtype=jnp.int32)
    half_index = jnp.arange(half_inner, dtype=jnp.int32)
    angle_outer = (
        2.0
        * math.pi
        / outer
        * (outer_index[:, None] * outer_index[None, :] % outer).astype(jnp.float32)
    )
    outer_table = jnp.concatenate([jnp.cos(angle_outer), jnp.sin(angle_outer)], axis=1)
    section_one = jnp.einsum("npq,pk->nkq", grid, outer_table, precision=highest)
    section_re = section_one[:, :outer]
    section_im = -section_one[:, outer:]
    angle_twist = (
        2.0
        * math.pi
        / total
        * (outer_index[:, None] * inner_index[None, :] % total).astype(jnp.float32)
    )
    twist_cos = jnp.cos(angle_twist)
    twist_sin = jnp.sin(angle_twist)
    rotated = jnp.stack(
        [
            section_re * twist_cos + section_im * twist_sin,
            section_im * twist_cos - section_re * twist_sin,
        ]
    )
    angle_inner = (
        2.0
        * math.pi
        / inner
        * (inner_index[:, None] * half_index[None, :] % inner).astype(jnp.float32)
    )
    inner_table = jnp.concatenate([jnp.cos(angle_inner), jnp.sin(angle_inner)], axis=1)
    section_two = jnp.einsum("snkq,qm->snkm", rotated, inner_table, precision=highest)
    final_re = section_two[0, :, :, :half_inner] + section_two[1, :, :, half_inner:]
    final_im = section_two[1, :, :, :half_inner] - section_two[0, :, :, half_inner:]
    spectrum_power = (final_re * final_re + final_im * final_im) / (C * total)
    spectrum_power = jnp.transpose(spectrum_power, (0, 2, 1)).reshape(count, total // 2)
    fundamentals = harmonic_bins.shape[1]
    fundamental = jnp.arange(fundamentals, dtype=jnp.int32)
    stride = jnp.arange(1, HARM + 1, dtype=jnp.int32)[:, None]
    offsets = (harmonic_bins - stride * fundamental[None, :])[:, :, None]
    vmem = pl.BlockSpec(memory_space=pltpu.VMEM)
    harmonic = pl.pallas_call(
        harmonic_kernel,
        out_shape=jax.ShapeDtypeStruct((count, fundamentals), jnp.float32),
        in_specs=[vmem, vmem],
        out_specs=vmem,
    )(jnp.transpose(spectrum_power), offsets)
    return spectrum_power, harmonic


def on_device(filterbank, first_rows, second_rows, shifts, harmonic_bins):
    channels = filterbank.shape[0]
    samples = filterbank.shape[1]
    local_levels = channels.bit_length() - 1
    chan_count = lax.axis_size("chan")
    tm_count = lax.axis_size("tm")
    cross_levels = chan_count.bit_length() - 1
    levels = local_levels + cross_levels
    rim = lax.ppermute(
        filterbank[:, samples - RAW_HALO :],
        "tm",
        [(source, source + 1) for source in range(tm_count - 1)],
    )
    widened = jnp.concatenate([rim, filterbank], axis=1)
    local_plan = [
        (2**level, 2 ** (level + 1), channels >> (level + 1)) for level in range(local_levels)
    ]
    sub = samples // chan_count
    pieces = run_local(
        widened.astype(jnp.float32).reshape(channels, -1, LANES).transpose(1, 0, 2)[None],
        jnp.stack([first_rows, second_rows, shifts])[:, :local_levels, :channels],
        local_plan,
        chan_count,
        sub,
        RAW_HALO - SUB_HALO,
    )
    pieces, first_rows, second_rows, shifts = lax.optimization_barrier(
        (pieces, first_rows, second_rows, shifts)
    )
    window = sub + SUB_HALO
    layers = lax.all_to_all(pieces, "chan", split_axis=0, concat_axis=0, tiled=True)
    cross_plan = []
    bands = chan_count
    for level in range(local_levels, levels):
        bands //= 2
        rows_in = min(2**level, NDM)
        cross_plan.append((rows_in, min(2 ** (level + 1), NDM), bands, min(rows_in, NDM // 2)))
    plane = run_matmul_levels(
        layers.reshape(chan_count * channels, window),
        first_rows,
        second_rows,
        shifts,
        list(range(local_levels, levels)),
        cross_plan,
    )
    groups = chan_count * tm_count
    share = NDM // groups
    outgoing = plane.reshape(groups, share, sub)
    incoming = lax.all_to_all(outgoing, ("chan", "tm"), split_axis=0, concat_axis=0, tiled=True)
    series = (
        incoming.reshape(chan_count, tm_count, share, sub)
        .transpose(2, 1, 0, 3)
        .reshape(share, tm_count * samples)
    )
    return spectra(series, harmonic_bins)


def solution(mesh):
    in_specs = (P("chan", "tm"), P(), P(), P(), P())
    out_specs = (P(("chan", "tm"), None), P(("chan", "tm"), None))
    return jax.shard_map(
        on_device, mesh=mesh, in_specs=in_specs, out_specs=out_specs, check_vma=False
    )
```

```python
import functools
import math

import jax
import jax.numpy as jnp
from jax import lax
from jax.experimental import pallas as pl
from jax.experimental.pallas import tpu as pltpu
from jax.sharding import PartitionSpec as P

C = 4096
NDM = 2048
SHIFT = 16
DFT_OUTER = 64
HARM = 8
RAW_HALO = 256
SUB_HALO = 64
TILE = 512
LANES = 128
PIECES = 2
MESH = pl.DeviceIdType.MESH


def shift_right(value, amount):
    width = value.shape[-1]
    pad = [(0, 0)] * (value.ndim - 1) + [(amount, 0)]
    return jnp.pad(value, pad)[..., :width]


def merge_level(paired, rows_first, rows_second, delays):
    lower_bands = jnp.take(paired[0::2], rows_first, axis=1)
    upper_bands = jnp.take(paired[1::2], rows_second, axis=1)
    delay_col = delays[None, :, None]
    shifted = upper_bands
    for bit in (1, 2, 4, 8):
        shifted = jnp.where((delay_col & bit) != 0, shift_right(shifted, bit), shifted)
    return lower_bands + shifted


def level_merge(layers, first_rows, second_rows, shifts, level):
    count = min(2 ** (level + 1), NDM)
    return merge_level(
        layers, first_rows[level, :count], second_rows[level, :count], shifts[level, :count]
    )


def split_pieces(block):
    high = block.astype(jnp.bfloat16)
    low = (block - high.astype(jnp.float32)).astype(jnp.bfloat16)
    return high, low


def matmul_kernel(plan, x_ref, *refs):
    count = len(plan)
    tables = refs[: 3 * count]
    out_ref, buf_a, buf_b, parts = refs[3 * count :]
    width = x_ref.shape[1]
    source = x_ref
    for step, (row_in, row_out, bands_out, depth) in enumerate(plan):
        pick_low, pick_high, delay = tables[3 * step : 3 * step + 3]
        target = out_ref if step == count - 1 else (buf_a, buf_b)[step % 2]
        group = 2 if bands_out >= 2 else 1
        lanes = group * width
        for first_band in range(0, bands_out, group):
            for member in range(group):
                band = first_band + member
                for side in range(2):
                    block = source[pl.ds((2 * band + side) * row_in, depth), :]
                    for piece, value in enumerate(split_pieces(block)):
                        parts[side, piece, pl.ds(0, depth), pl.ds(member * width, width)] = value

            def tile(index, carry, target=target, first_band=first_band, depth=depth,
                     row_out=row_out, group=group, lanes=lanes,
                     pick_low=pick_low, pick_high=pick_high, delay=delay):
                rows = pl.ds(pl.multiple_of(index * TILE, TILE), TILE)
                low_sel = pick_low[rows, :]
                high_sel = pick_high[rows, :]
                lower = None
                upper = None
                for piece in range(PIECES):
                    term = jnp.dot(low_sel, parts[0, piece, pl.ds(0, depth), pl.ds(0, lanes)],
                                   preferred_element_type=jnp.float32)
                    lower = term if lower is None else lower + term
                    term = jnp.dot(high_sel, parts[1, piece, pl.ds(0, depth), pl.ds(0, lanes)],
                                   preferred_element_type=jnp.float32)
                    upper = term if upper is None else upper + term
                amount = delay[rows, :]
                for bit in (1, 2, 4, 8):
                    upper = jnp.where((amount & bit) != 0, pltpu.roll(upper, bit, 1), upper)
                merged = lower + upper
                skip = SUB_HALO if target is out_ref else 0
                for member in range(group):
                    start = pl.multiple_of((first_band + member) * row_out + index * TILE, TILE)
                    target[pl.ds(start, TILE), :] = merged[
                        :, member * width + skip : (member + 1) * width
                    ]
                return carry

            lax.fori_loop(0, row_out // TILE, tile, 0)
        source = target


def run_matmul_levels(state, first_rows, second_rows, shifts, levels, plan):
    width = state.shape[1]
    tables = []
    for level, (row_in, row_out, bands_out, depth) in zip(levels, plan):
        columns = jnp.arange(depth, dtype=jnp.int32)[None, :]
        tables.append((first_rows[level, :row_out, None] == columns).astype(jnp.bfloat16))
        tables.append((second_rows[level, :row_out, None] == columns).astype(jnp.bfloat16))
        tables.append(shifts[level, :row_out, None])
    buf_rows = max(p[1] * p[2] for p in plan)
    depth_most = max(p[3] for p in plan)
    vmem = pl.BlockSpec(memory_space=pltpu.VMEM)
    return pl.pallas_call(
        functools.partial(matmul_kernel, plan),
        out_shape=jax.ShapeDtypeStruct((plan[-1][1] * plan[-1][2], width - SUB_HALO), jnp.float32),
        in_specs=[vmem] * (1 + len(tables)),
        out_specs=vmem,
        scratch_shapes=[
            pltpu.VMEM((buf_rows, width), jnp.float32),
            pltpu.VMEM((buf_rows, width), jnp.float32),
            pltpu.VMEM((2, PIECES, depth_most, 2 * width), jnp.bfloat16),
        ],
        compiler_params=pltpu.CompilerParams(vmem_limit_bytes=60 * 1024 * 1024),
    )(state, *tables)


def harmonic_kernel(power_ref, offset_ref, out_ref):
    fundamentals = out_ref.shape[1]
    total = None
    for order in range(HARM):
        stride = order + 1
        offset = offset_ref[order]
        for phase in range(stride):
            picked = power_ref[pl.ds(phase, fundamentals, stride=stride), :]
            term = jnp.where(offset == phase, picked, 0.0)
            total = term if total is None else total + term
    out_ref[...] = jnp.transpose(total * (1.0 / HARM))


def delayed(value, amount):
    rolled = pltpu.roll(value, amount, 2)
    previous = jnp.concatenate([rolled[-1:], rolled[:-1]], axis=0)
    lane = lax.broadcasted_iota(jnp.int32, value.shape, 2)
    return jnp.where(lane < amount, previous, rolled)


def local_kernel(plan, sub, base, table_ref, x_ref, out_ref, *bufs):
    count = len(plan)
    final = bufs[-1]
    source = x_ref
    for step, (row_in, row_out, bands_out) in enumerate(plan):
        target = final if step == count - 1 else bufs[step]

        def body(row, carry, source=source, target=target, step=step,
                 bands_out=bands_out, last=step == count - 1):
            lower = source[table_ref[0, step, row], :, pl.ds(0, bands_out, stride=2), :]
            upper = source[table_ref[1, step, row], :, pl.ds(1, bands_out, stride=2), :]
            merged = lower + delayed(upper, table_ref[2, step, row])
            if last:
                target[:, pl.ds(row, 1), :] = merged
            else:
                target[row] = merged
            return carry

        lax.fori_loop(0, row_out, body, 0, unroll=min(row_out, 8))
        source = target
    for dest in range(out_ref.shape[0]):
        start = base + sub * dest
        slab, offset = start // LANES, start % LANES
        if offset == 0:
            out_ref[dest] = final[slab]
        else:
            lane = lax.broadcasted_iota(jnp.int32, final.shape[1:], 1)
            head = pltpu.roll(final[slab], LANES - offset, 1)
            tail = pltpu.roll(final[slab + 1], LANES - offset, 1)
            out_ref[dest] = jnp.where(lane < LANES - offset, head, tail)


def run_local(state, tables, plan, parts, sub, base):
    slabs = state.shape[1]
    rows_last = plan[-1][1]
    smem = pl.BlockSpec(memory_space=pltpu.SMEM)
    vmem = pl.BlockSpec(memory_space=pltpu.VMEM)
    scratch = [pltpu.VMEM((p[1], slabs, p[2], LANES), jnp.float32) for p in plan[:-1]]
    scratch.append(pltpu.VMEM((slabs, rows_last, LANES), jnp.float32))
    return pl.pallas_call(
        functools.partial(local_kernel, plan, sub, base),
        out_shape=jax.ShapeDtypeStruct((parts, rows_last, sub + SUB_HALO), jnp.float32),
        in_specs=[smem, vmem],
        out_specs=vmem,
        scratch_shapes=scratch,
        compiler_params=pltpu.CompilerParams(vmem_limit_bytes=56 * 1024 * 1024),
    )(tables, state)


def exchange_kernel(axis, parts_ref, out_ref, landing, send_sem, recv_sem, local_sem):
    count = parts_ref.shape[0]
    me = lax.axis_index(axis)
    barrier = pltpu.get_barrier_semaphore()
    for step in range(1, count):
        pl.semaphore_signal(
            barrier, inc=1, device_id={axis: lax.rem(me + step, count)}, device_id_type=MESH
        )
    pl.semaphore_wait(barrier, count - 1)
    sends = []
    for step in range(1, count):
        peer = lax.rem(me + step, count)
        copy = pltpu.make_async_remote_copy(
            src_ref=parts_ref.at[peer],
            dst_ref=landing.at[me],
            send_sem=send_sem.at[step],
            recv_sem=recv_sem.at[step],
            device_id={axis: peer},
            device_id_type=MESH,
        )
        copy.start()
        sends.append(copy)
    local = pltpu.make_async_copy(parts_ref.at[me], landing.at[me], local_sem)
    local.start()
    local.wait()
    for step in range(1, count):
        sends[step - 1].wait_send()
        origin = lax.rem(me - step + count, count)
        pltpu.make_async_remote_copy(
            src_ref=parts_ref.at[origin],
            dst_ref=landing.at[origin],
            send_sem=send_sem.at[step],
            recv_sem=recv_sem.at[step],
            device_id={axis: origin},
            device_id_type=MESH,
        ).wait_recv()
    out_ref[...] = landing[...]


def exchange(parts, axis):
    count = parts.shape[0]
    vmem = pl.BlockSpec(memory_space=pltpu.VMEM)
    return pl.pallas_call(
        functools.partial(exchange_kernel, axis),
        out_shape=jax.ShapeDtypeStruct(parts.shape, parts.dtype),
        in_specs=[vmem],
        out_specs=vmem,
        scratch_shapes=[
            pltpu.VMEM(parts.shape, parts.dtype),
            pltpu.SemaphoreType.DMA((count,)),
            pltpu.SemaphoreType.DMA((count,)),
            pltpu.SemaphoreType.DMA(()),
        ],
        compiler_params=pltpu.CompilerParams(
            collective_id=0, has_side_effects=True, vmem_limit_bytes=32 * 1024 * 1024
        ),
    )(parts)


def spectra(series, harmonic_bins):
    count = series.shape[0]
    total = series.shape[1]
    outer = DFT_OUTER
    inner = total // outer
    half_inner = inner // 2
    highest = lax.Precision.HIGHEST
    grid = series.reshape(count, outer, inner)
    outer_index = jnp.arange(outer, dtype=jnp.int32)
    inner_index = jnp.arange(inner, dtype=jnp.int32)
    half_index = jnp.arange(half_inner, dtype=jnp.int32)
    angle_outer = (
        2.0
        * math.pi
        / outer
        * (outer_index[:, None] * outer_index[None, :] % outer).astype(jnp.float32)
    )
    outer_table = jnp.concatenate([jnp.cos(angle_outer), jnp.sin(angle_outer)], axis=1)
    section_one = jnp.einsum("npq,pk->nkq", grid, outer_table, precision=highest)
    section_re = section_one[:, :outer]
    section_im = -section_one[:, outer:]
    angle_twist = (
        2.0
        * math.pi
        / total
        * (outer_index[:, None] * inner_index[None, :] % total).astype(jnp.float32)
    )
    twist_cos = jnp.cos(angle_twist)
    twist_sin = jnp.sin(angle_twist)
    rotated = jnp.stack(
        [
            section_re * twist_cos + section_im * twist_sin,
            section_im * twist_cos - section_re * twist_sin,
        ]
    )
    angle_inner = (
        2.0
        * math.pi
        / inner
        * (inner_index[:, None] * half_index[None, :] % inner).astype(jnp.float32)
    )
    inner_table = jnp.concatenate([jnp.cos(angle_inner), jnp.sin(angle_inner)], axis=1)
    section_two = jnp.einsum("snkq,qm->snkm", rotated, inner_table, precision=highest)
    final_re = section_two[0, :, :, :half_inner] + section_two[1, :, :, half_inner:]
    final_im = section_two[1, :, :, :half_inner] - section_two[0, :, :, half_inner:]
    spectrum_power = (final_re * final_re + final_im * final_im) / (C * total)
    spectrum_power = jnp.transpose(spectrum_power, (0, 2, 1)).reshape(count, total // 2)
    fundamentals = harmonic_bins.shape[1]
    fundamental = jnp.arange(fundamentals, dtype=jnp.int32)
    stride = jnp.arange(1, HARM + 1, dtype=jnp.int32)[:, None]
    offsets = (harmonic_bins - stride * fundamental[None, :])[:, :, None]
    vmem = pl.BlockSpec(memory_space=pltpu.VMEM)
    harmonic = pl.pallas_call(
        harmonic_kernel,
        out_shape=jax.ShapeDtypeStruct((count, fundamentals), jnp.float32),
        in_specs=[vmem, vmem],
        out_specs=vmem,
    )(jnp.transpose(spectrum_power), offsets)
    return spectrum_power, harmonic


def on_device(filterbank, first_rows, second_rows, shifts, harmonic_bins):
    channels = filterbank.shape[0]
    samples = filterbank.shape[1]
    local_levels = channels.bit_length() - 1
    chan_count = lax.axis_size("chan")
    tm_count = lax.axis_size("tm")
    cross_levels = chan_count.bit_length() - 1
    levels = local_levels + cross_levels
    rim = lax.ppermute(
        filterbank[:, samples - RAW_HALO :],
        "tm",
        [(source, source + 1) for source in range(tm_count - 1)],
    )
    widened = jnp.concatenate([rim, filterbank], axis=1)
    local_plan = [
        (2**level, 2 ** (level + 1), channels >> (level + 1)) for level in range(local_levels)
    ]
    sub = samples // chan_count
    pieces = run_local(
        widened.astype(jnp.float32).reshape(channels, -1, LANES).transpose(1, 0, 2)[None],
        jnp.stack([first_rows, second_rows, shifts])[:, :local_levels, :channels],
        local_plan,
        chan_count,
        sub,
        RAW_HALO - SUB_HALO,
    )
    pieces, first_rows, second_rows, shifts = lax.optimization_barrier(
        (pieces, first_rows, second_rows, shifts)
    )
    window = sub + SUB_HALO
    layers = exchange(pieces, "chan")
    cross_plan = []
    bands = chan_count
    for level in range(local_levels, levels):
        bands //= 2
        rows_in = min(2**level, NDM)
        cross_plan.append((rows_in, min(2 ** (level + 1), NDM), bands, min(rows_in, NDM // 2)))
    plane = run_matmul_levels(
        layers.reshape(chan_count * channels, window),
        first_rows,
        second_rows,
        shifts,
        list(range(local_levels, levels)),
        cross_plan,
    )
    groups = chan_count * tm_count
    share = NDM // groups
    outgoing = plane.reshape(groups, share, sub)
    incoming = lax.all_to_all(outgoing, ("chan", "tm"), split_axis=0, concat_axis=0, tiled=True)
    series = (
        incoming.reshape(chan_count, tm_count, share, sub)
        .transpose(2, 1, 0, 3)
        .reshape(share, tm_count * samples)
    )
    return spectra(series, harmonic_bins)


def solution(mesh):
    in_specs = (P("chan", "tm"), P(), P(), P(), P())
    out_specs = (P(("chan", "tm"), None), P(("chan", "tm"), None))
    return jax.shard_map(
        on_device, mesh=mesh, in_specs=in_specs, out_specs=out_specs, check_vma=False
    )
```

```python
import functools
import math

import jax
import jax.numpy as jnp
from jax import lax
from jax.experimental import pallas as pl
from jax.experimental.pallas import tpu as pltpu
from jax.sharding import PartitionSpec as P

C = 4096
NDM = 2048
SHIFT = 16
DFT_OUTER = 64
HARM = 8
RAW_HALO = 256
SUB_HALO = 64
TILE = 512
LANES = 128
PIECES = 2


def shift_right(value, amount):
    width = value.shape[-1]
    pad = [(0, 0)] * (value.ndim - 1) + [(amount, 0)]
    return jnp.pad(value, pad)[..., :width]


def merge_level(paired, rows_first, rows_second, delays):
    lower_bands = jnp.take(paired[0::2], rows_first, axis=1)
    upper_bands = jnp.take(paired[1::2], rows_second, axis=1)
    delay_col = delays[None, :, None]
    shifted = upper_bands
    for bit in (1, 2, 4, 8):
        shifted = jnp.where((delay_col & bit) != 0, shift_right(shifted, bit), shifted)
    return lower_bands + shifted


def level_merge(layers, first_rows, second_rows, shifts, level):
    count = min(2 ** (level + 1), NDM)
    return merge_level(
        layers, first_rows[level, :count], second_rows[level, :count], shifts[level, :count]
    )


def split_pieces(block):
    high = block.astype(jnp.bfloat16)
    low = (block - high.astype(jnp.float32)).astype(jnp.bfloat16)
    return high, low


def matmul_kernel(plan, x_ref, *refs):
    count = len(plan)
    tables = refs[: 3 * count]
    out_ref, buf_a, buf_b, parts, pack = refs[3 * count :]
    width = x_ref.shape[1]
    source = x_ref
    for step, (row_in, row_out, bands_out, depth) in enumerate(plan):
        pick_low, pick_high, delay = tables[3 * step : 3 * step + 3]
        target = out_ref if step == count - 1 else (buf_a, buf_b)[step % 2]
        group = 2 if bands_out >= 2 else 1
        lanes = group * width
        for first_band in range(0, bands_out, group):
            for member in range(group):
                band = first_band + member
                for side in range(2):
                    block = source[pl.ds((2 * band + side) * row_in, depth), :]
                    for piece, value in enumerate(split_pieces(block)):
                        parts[side, piece, pl.ds(0, depth), pl.ds(member * width, width)] = value

            def tile(index, carry, target=target, first_band=first_band, depth=depth,
                     row_out=row_out, group=group, lanes=lanes,
                     pick_low=pick_low, pick_high=pick_high, delay=delay):
                rows = pl.ds(pl.multiple_of(index * TILE, TILE), TILE)
                low_sel = pick_low[rows, :]
                high_sel = pick_high[rows, :]
                lower = None
                upper = None
                for piece in range(PIECES):
                    term = jnp.dot(low_sel, parts[0, piece, pl.ds(0, depth), pl.ds(0, lanes)],
                                   preferred_element_type=jnp.float32)
                    lower = term if lower is None else lower + term
                    term = jnp.dot(high_sel, parts[1, piece, pl.ds(0, depth), pl.ds(0, lanes)],
                                   preferred_element_type=jnp.float32)
                    upper = term if upper is None else upper + term
                amount = delay[rows, :]
                for bit in (1, 2, 4, 8):
                    upper = jnp.where((amount & bit) != 0, pltpu.roll(upper, bit, 1), upper)
                merged = lower + upper
                if target is out_ref:
                    pack[...] = merged
                    even = pack[pl.ds(0, TILE // 2, stride=2), :]
                    odd = pack[pl.ds(1, TILE // 2, stride=2), :]
                    lane = lax.broadcasted_iota(jnp.int32, even.shape, 1)
                    start = pl.multiple_of(index * (TILE // 2), TILE // 2)
                    target[pl.ds(start, TILE // 2), :] = jnp.where(
                        lane < SUB_HALO, pltpu.roll(even, SUB_HALO, 1), odd
                    )
                    return carry
                for member in range(group):
                    start = pl.multiple_of((first_band + member) * row_out + index * TILE, TILE)
                    target[pl.ds(start, TILE), :] = merged[:, member * width : (member + 1) * width]
                return carry

            lax.fori_loop(0, row_out // TILE, tile, 0)
        source = target


def run_matmul_levels(state, first_rows, second_rows, shifts, levels, plan):
    width = state.shape[1]
    tables = []
    for level, (row_in, row_out, bands_out, depth) in zip(levels, plan):
        columns = jnp.arange(depth, dtype=jnp.int32)[None, :]
        tables.append((first_rows[level, :row_out, None] == columns).astype(jnp.bfloat16))
        tables.append((second_rows[level, :row_out, None] == columns).astype(jnp.bfloat16))
        tables.append(shifts[level, :row_out, None])
    buf_rows = max(p[1] * p[2] for p in plan)
    depth_most = max(p[3] for p in plan)
    vmem = pl.BlockSpec(memory_space=pltpu.VMEM)
    return pl.pallas_call(
        functools.partial(matmul_kernel, plan),
        out_shape=jax.ShapeDtypeStruct((plan[-1][1] * plan[-1][2] // 2, width), jnp.float32),
        in_specs=[vmem] * (1 + len(tables)),
        out_specs=vmem,
        scratch_shapes=[
            pltpu.VMEM((buf_rows, width), jnp.float32),
            pltpu.VMEM((buf_rows, width), jnp.float32),
            pltpu.VMEM((2, PIECES, depth_most, 2 * width), jnp.bfloat16),
            pltpu.VMEM((TILE, width), jnp.float32),
        ],
        compiler_params=pltpu.CompilerParams(vmem_limit_bytes=60 * 1024 * 1024),
    )(state, *tables)


def harmonic_kernel(power_ref, offset_ref, out_ref):
    fundamentals = out_ref.shape[1]
    total = None
    for order in range(HARM):
        stride = order + 1
        offset = offset_ref[order]
        for phase in range(stride):
            picked = power_ref[pl.ds(phase, fundamentals, stride=stride), :]
            term = jnp.where(offset == phase, picked, 0.0)
            total = term if total is None else total + term
    out_ref[...] = jnp.transpose(total * (1.0 / HARM))


def delayed(value, amount):
    rolled = pltpu.roll(value, amount, 2)
    previous = jnp.concatenate([rolled[-1:], rolled[:-1]], axis=0)
    lane = lax.broadcasted_iota(jnp.int32, value.shape, 2)
    return jnp.where(lane < amount, previous, rolled)


def local_kernel(plan, sub, base, table_ref, x_ref, out_ref, *bufs):
    count = len(plan)
    final = bufs[-1]
    source = x_ref
    for step, (row_in, row_out, bands_out) in enumerate(plan):
        target = final if step == count - 1 else bufs[step]

        def body(row, carry, source=source, target=target, step=step,
                 bands_out=bands_out, last=step == count - 1):
            lower = source[table_ref[0, step, row], :, pl.ds(0, bands_out, stride=2), :]
            upper = source[table_ref[1, step, row], :, pl.ds(1, bands_out, stride=2), :]
            merged = lower + delayed(upper, table_ref[2, step, row])
            if last:
                target[:, pl.ds(row, 1), :] = merged
            else:
                target[row] = merged
            return carry

        lax.fori_loop(0, row_out, body, 0, unroll=min(row_out, 8))
        source = target
    for dest in range(out_ref.shape[0]):
        start = base + sub * dest
        slab, offset = start // LANES, start % LANES
        if offset == 0:
            out_ref[dest] = final[slab]
        else:
            lane = lax.broadcasted_iota(jnp.int32, final.shape[1:], 1)
            head = pltpu.roll(final[slab], LANES - offset, 1)
            tail = pltpu.roll(final[slab + 1], LANES - offset, 1)
            out_ref[dest] = jnp.where(lane < LANES - offset, head, tail)


def run_local(state, tables, plan, parts, sub, base):
    slabs = state.shape[1]
    rows_last = plan[-1][1]
    smem = pl.BlockSpec(memory_space=pltpu.SMEM)
    vmem = pl.BlockSpec(memory_space=pltpu.VMEM)
    scratch = [pltpu.VMEM((p[1], slabs, p[2], LANES), jnp.float32) for p in plan[:-1]]
    scratch.append(pltpu.VMEM((slabs, rows_last, LANES), jnp.float32))
    return pl.pallas_call(
        functools.partial(local_kernel, plan, sub, base),
        out_shape=jax.ShapeDtypeStruct((parts, rows_last, sub + SUB_HALO), jnp.float32),
        in_specs=[smem, vmem],
        out_specs=vmem,
        scratch_shapes=scratch,
        compiler_params=pltpu.CompilerParams(vmem_limit_bytes=56 * 1024 * 1024),
    )(tables, state)


def spectra(series, harmonic_bins):
    count = series.shape[0]
    total = series.shape[1]
    outer = DFT_OUTER
    inner = total // outer
    half_inner = inner // 2
    highest = lax.Precision.HIGHEST
    grid = series.reshape(count, outer, inner)
    outer_index = jnp.arange(outer, dtype=jnp.int32)
    inner_index = jnp.arange(inner, dtype=jnp.int32)
    half_index = jnp.arange(half_inner, dtype=jnp.int32)
    angle_outer = (
        2.0
        * math.pi
        / outer
        * (outer_index[:, None] * outer_index[None, :] % outer).astype(jnp.float32)
    )
    outer_table = jnp.concatenate([jnp.cos(angle_outer), jnp.sin(angle_outer)], axis=1)
    section_one = jnp.einsum("npq,pk->nkq", grid, outer_table, precision=highest)
    section_re = section_one[:, :outer]
    section_im = -section_one[:, outer:]
    angle_twist = (
        2.0
        * math.pi
        / total
        * (outer_index[:, None] * inner_index[None, :] % total).astype(jnp.float32)
    )
    twist_cos = jnp.cos(angle_twist)
    twist_sin = jnp.sin(angle_twist)
    rotated = jnp.stack(
        [
            section_re * twist_cos + section_im * twist_sin,
            section_im * twist_cos - section_re * twist_sin,
        ]
    )
    angle_inner = (
        2.0
        * math.pi
        / inner
        * (inner_index[:, None] * half_index[None, :] % inner).astype(jnp.float32)
    )
    inner_table = jnp.concatenate([jnp.cos(angle_inner), jnp.sin(angle_inner)], axis=1)
    section_two = jnp.einsum("snkq,qm->snkm", rotated, inner_table, precision=highest)
    final_re = section_two[0, :, :, :half_inner] + section_two[1, :, :, half_inner:]
    final_im = section_two[1, :, :, :half_inner] - section_two[0, :, :, half_inner:]
    spectrum_power = (final_re * final_re + final_im * final_im) / (C * total)
    spectrum_power = jnp.transpose(spectrum_power, (0, 2, 1)).reshape(count, total // 2)
    fundamentals = harmonic_bins.shape[1]
    fundamental = jnp.arange(fundamentals, dtype=jnp.int32)
    stride = jnp.arange(1, HARM + 1, dtype=jnp.int32)[:, None]
    offsets = (harmonic_bins - stride * fundamental[None, :])[:, :, None]
    vmem = pl.BlockSpec(memory_space=pltpu.VMEM)
    harmonic = pl.pallas_call(
        harmonic_kernel,
        out_shape=jax.ShapeDtypeStruct((count, fundamentals), jnp.float32),
        in_specs=[vmem, vmem],
        out_specs=vmem,
    )(jnp.transpose(spectrum_power), offsets)
    return spectrum_power, harmonic


def on_device(filterbank, first_rows, second_rows, shifts, harmonic_bins):
    channels = filterbank.shape[0]
    samples = filterbank.shape[1]
    local_levels = channels.bit_length() - 1
    chan_count = lax.axis_size("chan")
    tm_count = lax.axis_size("tm")
    cross_levels = chan_count.bit_length() - 1
    levels = local_levels + cross_levels
    rim = lax.ppermute(
        filterbank[:, samples - RAW_HALO :],
        "tm",
        [(source, source + 1) for source in range(tm_count - 1)],
    )
    widened = jnp.concatenate([rim, filterbank], axis=1)
    local_plan = [
        (2**level, 2 ** (level + 1), channels >> (level + 1)) for level in range(local_levels)
    ]
    sub = samples // chan_count
    pieces = run_local(
        widened.astype(jnp.float32).reshape(channels, -1, LANES).transpose(1, 0, 2)[None],
        jnp.stack([first_rows, second_rows, shifts])[:, :local_levels, :channels],
        local_plan,
        chan_count,
        sub,
        RAW_HALO - SUB_HALO,
    )
    pieces, first_rows, second_rows, shifts = lax.optimization_barrier(
        (pieces, first_rows, second_rows, shifts)
    )
    window = sub + SUB_HALO
    layers = lax.all_to_all(pieces, "chan", split_axis=0, concat_axis=0, tiled=True)
    cross_plan = []
    bands = chan_count
    for level in range(local_levels, levels):
        bands //= 2
        rows_in = min(2**level, NDM)
        cross_plan.append((rows_in, min(2 ** (level + 1), NDM), bands, min(rows_in, NDM // 2)))
    plane = run_matmul_levels(
        layers.reshape(chan_count * channels, window),
        first_rows,
        second_rows,
        shifts,
        list(range(local_levels, levels)),
        cross_plan,
    )
    groups = chan_count * tm_count
    share = NDM // groups
    outgoing = plane.reshape(groups, share // 2, 2 * sub)
    incoming = lax.all_to_all(outgoing, ("chan", "tm"), split_axis=0, concat_axis=0, tiled=True)
    series = (
        incoming.reshape(chan_count, tm_count, share // 2, 2, sub)
        .transpose(2, 3, 1, 0, 4)
        .reshape(share, tm_count * samples)
    )
    return spectra(series, harmonic_bins)


def solution(mesh):
    in_specs = (P("chan", "tm"), P(), P(), P(), P())
    out_specs = (P(("chan", "tm"), None), P(("chan", "tm"), None))
    return jax.shard_map(
        on_device, mesh=mesh, in_specs=in_specs, out_specs=out_specs, check_vma=False
    )
```

```python
import functools
import math

import jax
import jax.numpy as jnp
from jax import lax
from jax.experimental import pallas as pl
from jax.experimental.pallas import tpu as pltpu
from jax.sharding import PartitionSpec as P

C = 4096
NDM = 2048
SHIFT = 16
DFT_OUTER = 64
HARM = 8
RAW_HALO = 256
SUB_HALO = 64
TILE = 1024
LANES = 128
PIECES = 2


def shift_right(value, amount):
    width = value.shape[-1]
    pad = [(0, 0)] * (value.ndim - 1) + [(amount, 0)]
    return jnp.pad(value, pad)[..., :width]


def merge_level(paired, rows_first, rows_second, delays):
    lower_bands = jnp.take(paired[0::2], rows_first, axis=1)
    upper_bands = jnp.take(paired[1::2], rows_second, axis=1)
    delay_col = delays[None, :, None]
    shifted = upper_bands
    for bit in (1, 2, 4, 8):
        shifted = jnp.where((delay_col & bit) != 0, shift_right(shifted, bit), shifted)
    return lower_bands + shifted


def level_merge(layers, first_rows, second_rows, shifts, level):
    count = min(2 ** (level + 1), NDM)
    return merge_level(
        layers, first_rows[level, :count], second_rows[level, :count], shifts[level, :count]
    )


def split_pieces(block):
    high = block.astype(jnp.bfloat16)
    low = (block - high.astype(jnp.float32)).astype(jnp.bfloat16)
    return high, low


def matmul_kernel(plan, x_ref, *refs):
    count = len(plan)
    tables = refs[: 3 * count]
    out_ref, buf_a, buf_b, parts, pack = refs[3 * count :]
    width = x_ref.shape[1]
    source = x_ref
    for step, (row_in, row_out, bands_out, depth) in enumerate(plan):
        pick_low, pick_high, delay = tables[3 * step : 3 * step + 3]
        target = out_ref if step == count - 1 else (buf_a, buf_b)[step % 2]
        group = 2 if bands_out >= 2 else 1
        lanes = group * width
        tile_rows = min(TILE, row_out)
        for first_band in range(0, bands_out, group):
            for member in range(group):
                band = first_band + member
                for side in range(2):
                    block = source[pl.ds((2 * band + side) * row_in, depth), :]
                    for piece, value in enumerate(split_pieces(block)):
                        parts[side, piece, pl.ds(0, depth), pl.ds(member * width, width)] = value

            def tile(index, carry, target=target, first_band=first_band, depth=depth,
                     row_out=row_out, group=group, lanes=lanes, tile_rows=tile_rows,
                     pick_low=pick_low, pick_high=pick_high, delay=delay):
                rows = pl.ds(pl.multiple_of(index * tile_rows, tile_rows), tile_rows)
                low_sel = pick_low[rows, :]
                high_sel = pick_high[rows, :]
                lower = None
                upper = None
                for piece in range(PIECES):
                    term = jnp.dot(low_sel, parts[0, piece, pl.ds(0, depth), pl.ds(0, lanes)],
                                   preferred_element_type=jnp.float32)
                    lower = term if lower is None else lower + term
                    term = jnp.dot(high_sel, parts[1, piece, pl.ds(0, depth), pl.ds(0, lanes)],
                                   preferred_element_type=jnp.float32)
                    upper = term if upper is None else upper + term
                amount = delay[rows, :]
                for bit in (1, 2, 4, 8):
                    upper = jnp.where((amount & bit) != 0, pltpu.roll(upper, bit, 1), upper)
                merged = lower + upper
                if target is out_ref:
                    pack[...] = merged
                    even = pack[pl.ds(0, tile_rows // 2, stride=2), :]
                    odd = pack[pl.ds(1, tile_rows // 2, stride=2), :]
                    lane = lax.broadcasted_iota(jnp.int32, even.shape, 1)
                    start = pl.multiple_of(index * (tile_rows // 2), tile_rows // 2)
                    target[pl.ds(start, tile_rows // 2), :] = jnp.where(
                        lane < SUB_HALO, pltpu.roll(even, SUB_HALO, 1), odd
                    )
                    return carry
                for member in range(group):
                    start = pl.multiple_of((first_band + member) * row_out + index * tile_rows, tile_rows)
                    target[pl.ds(start, tile_rows), :] = merged[:, member * width : (member + 1) * width]
                return carry

            lax.fori_loop(0, row_out // tile_rows, tile, 0)
        source = target


def run_matmul_levels(state, first_rows, second_rows, shifts, levels, plan):
    width = state.shape[1]
    tables = []
    for level, (row_in, row_out, bands_out, depth) in zip(levels, plan):
        columns = jnp.arange(depth, dtype=jnp.int32)[None, :]
        tables.append((first_rows[level, :row_out, None] == columns).astype(jnp.bfloat16))
        tables.append((second_rows[level, :row_out, None] == columns).astype(jnp.bfloat16))
        tables.append(shifts[level, :row_out, None])
    buf_rows = max(p[1] * p[2] for p in plan)
    depth_most = max(p[3] for p in plan)
    vmem = pl.BlockSpec(memory_space=pltpu.VMEM)
    return pl.pallas_call(
        functools.partial(matmul_kernel, plan),
        out_shape=jax.ShapeDtypeStruct((plan[-1][1] * plan[-1][2] // 2, width), jnp.float32),
        in_specs=[vmem] * (1 + len(tables)),
        out_specs=vmem,
        scratch_shapes=[
            pltpu.VMEM((buf_rows, width), jnp.float32),
            pltpu.VMEM((buf_rows, width), jnp.float32),
            pltpu.VMEM((2, PIECES, depth_most, 2 * width), jnp.bfloat16),
            pltpu.VMEM((min(TILE, plan[-1][1]), width), jnp.float32),
        ],
        compiler_params=pltpu.CompilerParams(vmem_limit_bytes=60 * 1024 * 1024),
    )(state, *tables)


def harmonic_kernel(power_ref, offset_ref, out_ref):
    fundamentals = out_ref.shape[1]
    total = None
    for order in range(HARM):
        stride = order + 1
        offset = offset_ref[order]
        for phase in range(stride):
            picked = power_ref[pl.ds(phase, fundamentals, stride=stride), :]
            term = jnp.where(offset == phase, picked, 0.0)
            total = term if total is None else total + term
    out_ref[...] = jnp.transpose(total * (1.0 / HARM))


def delayed(value, amount):
    rolled = pltpu.roll(value, amount, 2)
    previous = jnp.concatenate([rolled[-1:], rolled[:-1]], axis=0)
    lane = lax.broadcasted_iota(jnp.int32, value.shape, 2)
    return jnp.where(lane < amount, previous, rolled)


def local_kernel(plan, sub, base, table_ref, x_ref, out_ref, *bufs):
    count = len(plan)
    final = bufs[-1]
    source = x_ref
    for step, (row_in, row_out, bands_out) in enumerate(plan):
        target = final if step == count - 1 else bufs[step]

        def body(row, carry, source=source, target=target, step=step,
                 bands_out=bands_out, last=step == count - 1):
            lower = source[table_ref[0, step, row], :, pl.ds(0, bands_out, stride=2), :]
            upper = source[table_ref[1, step, row], :, pl.ds(1, bands_out, stride=2), :]
            merged = lower + delayed(upper, table_ref[2, step, row])
            if last:
                target[:, pl.ds(row, 1), :] = merged
            else:
                target[row] = merged
            return carry

        lax.fori_loop(0, row_out, body, 0, unroll=min(row_out, 16))
        source = target
    for dest in range(out_ref.shape[0]):
        start = base + sub * dest
        slab, offset = start // LANES, start % LANES
        if offset == 0:
            out_ref[dest] = final[slab]
        else:
            lane = lax.broadcasted_iota(jnp.int32, final.shape[1:], 1)
            head = pltpu.roll(final[slab], LANES - offset, 1)
            tail = pltpu.roll(final[slab + 1], LANES - offset, 1)
            out_ref[dest] = jnp.where(lane < LANES - offset, head, tail)


def run_local(state, tables, plan, parts, sub, base):
    slabs = state.shape[1]
    rows_last = plan[-1][1]
    smem = pl.BlockSpec(memory_space=pltpu.SMEM)
    vmem = pl.BlockSpec(memory_space=pltpu.VMEM)
    scratch = [pltpu.VMEM((p[1], slabs, p[2], LANES), jnp.float32) for p in plan[:-1]]
    scratch.append(pltpu.VMEM((slabs, rows_last, LANES), jnp.float32))
    return pl.pallas_call(
        functools.partial(local_kernel, plan, sub, base),
        out_shape=jax.ShapeDtypeStruct((parts, rows_last, sub + SUB_HALO), jnp.float32),
        in_specs=[smem, vmem],
        out_specs=vmem,
        scratch_shapes=scratch,
        compiler_params=pltpu.CompilerParams(vmem_limit_bytes=56 * 1024 * 1024),
    )(tables, state)


def spectra(series, harmonic_bins):
    count = series.shape[0]
    total = series.shape[1]
    outer = DFT_OUTER
    inner = total // outer
    half_inner = inner // 2
    highest = lax.Precision.HIGHEST
    grid = series.reshape(count, outer, inner)
    outer_index = jnp.arange(outer, dtype=jnp.int32)
    inner_index = jnp.arange(inner, dtype=jnp.int32)
    half_index = jnp.arange(half_inner, dtype=jnp.int32)
    angle_outer = (
        2.0
        * math.pi
        / outer
        * (outer_index[:, None] * outer_index[None, :] % outer).astype(jnp.float32)
    )
    outer_table = jnp.concatenate([jnp.cos(angle_outer), jnp.sin(angle_outer)], axis=1)
    section_one = jnp.einsum("npq,pk->nkq", grid, outer_table, precision=highest)
    section_re = section_one[:, :outer]
    section_im = -section_one[:, outer:]
    angle_twist = (
        2.0
        * math.pi
        / total
        * (outer_index[:, None] * inner_index[None, :] % total).astype(jnp.float32)
    )
    twist_cos = jnp.cos(angle_twist)
    twist_sin = jnp.sin(angle_twist)
    rotated = jnp.stack(
        [
            section_re * twist_cos + section_im * twist_sin,
            section_im * twist_cos - section_re * twist_sin,
        ]
    )
    angle_inner = (
        2.0
        * math.pi
        / inner
        * (inner_index[:, None] * half_index[None, :] % inner).astype(jnp.float32)
    )
    inner_table = jnp.concatenate([jnp.cos(angle_inner), jnp.sin(angle_inner)], axis=1)
    section_two = jnp.einsum("snkq,qm->snkm", rotated, inner_table, precision=highest)
    final_re = section_two[0, :, :, :half_inner] + section_two[1, :, :, half_inner:]
    final_im = section_two[1, :, :, :half_inner] - section_two[0, :, :, half_inner:]
    spectrum_power = (final_re * final_re + final_im * final_im) / (C * total)
    spectrum_power = jnp.transpose(spectrum_power, (0, 2, 1)).reshape(count, total // 2)
    fundamentals = harmonic_bins.shape[1]
    fundamental = jnp.arange(fundamentals, dtype=jnp.int32)
    stride = jnp.arange(1, HARM + 1, dtype=jnp.int32)[:, None]
    offsets = (harmonic_bins - stride * fundamental[None, :])[:, :, None]
    vmem = pl.BlockSpec(memory_space=pltpu.VMEM)
    harmonic = pl.pallas_call(
        harmonic_kernel,
        out_shape=jax.ShapeDtypeStruct((count, fundamentals), jnp.float32),
        in_specs=[vmem, vmem],
        out_specs=vmem,
    )(jnp.transpose(spectrum_power), offsets)
    return spectrum_power, harmonic


def on_device(filterbank, first_rows, second_rows, shifts, harmonic_bins):
    channels = filterbank.shape[0]
    samples = filterbank.shape[1]
    local_levels = channels.bit_length() - 1
    chan_count = lax.axis_size("chan")
    tm_count = lax.axis_size("tm")
    cross_levels = chan_count.bit_length() - 1
    levels = local_levels + cross_levels
    rim = lax.ppermute(
        filterbank[:, samples - RAW_HALO :],
        "tm",
        [(source, source + 1) for source in range(tm_count - 1)],
    )
    widened = jnp.concatenate([rim, filterbank], axis=1)
    local_plan = [
        (2**level, 2 ** (level + 1), channels >> (level + 1)) for level in range(local_levels)
    ]
    sub = samples // chan_count
    pieces = run_local(
        widened.astype(jnp.float32).reshape(channels, -1, LANES).transpose(1, 0, 2)[None],
        jnp.stack([first_rows, second_rows, shifts])[:, :local_levels, :channels],
        local_plan,
        chan_count,
        sub,
        RAW_HALO - SUB_HALO,
    )
    pieces, first_rows, second_rows, shifts = lax.optimization_barrier(
        (pieces, first_rows, second_rows, shifts)
    )
    window = sub + SUB_HALO
    layers = lax.all_to_all(pieces, "chan", split_axis=0, concat_axis=0, tiled=True)
    cross_plan = []
    bands = chan_count
    for level in range(local_levels, levels):
        bands //= 2
        rows_in = min(2**level, NDM)
        cross_plan.append((rows_in, min(2 ** (level + 1), NDM), bands, min(rows_in, NDM // 2)))
    plane = run_matmul_levels(
        layers.reshape(chan_count * channels, window),
        first_rows,
        second_rows,
        shifts,
        list(range(local_levels, levels)),
        cross_plan,
    )
    groups = chan_count * tm_count
    share = NDM // groups
    outgoing = plane.reshape(groups, share // 2, 2 * sub)
    incoming = lax.all_to_all(outgoing, ("chan", "tm"), split_axis=0, concat_axis=0, tiled=True)
    series = (
        incoming.reshape(chan_count, tm_count, share // 2, 2, sub)
        .transpose(2, 3, 1, 0, 4)
        .reshape(share, tm_count * samples)
    )
    return spectra(series, harmonic_bins)


def solution(mesh):
    in_specs = (P("chan", "tm"), P(), P(), P(), P())
    out_specs = (P(("chan", "tm"), None), P(("chan", "tm"), None))
    return jax.shard_map(
        on_device, mesh=mesh, in_specs=in_specs, out_specs=out_specs, check_vma=False
    )
```

```python
import functools
import math

import jax
import jax.numpy as jnp
from jax import lax
from jax.experimental import pallas as pl
from jax.experimental.pallas import tpu as pltpu
from jax.sharding import PartitionSpec as P

C = 4096
NDM = 2048
SHIFT = 16
DFT_OUTER = 64
HARM = 8
RAW_HALO = 256
SUB_HALO = 64
TILE = 1024
LANES = 128
PIECES = 2


def shift_right(value, amount):
    width = value.shape[-1]
    pad = [(0, 0)] * (value.ndim - 1) + [(amount, 0)]
    return jnp.pad(value, pad)[..., :width]


def merge_level(paired, rows_first, rows_second, delays):
    lower_bands = jnp.take(paired[0::2], rows_first, axis=1)
    upper_bands = jnp.take(paired[1::2], rows_second, axis=1)
    delay_col = delays[None, :, None]
    shifted = upper_bands
    for bit in (1, 2, 4, 8):
        shifted = jnp.where((delay_col & bit) != 0, shift_right(shifted, bit), shifted)
    return lower_bands + shifted


def level_merge(layers, first_rows, second_rows, shifts, level):
    count = min(2 ** (level + 1), NDM)
    return merge_level(
        layers, first_rows[level, :count], second_rows[level, :count], shifts[level, :count]
    )


def split_pieces(block):
    high = block.astype(jnp.bfloat16)
    low = (block - high.astype(jnp.float32)).astype(jnp.bfloat16)
    return high, low


def matmul_kernel(plan, x_ref, *refs):
    count = len(plan)
    tables = refs[: 3 * count]
    out_ref, buf_a, buf_b, parts, pack = refs[3 * count :]
    width = x_ref.shape[1]
    source = x_ref
    for step, (row_in, row_out, bands_out, depth) in enumerate(plan):
        pick_low, pick_high, delay = tables[3 * step : 3 * step + 3]
        target = out_ref if step == count - 1 else (buf_a, buf_b)[step % 2]
        group = 2 if bands_out >= 2 else 1
        lanes = group * width
        tile_rows = min(TILE, row_out)
        for first_band in range(0, bands_out, group):
            for member in range(group):
                band = first_band + member
                for side in range(2):
                    block = source[pl.ds((2 * band + side) * row_in, depth), :]
                    for piece, value in enumerate(split_pieces(block)):
                        parts[side, piece, pl.ds(0, depth), pl.ds(member * width, width)] = value

            def tile(index, carry, target=target, first_band=first_band, depth=depth,
                     row_out=row_out, group=group, lanes=lanes, tile_rows=tile_rows,
                     pick_low=pick_low, pick_high=pick_high, delay=delay):
                rows = pl.ds(pl.multiple_of(index * tile_rows, tile_rows), tile_rows)
                low_sel = pick_low[rows, :]
                high_sel = pick_high[rows, :]
                lower = None
                upper = None
                for piece in range(PIECES):
                    term = jnp.dot(low_sel, parts[0, piece, pl.ds(0, depth), pl.ds(0, lanes)],
                                   preferred_element_type=jnp.float32)
                    lower = term if lower is None else lower + term
                    term = jnp.dot(high_sel, parts[1, piece, pl.ds(0, depth), pl.ds(0, lanes)],
                                   preferred_element_type=jnp.float32)
                    upper = term if upper is None else upper + term
                amount = delay[rows, :]
                for bit in (1, 2, 4, 8):
                    upper = jnp.where((amount & bit) != 0, pltpu.roll(upper, bit, 1), upper)
                merged = lower + upper
                if target is out_ref:
                    pack[...] = merged
                    even = pack[pl.ds(0, tile_rows // 2, stride=2), :]
                    odd = pack[pl.ds(1, tile_rows // 2, stride=2), :]
                    lane = lax.broadcasted_iota(jnp.int32, even.shape, 1)
                    start = pl.multiple_of(index * (tile_rows // 2), tile_rows // 2)
                    target[pl.ds(start, tile_rows // 2), :] = jnp.where(
                        lane < SUB_HALO, pltpu.roll(even, SUB_HALO, 1), odd
                    )
                    return carry
                for member in range(group):
                    start = pl.multiple_of((first_band + member) * row_out + index * tile_rows, tile_rows)
                    target[pl.ds(start, tile_rows), :] = merged[:, member * width : (member + 1) * width]
                return carry

            lax.fori_loop(0, row_out // tile_rows, tile, 0)
        source = target


def run_matmul_levels(state, first_rows, second_rows, shifts, levels, plan):
    width = state.shape[1]
    tables = []
    for level, (row_in, row_out, bands_out, depth) in zip(levels, plan):
        columns = jnp.arange(depth, dtype=jnp.int32)[None, :]
        tables.append((first_rows[level, :row_out, None] == columns).astype(jnp.bfloat16))
        tables.append((second_rows[level, :row_out, None] == columns).astype(jnp.bfloat16))
        tables.append(shifts[level, :row_out, None])
    buf_rows = max(p[1] * p[2] for p in plan)
    depth_most = max(p[3] for p in plan)
    vmem = pl.BlockSpec(memory_space=pltpu.VMEM)
    return pl.pallas_call(
        functools.partial(matmul_kernel, plan),
        out_shape=jax.ShapeDtypeStruct((plan[-1][1] * plan[-1][2] // 2, width), jnp.float32),
        in_specs=[vmem] * (1 + len(tables)),
        out_specs=vmem,
        scratch_shapes=[
            pltpu.VMEM((buf_rows, width), jnp.float32),
            pltpu.VMEM((buf_rows, width), jnp.float32),
            pltpu.VMEM((2, PIECES, depth_most, 2 * width), jnp.bfloat16),
            pltpu.VMEM((min(TILE, plan[-1][1]), width), jnp.float32),
        ],
        compiler_params=pltpu.CompilerParams(vmem_limit_bytes=60 * 1024 * 1024),
    )(state, *tables)


def harmonic_kernel(power_ref, offset_ref, out_ref):
    fundamentals = out_ref.shape[1]
    total = None
    for order in range(HARM):
        stride = order + 1
        offset = offset_ref[order]
        for phase in range(stride):
            picked = power_ref[pl.ds(phase, fundamentals, stride=stride), :]
            term = jnp.where(offset == phase, picked, 0.0)
            total = term if total is None else total + term
    out_ref[...] = jnp.transpose(total * (1.0 / HARM))


def delayed(value, amount):
    rolled = pltpu.roll(value, amount, 2)
    previous = jnp.concatenate([rolled[-1:], rolled[:-1]], axis=0)
    lane = lax.broadcasted_iota(jnp.int32, value.shape, 2)
    return jnp.where(lane < amount, previous, rolled)


def local_kernel(plan, sub, base, table_ref, x_ref, out_ref, *bufs):
    count = len(plan)
    final = bufs[-1]
    source = x_ref
    for step, (row_in, row_out, bands_out) in enumerate(plan):
        target = final if step == count - 1 else bufs[step]

        def body(row, carry, source=source, target=target, step=step,
                 bands_out=bands_out, last=step == count - 1):
            lower = source[table_ref[0, step, row], :, pl.ds(0, bands_out, stride=2), :]
            upper = source[table_ref[1, step, row], :, pl.ds(1, bands_out, stride=2), :]
            merged = lower + delayed(upper, table_ref[2, step, row])
            if last:
                target[:, pl.ds(row, 1), :] = merged
            else:
                target[row] = merged
            return carry

        lax.fori_loop(0, row_out, body, 0, unroll=min(row_out, 16))
        source = target
    for dest in range(out_ref.shape[0]):
        start = base + sub * dest
        slab, offset = start // LANES, start % LANES
        if offset == 0:
            out_ref[dest] = final[slab]
        else:
            lane = lax.broadcasted_iota(jnp.int32, final.shape[1:], 1)
            head = pltpu.roll(final[slab], LANES - offset, 1)
            tail = pltpu.roll(final[slab + 1], LANES - offset, 1)
            out_ref[dest] = jnp.where(lane < LANES - offset, head, tail)


def run_local(state, tables, plan, parts, sub, base):
    slabs = state.shape[1]
    rows_last = plan[-1][1]
    smem = pl.BlockSpec(memory_space=pltpu.SMEM)
    vmem = pl.BlockSpec(memory_space=pltpu.VMEM)
    scratch = [pltpu.VMEM((p[1], slabs, p[2], LANES), jnp.float32) for p in plan[:-1]]
    scratch.append(pltpu.VMEM((slabs, rows_last, LANES), jnp.float32))
    return pl.pallas_call(
        functools.partial(local_kernel, plan, sub, base),
        out_shape=jax.ShapeDtypeStruct((parts, rows_last, sub + SUB_HALO), jnp.float32),
        in_specs=[smem, vmem],
        out_specs=vmem,
        scratch_shapes=scratch,
        compiler_params=pltpu.CompilerParams(vmem_limit_bytes=56 * 1024 * 1024),
    )(tables, state)


def spectra(series, harmonic_bins):
    count = series.shape[0]
    total = series.shape[1]
    outer = DFT_OUTER
    inner = total // outer
    half_inner = inner // 2
    highest = lax.Precision.HIGHEST
    grid = series.reshape(count, outer, inner)
    outer_index = jnp.arange(outer, dtype=jnp.int32)
    inner_index = jnp.arange(inner, dtype=jnp.int32)
    half_index = jnp.arange(half_inner, dtype=jnp.int32)
    angle_outer = (
        2.0
        * math.pi
        / outer
        * (outer_index[:, None] * outer_index[None, :] % outer).astype(jnp.float32)
    )
    outer_table = jnp.concatenate([jnp.cos(angle_outer), jnp.sin(angle_outer)], axis=1)
    section_one = jnp.einsum("npq,pk->nkq", grid, outer_table, precision=highest)
    section_re = section_one[:, :outer]
    section_im = -section_one[:, outer:]
    angle_twist = (
        2.0
        * math.pi
        / total
        * (outer_index[:, None] * inner_index[None, :] % total).astype(jnp.float32)
    )
    twist_cos = jnp.cos(angle_twist)
    twist_sin = jnp.sin(angle_twist)
    rotated = jnp.stack(
        [
            section_re * twist_cos + section_im * twist_sin,
            section_im * twist_cos - section_re * twist_sin,
        ]
    )
    angle_inner = (
        2.0
        * math.pi
        / inner
        * (inner_index[:, None] * half_index[None, :] % inner).astype(jnp.float32)
    )
    inner_table = jnp.concatenate([jnp.cos(angle_inner), jnp.sin(angle_inner)], axis=1)
    section_two = jnp.einsum("snkq,qm->snkm", rotated, inner_table, precision=highest)
    final_re = section_two[0, :, :, :half_inner] + section_two[1, :, :, half_inner:]
    final_im = section_two[1, :, :, :half_inner] - section_two[0, :, :, half_inner:]
    spectrum_power = (final_re * final_re + final_im * final_im) / (C * total)
    spectrum_power = jnp.transpose(spectrum_power, (0, 2, 1)).reshape(count, total // 2)
    fundamentals = harmonic_bins.shape[1]
    fundamental = jnp.arange(fundamentals, dtype=jnp.int32)
    stride = jnp.arange(1, HARM + 1, dtype=jnp.int32)[:, None]
    offsets = (harmonic_bins - stride * fundamental[None, :])[:, :, None]
    vmem = pl.BlockSpec(memory_space=pltpu.VMEM)
    harmonic = pl.pallas_call(
        harmonic_kernel,
        out_shape=jax.ShapeDtypeStruct((count, fundamentals), jnp.float32),
        in_specs=[vmem, vmem],
        out_specs=vmem,
    )(jnp.transpose(spectrum_power), offsets)
    return spectrum_power, harmonic


def on_device(filterbank, first_rows, second_rows, shifts, harmonic_bins):
    channels = filterbank.shape[0]
    samples = filterbank.shape[1]
    local_levels = channels.bit_length() - 1
    chan_count = lax.axis_size("chan")
    tm_count = lax.axis_size("tm")
    cross_levels = chan_count.bit_length() - 1
    levels = local_levels + cross_levels
    rim = lax.ppermute(
        filterbank[:, samples - RAW_HALO :],
        "tm",
        [(source, source + 1) for source in range(tm_count - 1)],
    )
    widened = jnp.concatenate([rim, filterbank], axis=1)
    local_plan = [
        (2**level, 2 ** (level + 1), channels >> (level + 1)) for level in range(local_levels)
    ]
    sub = samples // chan_count
    pieces = run_local(
        widened.astype(jnp.float32).reshape(channels, -1, LANES).transpose(1, 0, 2)[None],
        jnp.stack([first_rows, second_rows, shifts])[:, :local_levels, :channels],
        local_plan,
        chan_count,
        sub,
        RAW_HALO - SUB_HALO,
    )
    cross_tables = jnp.stack([first_rows, second_rows, shifts])[:, local_levels:]
    pieces, cross_tables = lax.optimization_barrier((pieces, cross_tables))
    window = sub + SUB_HALO
    layers = lax.all_to_all(pieces, "chan", split_axis=0, concat_axis=0, tiled=True)
    cross_plan = []
    bands = chan_count
    for level in range(local_levels, levels):
        bands //= 2
        rows_in = min(2**level, NDM)
        cross_plan.append((rows_in, min(2 ** (level + 1), NDM), bands, min(rows_in, NDM // 2)))
    plane = run_matmul_levels(
        layers.reshape(chan_count * channels, window),
        cross_tables[0],
        cross_tables[1],
        cross_tables[2],
        list(range(levels - local_levels)),
        cross_plan,
    )
    groups = chan_count * tm_count
    share = NDM // groups
    outgoing = plane.reshape(groups, share // 2, 2 * sub)
    incoming = lax.all_to_all(outgoing, ("chan", "tm"), split_axis=0, concat_axis=0, tiled=True)
    series = (
        incoming.reshape(chan_count, tm_count, share // 2, 2, sub)
        .transpose(2, 3, 1, 0, 4)
        .reshape(share, tm_count * samples)
    )
    return spectra(series, harmonic_bins)


def solution(mesh):
    in_specs = (P("chan", "tm"), P(), P(), P(), P())
    out_specs = (P(("chan", "tm"), None), P(("chan", "tm"), None))
    return jax.shard_map(
        on_device, mesh=mesh, in_specs=in_specs, out_specs=out_specs, check_vma=False
    )
```

```python
import functools
import math

import jax
import jax.numpy as jnp
from jax import lax
from jax.experimental import pallas as pl
from jax.experimental.pallas import tpu as pltpu
from jax.sharding import PartitionSpec as P

C = 4096
NDM = 2048
SHIFT = 16
DFT_OUTER = 64
HARM = 8
RAW_HALO = 256
SUB_HALO = 64
TILE = 1024
LANES = 128
PIECES = 2


def shift_right(value, amount):
    width = value.shape[-1]
    pad = [(0, 0)] * (value.ndim - 1) + [(amount, 0)]
    return jnp.pad(value, pad)[..., :width]


def merge_level(paired, rows_first, rows_second, delays):
    lower_bands = jnp.take(paired[0::2], rows_first, axis=1)
    upper_bands = jnp.take(paired[1::2], rows_second, axis=1)
    delay_col = delays[None, :, None]
    shifted = upper_bands
    for bit in (1, 2, 4, 8):
        shifted = jnp.where((delay_col & bit) != 0, shift_right(shifted, bit), shifted)
    return lower_bands + shifted


def level_merge(layers, first_rows, second_rows, shifts, level):
    count = min(2 ** (level + 1), NDM)
    return merge_level(
        layers, first_rows[level, :count], second_rows[level, :count], shifts[level, :count]
    )


def split_pieces(block):
    high = block.astype(jnp.bfloat16)
    low = (block - high.astype(jnp.float32)).astype(jnp.bfloat16)
    return high, low


def matmul_kernel(plan, x_ref, *refs):
    count = len(plan)
    tables = refs[: 3 * count]
    out_ref, buf_a, buf_b, parts, pack = refs[3 * count :]
    width = x_ref.shape[1]
    source = x_ref
    for step, (row_in, row_out, bands_out, depth) in enumerate(plan):
        pick_low, pick_high, delay = tables[3 * step : 3 * step + 3]
        target = out_ref if step == count - 1 else (buf_a, buf_b)[step % 2]
        group = 2 if bands_out >= 2 else 1
        lanes = group * width
        tile_rows = min(TILE, row_out)
        for first_band in range(0, bands_out, group):
            for member in range(group):
                band = first_band + member
                for side in range(2):
                    block = source[pl.ds((2 * band + side) * row_in, depth), :]
                    for piece, value in enumerate(split_pieces(block)):
                        parts[side, piece, pl.ds(0, depth), pl.ds(member * width, width)] = value

            def tile(index, carry, target=target, first_band=first_band, depth=depth,
                     row_out=row_out, group=group, lanes=lanes, tile_rows=tile_rows,
                     pick_low=pick_low, pick_high=pick_high, delay=delay):
                rows = pl.ds(pl.multiple_of(index * tile_rows, tile_rows), tile_rows)
                low_sel = pick_low[rows, :]
                high_sel = pick_high[rows, :]
                lower = None
                upper = None
                for piece in range(PIECES):
                    term = jnp.dot(low_sel, parts[0, piece, pl.ds(0, depth), pl.ds(0, lanes)],
                                   preferred_element_type=jnp.float32)
                    lower = term if lower is None else lower + term
                    term = jnp.dot(high_sel, parts[1, piece, pl.ds(0, depth), pl.ds(0, lanes)],
                                   preferred_element_type=jnp.float32)
                    upper = term if upper is None else upper + term
                amount = delay[rows, :]
                for bit in (1, 2, 4, 8):
                    upper = jnp.where((amount & bit) != 0, pltpu.roll(upper, bit, 1), upper)
                merged = lower + upper
                if target is out_ref:
                    pack[...] = merged
                    even = pack[pl.ds(0, tile_rows // 2, stride=2), :]
                    odd = pack[pl.ds(1, tile_rows // 2, stride=2), :]
                    lane = lax.broadcasted_iota(jnp.int32, even.shape, 1)
                    start = pl.multiple_of(index * (tile_rows // 2), tile_rows // 2)
                    target[pl.ds(start, tile_rows // 2), :] = jnp.where(
                        lane < SUB_HALO, pltpu.roll(even, SUB_HALO, 1), odd
                    )
                    return carry
                for member in range(group):
                    start = pl.multiple_of((first_band + member) * row_out + index * tile_rows, tile_rows)
                    target[pl.ds(start, tile_rows), :] = merged[:, member * width : (member + 1) * width]
                return carry

            lax.fori_loop(0, row_out // tile_rows, tile, 0)
        source = target


def run_matmul_levels(state, first_rows, second_rows, shifts, levels, plan):
    width = state.shape[1]
    tables = []
    for level, (row_in, row_out, bands_out, depth) in zip(levels, plan):
        columns = jnp.arange(depth, dtype=jnp.int32)[None, :]
        tables.append((first_rows[level, :row_out, None] == columns).astype(jnp.bfloat16))
        tables.append((second_rows[level, :row_out, None] == columns).astype(jnp.bfloat16))
        tables.append(shifts[level, :row_out, None])
    buf_rows = max(p[1] * p[2] for p in plan)
    depth_most = max(p[3] for p in plan)
    vmem = pl.BlockSpec(memory_space=pltpu.VMEM)
    return pl.pallas_call(
        functools.partial(matmul_kernel, plan),
        out_shape=jax.ShapeDtypeStruct((plan[-1][1] * plan[-1][2] // 2, width), jnp.float32),
        in_specs=[vmem] * (1 + len(tables)),
        out_specs=vmem,
        scratch_shapes=[
            pltpu.VMEM((buf_rows, width), jnp.float32),
            pltpu.VMEM((buf_rows, width), jnp.float32),
            pltpu.VMEM((2, PIECES, depth_most, 2 * width), jnp.bfloat16),
            pltpu.VMEM((min(TILE, plan[-1][1]), width), jnp.float32),
        ],
        compiler_params=pltpu.CompilerParams(vmem_limit_bytes=60 * 1024 * 1024),
    )(state, *tables)


def harmonic_kernel(spectrum_ref, offset_ref, out_ref, power_ref):
    fundamentals = out_ref.shape[1]
    power_ref[...] = jnp.transpose(spectrum_ref[...])
    total = None
    for order in range(HARM):
        stride = order + 1
        offset = offset_ref[order]
        for phase in range(stride):
            picked = power_ref[pl.ds(phase, fundamentals, stride=stride), :]
            term = jnp.where(offset == phase, picked, 0.0)
            total = term if total is None else total + term
    out_ref[...] = jnp.transpose(total * (1.0 / HARM))


def delayed(value, amount):
    rolled = pltpu.roll(value, amount, 2)
    previous = jnp.concatenate([rolled[-1:], rolled[:-1]], axis=0)
    lane = lax.broadcasted_iota(jnp.int32, value.shape, 2)
    return jnp.where(lane < amount, previous, rolled)


def local_kernel(plan, sub, base, table_ref, x_ref, out_ref, *bufs):
    count = len(plan)
    final = bufs[-1]
    source = x_ref
    for step, (row_in, row_out, bands_out) in enumerate(plan):
        target = final if step == count - 1 else bufs[step]

        def body(row, carry, source=source, target=target, step=step,
                 bands_out=bands_out, last=step == count - 1):
            lower = source[table_ref[0, step, row], :, pl.ds(0, bands_out, stride=2), :]
            upper = source[table_ref[1, step, row], :, pl.ds(1, bands_out, stride=2), :]
            merged = lower + delayed(upper, table_ref[2, step, row])
            if last:
                target[:, pl.ds(row, 1), :] = merged
            else:
                target[row] = merged
            return carry

        lax.fori_loop(0, row_out, body, 0, unroll=min(row_out, 16))
        source = target
    for dest in range(out_ref.shape[0]):
        start = base + sub * dest
        slab, offset = start // LANES, start % LANES
        if offset == 0:
            out_ref[dest] = final[slab]
        else:
            lane = lax.broadcasted_iota(jnp.int32, final.shape[1:], 1)
            head = pltpu.roll(final[slab], LANES - offset, 1)
            tail = pltpu.roll(final[slab + 1], LANES - offset, 1)
            out_ref[dest] = jnp.where(lane < LANES - offset, head, tail)


def run_local(state, tables, plan, parts, sub, base):
    slabs = state.shape[1]
    rows_last = plan[-1][1]
    smem = pl.BlockSpec(memory_space=pltpu.SMEM)
    vmem = pl.BlockSpec(memory_space=pltpu.VMEM)
    scratch = [pltpu.VMEM((p[1], slabs, p[2], LANES), jnp.float32) for p in plan[:-1]]
    scratch.append(pltpu.VMEM((slabs, rows_last, LANES), jnp.float32))
    return pl.pallas_call(
        functools.partial(local_kernel, plan, sub, base),
        out_shape=jax.ShapeDtypeStruct((parts, rows_last, sub + SUB_HALO), jnp.float32),
        in_specs=[smem, vmem],
        out_specs=vmem,
        scratch_shapes=scratch,
        compiler_params=pltpu.CompilerParams(vmem_limit_bytes=56 * 1024 * 1024),
    )(tables, state)


def spectra(series, harmonic_bins):
    count = series.shape[0]
    total = series.shape[1]
    outer = DFT_OUTER
    inner = total // outer
    half_inner = inner // 2
    highest = lax.Precision.HIGHEST
    grid = series.reshape(count, outer, inner)
    outer_index = jnp.arange(outer, dtype=jnp.int32)
    inner_index = jnp.arange(inner, dtype=jnp.int32)
    half_index = jnp.arange(half_inner, dtype=jnp.int32)
    angle_outer = (
        2.0
        * math.pi
        / outer
        * (outer_index[:, None] * outer_index[None, :] % outer).astype(jnp.float32)
    )
    outer_table = jnp.concatenate([jnp.cos(angle_outer), jnp.sin(angle_outer)], axis=1)
    section_one = jnp.einsum("npq,pk->nkq", grid, outer_table, precision=highest)
    section_re = section_one[:, :outer]
    section_im = -section_one[:, outer:]
    angle_twist = (
        2.0
        * math.pi
        / total
        * (outer_index[:, None] * inner_index[None, :] % total).astype(jnp.float32)
    )
    twist_cos = jnp.cos(angle_twist)
    twist_sin = jnp.sin(angle_twist)
    rotated = jnp.stack(
        [
            section_re * twist_cos + section_im * twist_sin,
            section_im * twist_cos - section_re * twist_sin,
        ]
    )
    angle_inner = (
        2.0
        * math.pi
        / inner
        * (inner_index[:, None] * half_index[None, :] % inner).astype(jnp.float32)
    )
    inner_table = jnp.concatenate([jnp.cos(angle_inner), jnp.sin(angle_inner)], axis=1)
    section_two = jnp.einsum("snkq,qm->snkm", rotated, inner_table, precision=highest)
    final_re = section_two[0, :, :, :half_inner] + section_two[1, :, :, half_inner:]
    final_im = section_two[1, :, :, :half_inner] - section_two[0, :, :, half_inner:]
    spectrum_power = (final_re * final_re + final_im * final_im) / (C * total)
    spectrum_power = jnp.transpose(spectrum_power, (0, 2, 1)).reshape(count, total // 2)
    fundamentals = harmonic_bins.shape[1]
    fundamental = jnp.arange(fundamentals, dtype=jnp.int32)
    stride = jnp.arange(1, HARM + 1, dtype=jnp.int32)[:, None]
    offsets = (harmonic_bins - stride * fundamental[None, :])[:, :, None]
    vmem = pl.BlockSpec(memory_space=pltpu.VMEM)
    harmonic = pl.pallas_call(
        harmonic_kernel,
        out_shape=jax.ShapeDtypeStruct((count, fundamentals), jnp.float32),
        in_specs=[vmem, vmem],
        out_specs=vmem,
        scratch_shapes=[pltpu.VMEM((total // 2, count), jnp.float32)],
    )(spectrum_power, offsets)
    return spectrum_power, harmonic


def on_device(filterbank, first_rows, second_rows, shifts, harmonic_bins):
    channels = filterbank.shape[0]
    samples = filterbank.shape[1]
    local_levels = channels.bit_length() - 1
    chan_count = lax.axis_size("chan")
    tm_count = lax.axis_size("tm")
    cross_levels = chan_count.bit_length() - 1
    levels = local_levels + cross_levels
    rim = lax.ppermute(
        filterbank[:, samples - RAW_HALO :],
        "tm",
        [(source, source + 1) for source in range(tm_count - 1)],
    )
    widened = jnp.concatenate([rim, filterbank], axis=1)
    local_plan = [
        (2**level, 2 ** (level + 1), channels >> (level + 1)) for level in range(local_levels)
    ]
    sub = samples // chan_count
    pieces = run_local(
        widened.astype(jnp.float32).reshape(channels, -1, LANES).transpose(1, 0, 2)[None],
        jnp.stack([first_rows, second_rows, shifts])[:, :local_levels, :channels],
        local_plan,
        chan_count,
        sub,
        RAW_HALO - SUB_HALO,
    )
    cross_tables = jnp.stack([first_rows, second_rows, shifts])[:, local_levels:]
    pieces, cross_tables = lax.optimization_barrier((pieces, cross_tables))
    window = sub + SUB_HALO
    layers = lax.all_to_all(pieces, "chan", split_axis=0, concat_axis=0, tiled=True)
    cross_plan = []
    bands = chan_count
    for level in range(local_levels, levels):
        bands //= 2
        rows_in = min(2**level, NDM)
        cross_plan.append((rows_in, min(2 ** (level + 1), NDM), bands, min(rows_in, NDM // 2)))
    plane = run_matmul_levels(
        layers.reshape(chan_count * channels, window),
        cross_tables[0],
        cross_tables[1],
        cross_tables[2],
        list(range(levels - local_levels)),
        cross_plan,
    )
    groups = chan_count * tm_count
    share = NDM // groups
    outgoing = plane.reshape(groups, share // 2, 2 * sub)
    incoming = lax.all_to_all(outgoing, ("chan", "tm"), split_axis=0, concat_axis=0, tiled=True)
    series = (
        incoming.reshape(chan_count, tm_count, share // 2, 2, sub)
        .transpose(2, 3, 1, 0, 4)
        .reshape(share, tm_count * samples)
    )
    return spectra(series, harmonic_bins)


def solution(mesh):
    in_specs = (P("chan", "tm"), P(), P(), P(), P())
    out_specs = (P(("chan", "tm"), None), P(("chan", "tm"), None))
    return jax.shard_map(
        on_device, mesh=mesh, in_specs=in_specs, out_specs=out_specs, check_vma=False
    )
```

```python
import functools
import math

import jax
import jax.numpy as jnp
from jax import lax
from jax.experimental import pallas as pl
from jax.experimental.pallas import tpu as pltpu
from jax.sharding import PartitionSpec as P

C = 4096
NDM = 2048
SHIFT = 16
DFT_OUTER = 64
HARM = 8
RAW_HALO = 256
SUB_HALO = 64
TILE = 1024
LANES = 128
PIECES = 2


def shift_right(value, amount):
    width = value.shape[-1]
    pad = [(0, 0)] * (value.ndim - 1) + [(amount, 0)]
    return jnp.pad(value, pad)[..., :width]


def merge_level(paired, rows_first, rows_second, delays):
    lower_bands = jnp.take(paired[0::2], rows_first, axis=1)
    upper_bands = jnp.take(paired[1::2], rows_second, axis=1)
    delay_col = delays[None, :, None]
    shifted = upper_bands
    for bit in (1, 2, 4, 8):
        shifted = jnp.where((delay_col & bit) != 0, shift_right(shifted, bit), shifted)
    return lower_bands + shifted


def level_merge(layers, first_rows, second_rows, shifts, level):
    count = min(2 ** (level + 1), NDM)
    return merge_level(
        layers, first_rows[level, :count], second_rows[level, :count], shifts[level, :count]
    )


def split_pieces(block):
    high = block.astype(jnp.bfloat16)
    low = (block - high.astype(jnp.float32)).astype(jnp.bfloat16)
    return high, low


def matmul_kernel(plan, x_ref, *refs):
    count = len(plan)
    tables = refs[: 3 * count]
    out_ref, buf_a, buf_b, parts, pack = refs[3 * count :]
    width = x_ref.shape[1]
    source = x_ref
    for step, (row_in, row_out, bands_out, depth) in enumerate(plan):
        pick_low, pick_high, delay = tables[3 * step : 3 * step + 3]
        target = out_ref if step == count - 1 else (buf_a, buf_b)[step % 2]
        group = 2 if bands_out >= 2 else 1
        lanes = group * width
        tile_rows = min(TILE, row_out)
        for first_band in range(0, bands_out, group):
            for member in range(group):
                band = first_band + member
                for side in range(2):
                    block = source[pl.ds((2 * band + side) * row_in, depth), :]
                    for piece, value in enumerate(split_pieces(block)):
                        parts[side, piece, pl.ds(0, depth), pl.ds(member * width, width)] = value

            def tile(index, carry, target=target, first_band=first_band, depth=depth,
                     row_out=row_out, group=group, lanes=lanes, tile_rows=tile_rows,
                     pick_low=pick_low, pick_high=pick_high, delay=delay):
                rows = pl.ds(pl.multiple_of(index * tile_rows, tile_rows), tile_rows)
                low_sel = pick_low[rows, :]
                high_sel = pick_high[rows, :]
                lower = None
                upper = None
                for piece in range(PIECES):
                    term = jnp.dot(low_sel, parts[0, piece, pl.ds(0, depth), pl.ds(0, lanes)],
                                   preferred_element_type=jnp.float32)
                    lower = term if lower is None else lower + term
                    term = jnp.dot(high_sel, parts[1, piece, pl.ds(0, depth), pl.ds(0, lanes)],
                                   preferred_element_type=jnp.float32)
                    upper = term if upper is None else upper + term
                amount = delay[rows, :]
                for bit in (1, 2, 4, 8):
                    upper = jnp.where((amount & bit) != 0, pltpu.roll(upper, bit, 1), upper)
                merged = lower + upper
                if target is out_ref:
                    pack[...] = merged
                    even = pack[pl.ds(0, tile_rows // 2, stride=2), :]
                    odd = pack[pl.ds(1, tile_rows // 2, stride=2), :]
                    lane = lax.broadcasted_iota(jnp.int32, even.shape, 1)
                    start = pl.multiple_of(index * (tile_rows // 2), tile_rows // 2)
                    target[pl.ds(start, tile_rows // 2), :] = jnp.where(
                        lane < SUB_HALO, pltpu.roll(even, SUB_HALO, 1), odd
                    )
                    return carry
                for member in range(group):
                    start = pl.multiple_of((first_band + member) * row_out + index * tile_rows, tile_rows)
                    target[pl.ds(start, tile_rows), :] = merged[:, member * width : (member + 1) * width]
                return carry

            lax.fori_loop(0, row_out // tile_rows, tile, 0)
        source = target


def run_matmul_levels(state, first_rows, second_rows, shifts, levels, plan):
    width = state.shape[1]
    tables = []
    for level, (row_in, row_out, bands_out, depth) in zip(levels, plan):
        columns = jnp.arange(depth, dtype=jnp.int32)[None, :]
        tables.append((first_rows[level, :row_out, None] == columns).astype(jnp.bfloat16))
        tables.append((second_rows[level, :row_out, None] == columns).astype(jnp.bfloat16))
        tables.append(shifts[level, :row_out, None])
    buf_rows = max(p[1] * p[2] for p in plan)
    depth_most = max(p[3] for p in plan)
    vmem = pl.BlockSpec(memory_space=pltpu.VMEM)
    return pl.pallas_call(
        functools.partial(matmul_kernel, plan),
        out_shape=jax.ShapeDtypeStruct((plan[-1][1] * plan[-1][2] // 2, width), jnp.float32),
        in_specs=[vmem] * (1 + len(tables)),
        out_specs=vmem,
        scratch_shapes=[
            pltpu.VMEM((buf_rows, width), jnp.float32),
            pltpu.VMEM((buf_rows, width), jnp.float32),
            pltpu.VMEM((2, PIECES, depth_most, 2 * width), jnp.bfloat16),
            pltpu.VMEM((min(TILE, plan[-1][1]), width), jnp.float32),
        ],
        compiler_params=pltpu.CompilerParams(vmem_limit_bytes=60 * 1024 * 1024),
    )(state, *tables)


def harmonic_kernel(spectrum_ref, offset_ref, out_ref, power_ref):
    fundamentals = out_ref.shape[1]
    power_ref[...] = jnp.transpose(spectrum_ref[...])
    total = None
    for order in range(HARM):
        stride = order + 1
        offset = jnp.broadcast_to(offset_ref[order], (fundamentals, power_ref.shape[1]))
        term = power_ref[pl.ds(0, fundamentals, stride=stride), :]
        for phase in range(1, stride):
            picked = power_ref[pl.ds(phase, fundamentals, stride=stride), :]
            term = jnp.where(offset == phase, picked, term)
        total = term if total is None else total + term
    out_ref[...] = jnp.transpose(total * (1.0 / HARM))


def delayed(value, amount):
    rolled = pltpu.roll(value, amount, 2)
    previous = jnp.concatenate([rolled[-1:], rolled[:-1]], axis=0)
    lane = lax.broadcasted_iota(jnp.int32, value.shape, 2)
    return jnp.where(lane < amount, previous, rolled)


def local_kernel(plan, sub, base, table_ref, x_ref, out_ref, *bufs):
    count = len(plan)
    final = bufs[-1]
    source = x_ref
    for step, (row_in, row_out, bands_out) in enumerate(plan):
        target = final if step == count - 1 else bufs[step]

        def body(row, carry, source=source, target=target, step=step,
                 bands_out=bands_out, last=step == count - 1):
            lower = source[table_ref[0, step, row], :, pl.ds(0, bands_out, stride=2), :]
            upper = source[table_ref[1, step, row], :, pl.ds(1, bands_out, stride=2), :]
            merged = lower + delayed(upper, table_ref[2, step, row])
            if last:
                target[:, pl.ds(row, 1), :] = merged
            else:
                target[row] = merged
            return carry

        lax.fori_loop(0, row_out, body, 0, unroll=min(row_out, 16))
        source = target
    for dest in range(out_ref.shape[0]):
        start = base + sub * dest
        slab, offset = start // LANES, start % LANES
        if offset == 0:
            out_ref[dest] = final[slab]
        else:
            lane = lax.broadcasted_iota(jnp.int32, final.shape[1:], 1)
            head = pltpu.roll(final[slab], LANES - offset, 1)
            tail = pltpu.roll(final[slab + 1], LANES - offset, 1)
            out_ref[dest] = jnp.where(lane < LANES - offset, head, tail)


def run_local(state, tables, plan, parts, sub, base):
    slabs = state.shape[1]
    rows_last = plan[-1][1]
    smem = pl.BlockSpec(memory_space=pltpu.SMEM)
    vmem = pl.BlockSpec(memory_space=pltpu.VMEM)
    scratch = [pltpu.VMEM((p[1], slabs, p[2], LANES), jnp.float32) for p in plan[:-1]]
    scratch.append(pltpu.VMEM((slabs, rows_last, LANES), jnp.float32))
    return pl.pallas_call(
        functools.partial(local_kernel, plan, sub, base),
        out_shape=jax.ShapeDtypeStruct((parts, rows_last, sub + SUB_HALO), jnp.float32),
        in_specs=[smem, vmem],
        out_specs=vmem,
        scratch_shapes=scratch,
        compiler_params=pltpu.CompilerParams(vmem_limit_bytes=56 * 1024 * 1024),
    )(tables, state)


def spectra(series, harmonic_bins):
    count = series.shape[0]
    total = series.shape[1]
    outer = DFT_OUTER
    inner = total // outer
    half_inner = inner // 2
    highest = lax.Precision.HIGHEST
    grid = series.reshape(count, outer, inner)
    outer_index = jnp.arange(outer, dtype=jnp.int32)
    inner_index = jnp.arange(inner, dtype=jnp.int32)
    half_index = jnp.arange(half_inner, dtype=jnp.int32)
    angle_outer = (
        2.0
        * math.pi
        / outer
        * (outer_index[:, None] * outer_index[None, :] % outer).astype(jnp.float32)
    )
    outer_table = jnp.concatenate([jnp.cos(angle_outer), jnp.sin(angle_outer)], axis=1)
    section_one = jnp.einsum("npq,pk->nkq", grid, outer_table, precision=highest)
    section_re = section_one[:, :outer]
    section_im = -section_one[:, outer:]
    angle_twist = (
        2.0
        * math.pi
        / total
        * (outer_index[:, None] * inner_index[None, :] % total).astype(jnp.float32)
    )
    twist_cos = jnp.cos(angle_twist)
    twist_sin = jnp.sin(angle_twist)
    rotated = jnp.stack(
        [
            section_re * twist_cos + section_im * twist_sin,
            section_im * twist_cos - section_re * twist_sin,
        ]
    )
    angle_inner = (
        2.0
        * math.pi
        / inner
        * (inner_index[:, None] * half_index[None, :] % inner).astype(jnp.float32)
    )
    inner_table = jnp.concatenate([jnp.cos(angle_inner), jnp.sin(angle_inner)], axis=1)
    section_two = jnp.einsum("snkq,qm->snkm", rotated, inner_table, precision=highest)
    final_re = section_two[0, :, :, :half_inner] + section_two[1, :, :, half_inner:]
    final_im = section_two[1, :, :, :half_inner] - section_two[0, :, :, half_inner:]
    spectrum_power = (final_re * final_re + final_im * final_im) / (C * total)
    spectrum_power = jnp.transpose(spectrum_power, (0, 2, 1)).reshape(count, total // 2)
    fundamentals = harmonic_bins.shape[1]
    fundamental = jnp.arange(fundamentals, dtype=jnp.int32)
    stride = jnp.arange(1, HARM + 1, dtype=jnp.int32)[:, None]
    offsets = (harmonic_bins - stride * fundamental[None, :])[:, :, None]
    vmem = pl.BlockSpec(memory_space=pltpu.VMEM)
    harmonic = pl.pallas_call(
        harmonic_kernel,
        out_shape=jax.ShapeDtypeStruct((count, fundamentals), jnp.float32),
        in_specs=[vmem, vmem],
        out_specs=vmem,
        scratch_shapes=[pltpu.VMEM((total // 2, count), jnp.float32)],
    )(spectrum_power, offsets)
    return spectrum_power, harmonic


def on_device(filterbank, first_rows, second_rows, shifts, harmonic_bins):
    channels = filterbank.shape[0]
    samples = filterbank.shape[1]
    local_levels = channels.bit_length() - 1
    chan_count = lax.axis_size("chan")
    tm_count = lax.axis_size("tm")
    cross_levels = chan_count.bit_length() - 1
    levels = local_levels + cross_levels
    rim = lax.ppermute(
        filterbank[:, samples - RAW_HALO :],
        "tm",
        [(source, source + 1) for source in range(tm_count - 1)],
    )
    widened = jnp.concatenate([rim, filterbank], axis=1)
    local_plan = [
        (2**level, 2 ** (level + 1), channels >> (level + 1)) for level in range(local_levels)
    ]
    sub = samples // chan_count
    pieces = run_local(
        widened.astype(jnp.float32).reshape(channels, -1, LANES).transpose(1, 0, 2)[None],
        jnp.stack([first_rows, second_rows, shifts])[:, :local_levels, :channels],
        local_plan,
        chan_count,
        sub,
        RAW_HALO - SUB_HALO,
    )
    cross_tables = jnp.stack([first_rows, second_rows, shifts])[:, local_levels:]
    pieces, cross_tables = lax.optimization_barrier((pieces, cross_tables))
    window = sub + SUB_HALO
    layers = lax.all_to_all(pieces, "chan", split_axis=0, concat_axis=0, tiled=True)
    cross_plan = []
    bands = chan_count
    for level in range(local_levels, levels):
        bands //= 2
        rows_in = min(2**level, NDM)
        cross_plan.append((rows_in, min(2 ** (level + 1), NDM), bands, min(rows_in, NDM // 2)))
    plane = run_matmul_levels(
        layers.reshape(chan_count * channels, window),
        cross_tables[0],
        cross_tables[1],
        cross_tables[2],
        list(range(levels - local_levels)),
        cross_plan,
    )
    groups = chan_count * tm_count
    share = NDM // groups
    outgoing = plane.reshape(groups, share // 2, 2 * sub)
    incoming = lax.all_to_all(outgoing, ("chan", "tm"), split_axis=0, concat_axis=0, tiled=True)
    series = (
        incoming.reshape(chan_count, tm_count, share // 2, 2, sub)
        .transpose(2, 3, 1, 0, 4)
        .reshape(share, tm_count * samples)
    )
    return spectra(series, harmonic_bins)


def solution(mesh):
    in_specs = (P("chan", "tm"), P(), P(), P(), P())
    out_specs = (P(("chan", "tm"), None), P(("chan", "tm"), None))
    return jax.shard_map(
        on_device, mesh=mesh, in_specs=in_specs, out_specs=out_specs, check_vma=False
    )
```

```python
import functools
import math

import jax
import jax.numpy as jnp
from jax import lax
from jax.experimental import pallas as pl
from jax.experimental.pallas import tpu as pltpu
from jax.sharding import PartitionSpec as P

C = 4096
NDM = 2048
SHIFT = 16
DFT_OUTER = 64
HARM = 8
RAW_HALO = 256
SUB_HALO = 64
TILE = 1024
LANES = 128
PIECES = 2


def shift_right(value, amount):
    width = value.shape[-1]
    pad = [(0, 0)] * (value.ndim - 1) + [(amount, 0)]
    return jnp.pad(value, pad)[..., :width]


def merge_level(paired, rows_first, rows_second, delays):
    lower_bands = jnp.take(paired[0::2], rows_first, axis=1)
    upper_bands = jnp.take(paired[1::2], rows_second, axis=1)
    delay_col = delays[None, :, None]
    shifted = upper_bands
    for bit in (1, 2, 4, 8):
        shifted = jnp.where((delay_col & bit) != 0, shift_right(shifted, bit), shifted)
    return lower_bands + shifted


def level_merge(layers, first_rows, second_rows, shifts, level):
    count = min(2 ** (level + 1), NDM)
    return merge_level(
        layers, first_rows[level, :count], second_rows[level, :count], shifts[level, :count]
    )


def split_pieces(block):
    high = block.astype(jnp.bfloat16)
    low = (block - high.astype(jnp.float32)).astype(jnp.bfloat16)
    return high, low


def matmul_kernel(plan, x_ref, *refs):
    count = len(plan)
    tables = refs[: 3 * count]
    out_ref, buf_a, buf_b, parts, pack = refs[3 * count :]
    width = x_ref.shape[1]
    source = x_ref
    for step, (row_in, row_out, bands_out, depth) in enumerate(plan):
        pick_low, pick_high, delay = tables[3 * step : 3 * step + 3]
        target = out_ref if step == count - 1 else (buf_a, buf_b)[step % 2]
        group = 2 if bands_out >= 2 else 1
        lanes = group * width
        tile_rows = min(TILE, row_out)
        for first_band in range(0, bands_out, group):
            for member in range(group):
                band = first_band + member
                for side in range(2):
                    block = source[pl.ds((2 * band + side) * row_in, depth), :]
                    for piece, value in enumerate(split_pieces(block)):
                        parts[side, piece, pl.ds(0, depth), pl.ds(member * width, width)] = value

            def tile(index, carry, target=target, first_band=first_band, depth=depth,
                     row_out=row_out, group=group, lanes=lanes, tile_rows=tile_rows,
                     pick_low=pick_low, pick_high=pick_high, delay=delay):
                rows = pl.ds(pl.multiple_of(index * tile_rows, tile_rows), tile_rows)
                low_sel = pick_low[rows, :]
                high_sel = pick_high[rows, :]
                lower = None
                upper = None
                for piece in range(PIECES):
                    term = jnp.dot(low_sel, parts[0, piece, pl.ds(0, depth), pl.ds(0, lanes)],
                                   preferred_element_type=jnp.float32)
                    lower = term if lower is None else lower + term
                    term = jnp.dot(high_sel, parts[1, piece, pl.ds(0, depth), pl.ds(0, lanes)],
                                   preferred_element_type=jnp.float32)
                    upper = term if upper is None else upper + term
                amount = delay[rows, :]
                for bit in (1, 2, 4, 8):
                    upper = jnp.where((amount & bit) != 0, pltpu.roll(upper, bit, 1), upper)
                merged = lower + upper
                if target is out_ref:
                    pack[...] = merged
                    even = pack[pl.ds(0, tile_rows // 2, stride=2), :]
                    odd = pack[pl.ds(1, tile_rows // 2, stride=2), :]
                    lane = lax.broadcasted_iota(jnp.int32, even.shape, 1)
                    start = pl.multiple_of(index * (tile_rows // 2), tile_rows // 2)
                    target[pl.ds(start, tile_rows // 2), :] = jnp.where(
                        lane < SUB_HALO, pltpu.roll(even, SUB_HALO, 1), odd
                    )
                    return carry
                for member in range(group):
                    start = pl.multiple_of((first_band + member) * row_out + index * tile_rows, tile_rows)
                    target[pl.ds(start, tile_rows), :] = merged[:, member * width : (member + 1) * width]
                return carry

            lax.fori_loop(0, row_out // tile_rows, tile, 0)
        source = target


def run_matmul_levels(state, first_rows, second_rows, shifts, levels, plan):
    width = state.shape[1]
    tables = []
    for level, (row_in, row_out, bands_out, depth) in zip(levels, plan):
        columns = jnp.arange(depth, dtype=jnp.int32)[None, :]
        tables.append((first_rows[level, :row_out, None] == columns).astype(jnp.bfloat16))
        tables.append((second_rows[level, :row_out, None] == columns).astype(jnp.bfloat16))
        tables.append(shifts[level, :row_out, None])
    buf_rows = max(p[1] * p[2] for p in plan)
    depth_most = max(p[3] for p in plan)
    vmem = pl.BlockSpec(memory_space=pltpu.VMEM)
    return pl.pallas_call(
        functools.partial(matmul_kernel, plan),
        out_shape=jax.ShapeDtypeStruct((plan[-1][1] * plan[-1][2] // 2, width), jnp.float32),
        in_specs=[vmem] * (1 + len(tables)),
        out_specs=vmem,
        scratch_shapes=[
            pltpu.VMEM((buf_rows, width), jnp.float32),
            pltpu.VMEM((buf_rows, width), jnp.float32),
            pltpu.VMEM((2, PIECES, depth_most, 2 * width), jnp.bfloat16),
            pltpu.VMEM((min(TILE, plan[-1][1]), width), jnp.float32),
        ],
        compiler_params=pltpu.CompilerParams(vmem_limit_bytes=60 * 1024 * 1024),
    )(state, *tables)


def harmonic_kernel(spectrum_ref, offset_ref, out_ref, power_ref):
    fundamentals = out_ref.shape[1]
    power_ref[...] = jnp.transpose(spectrum_ref[...])
    total = None
    for order in range(HARM):
        stride = order + 1
        offset = jnp.broadcast_to(offset_ref[order], (fundamentals, power_ref.shape[1]))
        term = power_ref[pl.ds(0, fundamentals, stride=stride), :]
        for phase in range(1, stride):
            picked = power_ref[pl.ds(phase, fundamentals, stride=stride), :]
            term = jnp.where(offset == phase, picked, term)
        total = term if total is None else total + term
    out_ref[...] = jnp.transpose(total * (1.0 / HARM))


def delayed(value, amount):
    rolled = pltpu.roll(value, amount, 2)
    previous = jnp.concatenate([rolled[-1:], rolled[:-1]], axis=0)
    lane = lax.broadcasted_iota(jnp.int32, value.shape, 2)
    return jnp.where(lane < amount, previous, rolled)


def local_kernel(plan, sub, base, table_ref, x_ref, out_ref, *bufs):
    count = len(plan)
    final = bufs[-1]
    source = x_ref
    for step, (row_in, row_out, bands_out) in enumerate(plan):
        target = final if step == count - 1 else bufs[step]

        def body(row, carry, source=source, target=target, step=step,
                 bands_out=bands_out, last=step == count - 1):
            lower = source[table_ref[0, step, row], :, pl.ds(0, bands_out, stride=2), :]
            upper = source[table_ref[1, step, row], :, pl.ds(1, bands_out, stride=2), :]
            merged = lower + delayed(upper, table_ref[2, step, row])
            if last:
                target[:, pl.ds(row, 1), :] = merged
            else:
                target[row] = merged
            return carry

        lax.fori_loop(0, row_out, body, 0, unroll=min(row_out, 32 if bands_out <= 2 else 16))
        source = target
    for dest in range(out_ref.shape[0]):
        start = base + sub * dest
        slab, offset = start // LANES, start % LANES
        if offset == 0:
            out_ref[dest] = final[slab]
        else:
            lane = lax.broadcasted_iota(jnp.int32, final.shape[1:], 1)
            head = pltpu.roll(final[slab], LANES - offset, 1)
            tail = pltpu.roll(final[slab + 1], LANES - offset, 1)
            out_ref[dest] = jnp.where(lane < LANES - offset, head, tail)


def run_local(state, tables, plan, parts, sub, base):
    slabs = state.shape[1]
    rows_last = plan[-1][1]
    smem = pl.BlockSpec(memory_space=pltpu.SMEM)
    vmem = pl.BlockSpec(memory_space=pltpu.VMEM)
    scratch = [pltpu.VMEM((p[1], slabs, p[2], LANES), jnp.float32) for p in plan[:-1]]
    scratch.append(pltpu.VMEM((slabs, rows_last, LANES), jnp.float32))
    return pl.pallas_call(
        functools.partial(local_kernel, plan, sub, base),
        out_shape=jax.ShapeDtypeStruct((parts, rows_last, sub + SUB_HALO), jnp.float32),
        in_specs=[smem, vmem],
        out_specs=vmem,
        scratch_shapes=scratch,
        compiler_params=pltpu.CompilerParams(vmem_limit_bytes=56 * 1024 * 1024),
    )(tables, state)


def spectra(series, harmonic_bins):
    count = series.shape[0]
    total = series.shape[1]
    outer = DFT_OUTER
    inner = total // outer
    half_inner = inner // 2
    highest = lax.Precision.HIGHEST
    grid = series.reshape(count, outer, inner)
    outer_index = jnp.arange(outer, dtype=jnp.int32)
    inner_index = jnp.arange(inner, dtype=jnp.int32)
    half_index = jnp.arange(half_inner, dtype=jnp.int32)
    angle_outer = (
        2.0
        * math.pi
        / outer
        * (outer_index[:, None] * outer_index[None, :] % outer).astype(jnp.float32)
    )
    outer_table = jnp.concatenate([jnp.cos(angle_outer), jnp.sin(angle_outer)], axis=1)
    section_one = jnp.einsum("npq,pk->nkq", grid, outer_table, precision=highest)
    section_re = section_one[:, :outer]
    section_im = -section_one[:, outer:]
    angle_twist = (
        2.0
        * math.pi
        / total
        * (outer_index[:, None] * inner_index[None, :] % total).astype(jnp.float32)
    )
    twist_cos = jnp.cos(angle_twist)
    twist_sin = jnp.sin(angle_twist)
    rotated = jnp.stack(
        [
            section_re * twist_cos + section_im * twist_sin,
            section_im * twist_cos - section_re * twist_sin,
        ]
    )
    angle_inner = (
        2.0
        * math.pi
        / inner
        * (inner_index[:, None] * half_index[None, :] % inner).astype(jnp.float32)
    )
    inner_table = jnp.concatenate([jnp.cos(angle_inner), jnp.sin(angle_inner)], axis=1)
    section_two = jnp.einsum("snkq,qm->snkm", rotated, inner_table, precision=highest)
    final_re = section_two[0, :, :, :half_inner] + section_two[1, :, :, half_inner:]
    final_im = section_two[1, :, :, :half_inner] - section_two[0, :, :, half_inner:]
    spectrum_power = (final_re * final_re + final_im * final_im) / (C * total)
    spectrum_power = jnp.transpose(spectrum_power, (0, 2, 1)).reshape(count, total // 2)
    fundamentals = harmonic_bins.shape[1]
    fundamental = jnp.arange(fundamentals, dtype=jnp.int32)
    stride = jnp.arange(1, HARM + 1, dtype=jnp.int32)[:, None]
    offsets = (harmonic_bins - stride * fundamental[None, :])[:, :, None]
    vmem = pl.BlockSpec(memory_space=pltpu.VMEM)
    harmonic = pl.pallas_call(
        harmonic_kernel,
        out_shape=jax.ShapeDtypeStruct((count, fundamentals), jnp.float32),
        in_specs=[vmem, vmem],
        out_specs=vmem,
        scratch_shapes=[pltpu.VMEM((total // 2, count), jnp.float32)],
    )(spectrum_power, offsets)
    return spectrum_power, harmonic


def on_device(filterbank, first_rows, second_rows, shifts, harmonic_bins):
    channels = filterbank.shape[0]
    samples = filterbank.shape[1]
    local_levels = channels.bit_length() - 1
    chan_count = lax.axis_size("chan")
    tm_count = lax.axis_size("tm")
    cross_levels = chan_count.bit_length() - 1
    levels = local_levels + cross_levels
    rim = lax.ppermute(
        filterbank[:, samples - RAW_HALO :],
        "tm",
        [(source, source + 1) for source in range(tm_count - 1)],
    )
    widened = jnp.concatenate([rim, filterbank], axis=1)
    local_plan = [
        (2**level, 2 ** (level + 1), channels >> (level + 1)) for level in range(local_levels)
    ]
    sub = samples // chan_count
    pieces = run_local(
        widened.astype(jnp.float32).reshape(channels, -1, LANES).transpose(1, 0, 2)[None],
        jnp.stack([first_rows, second_rows, shifts])[:, :local_levels, :channels],
        local_plan,
        chan_count,
        sub,
        RAW_HALO - SUB_HALO,
    )
    cross_tables = jnp.stack([first_rows, second_rows, shifts])[:, local_levels:]
    pieces, cross_tables = lax.optimization_barrier((pieces, cross_tables))
    window = sub + SUB_HALO
    layers = lax.all_to_all(pieces, "chan", split_axis=0, concat_axis=0, tiled=True)
    cross_plan = []
    bands = chan_count
    for level in range(local_levels, levels):
        bands //= 2
        rows_in = min(2**level, NDM)
        cross_plan.append((rows_in, min(2 ** (level + 1), NDM), bands, min(rows_in, NDM // 2)))
    plane = run_matmul_levels(
        layers.reshape(chan_count * channels, window),
        cross_tables[0],
        cross_tables[1],
        cross_tables[2],
        list(range(levels - local_levels)),
        cross_plan,
    )
    groups = chan_count * tm_count
    share = NDM // groups
    outgoing = plane.reshape(groups, share // 2, 2 * sub)
    incoming = lax.all_to_all(outgoing, ("chan", "tm"), split_axis=0, concat_axis=0, tiled=True)
    series = (
        incoming.reshape(chan_count, tm_count, share // 2, 2, sub)
        .transpose(2, 3, 1, 0, 4)
        .reshape(share, tm_count * samples)
    )
    return spectra(series, harmonic_bins)


def solution(mesh):
    in_specs = (P("chan", "tm"), P(), P(), P(), P())
    out_specs = (P(("chan", "tm"), None), P(("chan", "tm"), None))
    return jax.shard_map(
        on_device, mesh=mesh, in_specs=in_specs, out_specs=out_specs, check_vma=False
    )
```

```python
import functools
import math

import jax
import jax.numpy as jnp
from jax import lax
from jax.experimental import pallas as pl
from jax.experimental.pallas import tpu as pltpu
from jax.sharding import PartitionSpec as P

C = 4096
NDM = 2048
SHIFT = 16
DFT_OUTER = 64
HARM = 8
RAW_HALO = 256
SUB_HALO = 64
TILE = 2048
LANES = 128
PIECES = 2


def shift_right(value, amount):
    width = value.shape[-1]
    pad = [(0, 0)] * (value.ndim - 1) + [(amount, 0)]
    return jnp.pad(value, pad)[..., :width]


def merge_level(paired, rows_first, rows_second, delays):
    lower_bands = jnp.take(paired[0::2], rows_first, axis=1)
    upper_bands = jnp.take(paired[1::2], rows_second, axis=1)
    delay_col = delays[None, :, None]
    shifted = upper_bands
    for bit in (1, 2, 4, 8):
        shifted = jnp.where((delay_col & bit) != 0, shift_right(shifted, bit), shifted)
    return lower_bands + shifted


def level_merge(layers, first_rows, second_rows, shifts, level):
    count = min(2 ** (level + 1), NDM)
    return merge_level(
        layers, first_rows[level, :count], second_rows[level, :count], shifts[level, :count]
    )


def split_pieces(block):
    high = block.astype(jnp.bfloat16)
    low = (block - high.astype(jnp.float32)).astype(jnp.bfloat16)
    return high, low


def matmul_kernel(plan, x_ref, *refs):
    count = len(plan)
    tables = refs[: 3 * count]
    out_ref, buf_a, buf_b, parts, pack = refs[3 * count :]
    width = x_ref.shape[1]
    source = x_ref
    for step, (row_in, row_out, bands_out, depth) in enumerate(plan):
        pick_low, pick_high, delay = tables[3 * step : 3 * step + 3]
        target = out_ref if step == count - 1 else (buf_a, buf_b)[step % 2]
        group = 2 if bands_out >= 2 else 1
        lanes = group * width
        tile_rows = min(TILE, row_out)
        for first_band in range(0, bands_out, group):
            for member in range(group):
                band = first_band + member
                for side in range(2):
                    block = source[pl.ds((2 * band + side) * row_in, depth), :]
                    for piece, value in enumerate(split_pieces(block)):
                        parts[side, piece, pl.ds(0, depth), pl.ds(member * width, width)] = value

            def tile(index, carry, target=target, first_band=first_band, depth=depth,
                     row_out=row_out, group=group, lanes=lanes, tile_rows=tile_rows,
                     pick_low=pick_low, pick_high=pick_high, delay=delay):
                rows = pl.ds(pl.multiple_of(index * tile_rows, tile_rows), tile_rows)
                low_sel = pick_low[rows, :]
                high_sel = pick_high[rows, :]
                lower = None
                upper = None
                for piece in range(PIECES):
                    term = jnp.dot(low_sel, parts[0, piece, pl.ds(0, depth), pl.ds(0, lanes)],
                                   preferred_element_type=jnp.float32)
                    lower = term if lower is None else lower + term
                    term = jnp.dot(high_sel, parts[1, piece, pl.ds(0, depth), pl.ds(0, lanes)],
                                   preferred_element_type=jnp.float32)
                    upper = term if upper is None else upper + term
                amount = delay[rows, :]
                for bit in (1, 2, 4, 8):
                    upper = jnp.where((amount & bit) != 0, pltpu.roll(upper, bit, 1), upper)
                merged = lower + upper
                if target is out_ref:
                    pack[...] = merged
                    even = pack[pl.ds(0, tile_rows // 2, stride=2), :]
                    odd = pack[pl.ds(1, tile_rows // 2, stride=2), :]
                    lane = lax.broadcasted_iota(jnp.int32, even.shape, 1)
                    start = pl.multiple_of(index * (tile_rows // 2), tile_rows // 2)
                    target[pl.ds(start, tile_rows // 2), :] = jnp.where(
                        lane < SUB_HALO, pltpu.roll(even, SUB_HALO, 1), odd
                    )
                    return carry
                for member in range(group):
                    start = pl.multiple_of((first_band + member) * row_out + index * tile_rows, tile_rows)
                    target[pl.ds(start, tile_rows), :] = merged[:, member * width : (member + 1) * width]
                return carry

            lax.fori_loop(0, row_out // tile_rows, tile, 0)
        source = target


def run_matmul_levels(state, first_rows, second_rows, shifts, levels, plan):
    width = state.shape[1]
    tables = []
    for level, (row_in, row_out, bands_out, depth) in zip(levels, plan):
        columns = jnp.arange(depth, dtype=jnp.int32)[None, :]
        tables.append((first_rows[level, :row_out, None] == columns).astype(jnp.bfloat16))
        tables.append((second_rows[level, :row_out, None] == columns).astype(jnp.bfloat16))
        tables.append(shifts[level, :row_out, None])
    buf_rows = max(p[1] * p[2] for p in plan)
    depth_most = max(p[3] for p in plan)
    vmem = pl.BlockSpec(memory_space=pltpu.VMEM)
    return pl.pallas_call(
        functools.partial(matmul_kernel, plan),
        out_shape=jax.ShapeDtypeStruct((plan[-1][1] * plan[-1][2] // 2, width), jnp.float32),
        in_specs=[vmem] * (1 + len(tables)),
        out_specs=vmem,
        scratch_shapes=[
            pltpu.VMEM((buf_rows, width), jnp.float32),
            pltpu.VMEM((buf_rows, width), jnp.float32),
            pltpu.VMEM((2, PIECES, depth_most, 2 * width), jnp.bfloat16),
            pltpu.VMEM((min(TILE, plan[-1][1]), width), jnp.float32),
        ],
        compiler_params=pltpu.CompilerParams(vmem_limit_bytes=60 * 1024 * 1024),
    )(state, *tables)


def harmonic_kernel(spectrum_ref, offset_ref, out_ref, power_ref):
    fundamentals = out_ref.shape[1]
    power_ref[...] = jnp.transpose(spectrum_ref[...])
    total = None
    for order in range(HARM):
        stride = order + 1
        offset = jnp.broadcast_to(offset_ref[order], (fundamentals, power_ref.shape[1]))
        term = power_ref[pl.ds(0, fundamentals, stride=stride), :]
        for phase in range(1, stride):
            picked = power_ref[pl.ds(phase, fundamentals, stride=stride), :]
            term = jnp.where(offset == phase, picked, term)
        total = term if total is None else total + term
    out_ref[...] = jnp.transpose(total * (1.0 / HARM))


def delayed(value, amount):
    rolled = pltpu.roll(value, amount, 2)
    previous = jnp.concatenate([rolled[-1:], rolled[:-1]], axis=0)
    lane = lax.broadcasted_iota(jnp.int32, value.shape, 2)
    return jnp.where(lane < amount, previous, rolled)


def local_kernel(plan, sub, base, table_ref, x_ref, out_ref, *bufs):
    count = len(plan)
    final = bufs[-1]
    source = x_ref
    for step, (row_in, row_out, bands_out) in enumerate(plan):
        target = final if step == count - 1 else bufs[step]

        def body(row, carry, source=source, target=target, step=step,
                 bands_out=bands_out, last=step == count - 1):
            lower = source[table_ref[0, step, row], :, pl.ds(0, bands_out, stride=2), :]
            upper = source[table_ref[1, step, row], :, pl.ds(1, bands_out, stride=2), :]
            merged = lower + delayed(upper, table_ref[2, step, row])
            if last:
                target[:, pl.ds(row, 1), :] = merged
            else:
                target[row] = merged
            return carry

        lax.fori_loop(0, row_out, body, 0, unroll=min(row_out, 32 if bands_out <= 2 else 16))
        source = target
    for dest in range(out_ref.shape[0]):
        start = base + sub * dest
        slab, offset = start // LANES, start % LANES
        if offset == 0:
            out_ref[dest] = final[slab]
        else:
            lane = lax.broadcasted_iota(jnp.int32, final.shape[1:], 1)
            head = pltpu.roll(final[slab], LANES - offset, 1)
            tail = pltpu.roll(final[slab + 1], LANES - offset, 1)
            out_ref[dest] = jnp.where(lane < LANES - offset, head, tail)


def run_local(state, tables, plan, parts, sub, base):
    slabs = state.shape[1]
    rows_last = plan[-1][1]
    smem = pl.BlockSpec(memory_space=pltpu.SMEM)
    vmem = pl.BlockSpec(memory_space=pltpu.VMEM)
    scratch = [pltpu.VMEM((p[1], slabs, p[2], LANES), jnp.float32) for p in plan[:-1]]
    scratch.append(pltpu.VMEM((slabs, rows_last, LANES), jnp.float32))
    return pl.pallas_call(
        functools.partial(local_kernel, plan, sub, base),
        out_shape=jax.ShapeDtypeStruct((parts, rows_last, sub + SUB_HALO), jnp.float32),
        in_specs=[smem, vmem],
        out_specs=vmem,
        scratch_shapes=scratch,
        compiler_params=pltpu.CompilerParams(vmem_limit_bytes=56 * 1024 * 1024),
    )(tables, state)


def spectra(series, harmonic_bins):
    count = series.shape[0]
    total = series.shape[1]
    outer = DFT_OUTER
    inner = total // outer
    half_inner = inner // 2
    highest = lax.Precision.HIGHEST
    grid = series.reshape(count, outer, inner)
    outer_index = jnp.arange(outer, dtype=jnp.int32)
    inner_index = jnp.arange(inner, dtype=jnp.int32)
    half_index = jnp.arange(half_inner, dtype=jnp.int32)
    angle_outer = (
        2.0
        * math.pi
        / outer
        * (outer_index[:, None] * outer_index[None, :] % outer).astype(jnp.float32)
    )
    outer_table = jnp.concatenate([jnp.cos(angle_outer), jnp.sin(angle_outer)], axis=1)
    section_one = jnp.einsum("npq,pk->nkq", grid, outer_table, precision=highest)
    section_re = section_one[:, :outer]
    section_im = -section_one[:, outer:]
    angle_twist = (
        2.0
        * math.pi
        / total
        * (outer_index[:, None] * inner_index[None, :] % total).astype(jnp.float32)
    )
    twist_cos = jnp.cos(angle_twist)
    twist_sin = jnp.sin(angle_twist)
    rotated = jnp.stack(
        [
            section_re * twist_cos + section_im * twist_sin,
            section_im * twist_cos - section_re * twist_sin,
        ]
    )
    angle_inner = (
        2.0
        * math.pi
        / inner
        * (inner_index[:, None] * half_index[None, :] % inner).astype(jnp.float32)
    )
    inner_table = jnp.concatenate([jnp.cos(angle_inner), jnp.sin(angle_inner)], axis=1)
    section_two = jnp.einsum("snkq,qm->snkm", rotated, inner_table, precision=highest)
    final_re = section_two[0, :, :, :half_inner] + section_two[1, :, :, half_inner:]
    final_im = section_two[1, :, :, :half_inner] - section_two[0, :, :, half_inner:]
    spectrum_power = (final_re * final_re + final_im * final_im) / (C * total)
    spectrum_power = jnp.transpose(spectrum_power, (0, 2, 1)).reshape(count, total // 2)
    fundamentals = harmonic_bins.shape[1]
    fundamental = jnp.arange(fundamentals, dtype=jnp.int32)
    stride = jnp.arange(1, HARM + 1, dtype=jnp.int32)[:, None]
    offsets = (harmonic_bins - stride * fundamental[None, :])[:, :, None]
    vmem = pl.BlockSpec(memory_space=pltpu.VMEM)
    harmonic = pl.pallas_call(
        harmonic_kernel,
        out_shape=jax.ShapeDtypeStruct((count, fundamentals), jnp.float32),
        in_specs=[vmem, vmem],
        out_specs=vmem,
        scratch_shapes=[pltpu.VMEM((total // 2, count), jnp.float32)],
    )(spectrum_power, offsets)
    return spectrum_power, harmonic


def on_device(filterbank, first_rows, second_rows, shifts, harmonic_bins):
    channels = filterbank.shape[0]
    samples = filterbank.shape[1]
    local_levels = channels.bit_length() - 1
    chan_count = lax.axis_size("chan")
    tm_count = lax.axis_size("tm")
    cross_levels = chan_count.bit_length() - 1
    levels = local_levels + cross_levels
    rim = lax.ppermute(
        filterbank[:, samples - RAW_HALO :],
        "tm",
        [(source, source + 1) for source in range(tm_count - 1)],
    )
    widened = jnp.concatenate([rim, filterbank], axis=1)
    local_plan = [
        (2**level, 2 ** (level + 1), channels >> (level + 1)) for level in range(local_levels)
    ]
    sub = samples // chan_count
    pieces = run_local(
        widened.astype(jnp.float32).reshape(channels, -1, LANES).transpose(1, 0, 2)[None],
        jnp.stack([first_rows, second_rows, shifts])[:, :local_levels, :channels],
        local_plan,
        chan_count,
        sub,
        RAW_HALO - SUB_HALO,
    )
    cross_tables = jnp.stack([first_rows, second_rows, shifts])[:, local_levels:]
    pieces, cross_tables = lax.optimization_barrier((pieces, cross_tables))
    window = sub + SUB_HALO
    layers = lax.all_to_all(pieces, "chan", split_axis=0, concat_axis=0, tiled=True)
    cross_plan = []
    bands = chan_count
    for level in range(local_levels, levels):
        bands //= 2
        rows_in = min(2**level, NDM)
        cross_plan.append((rows_in, min(2 ** (level + 1), NDM), bands, min(rows_in, NDM // 2)))
    plane = run_matmul_levels(
        layers.reshape(chan_count * channels, window),
        cross_tables[0],
        cross_tables[1],
        cross_tables[2],
        list(range(levels - local_levels)),
        cross_plan,
    )
    groups = chan_count * tm_count
    share = NDM // groups
    outgoing = plane.reshape(groups, share // 2, 2 * sub)
    incoming = lax.all_to_all(outgoing, ("chan", "tm"), split_axis=0, concat_axis=0, tiled=True)
    series = (
        incoming.reshape(chan_count, tm_count, share // 2, 2, sub)
        .transpose(2, 3, 1, 0, 4)
        .reshape(share, tm_count * samples)
    )
    return spectra(series, harmonic_bins)


def solution(mesh):
    in_specs = (P("chan", "tm"), P(), P(), P(), P())
    out_specs = (P(("chan", "tm"), None), P(("chan", "tm"), None))
    return jax.shard_map(
        on_device, mesh=mesh, in_specs=in_specs, out_specs=out_specs, check_vma=False
    )
```

```python
import functools
import math

import jax
import jax.numpy as jnp
from jax import lax
from jax.experimental import pallas as pl
from jax.experimental.pallas import tpu as pltpu
from jax.sharding import PartitionSpec as P

C = 4096
NDM = 2048
SHIFT = 16
DFT_OUTER = 64
HARM = 8
RAW_HALO = 256
SUB_HALO = 64
TILE = 1024
LANES = 128
PIECES = 2


def shift_right(value, amount):
    width = value.shape[-1]
    pad = [(0, 0)] * (value.ndim - 1) + [(amount, 0)]
    return jnp.pad(value, pad)[..., :width]


def merge_level(paired, rows_first, rows_second, delays):
    lower_bands = jnp.take(paired[0::2], rows_first, axis=1)
    upper_bands = jnp.take(paired[1::2], rows_second, axis=1)
    delay_col = delays[None, :, None]
    shifted = upper_bands
    for bit in (1, 2, 4, 8):
        shifted = jnp.where((delay_col & bit) != 0, shift_right(shifted, bit), shifted)
    return lower_bands + shifted


def level_merge(layers, first_rows, second_rows, shifts, level):
    count = min(2 ** (level + 1), NDM)
    return merge_level(
        layers, first_rows[level, :count], second_rows[level, :count], shifts[level, :count]
    )


def split_pieces(block):
    high = block.astype(jnp.bfloat16)
    low = (block - high.astype(jnp.float32)).astype(jnp.bfloat16)
    return high, low


def matmul_kernel(plan, x_ref, *refs):
    count = len(plan)
    tables = refs[: 3 * count]
    out_ref, buf_a, buf_b, parts, pack = refs[3 * count :]
    width = x_ref.shape[1]
    source = x_ref
    for step, (row_in, row_out, bands_out, depth) in enumerate(plan):
        pick_low, pick_high, delay = tables[3 * step : 3 * step + 3]
        target = out_ref if step == count - 1 else (buf_a, buf_b)[step % 2]
        group = 2 if bands_out >= 2 else 1
        lanes = group * width
        tile_rows = min(TILE, row_out)
        for first_band in range(0, bands_out, group):
            for member in range(group):
                band = first_band + member
                for side in range(2):
                    block = source[pl.ds((2 * band + side) * row_in, depth), :]
                    for piece, value in enumerate(split_pieces(block)):
                        parts[side, piece, pl.ds(0, depth), pl.ds(member * width, width)] = value

            def tile(index, carry, target=target, first_band=first_band, depth=depth,
                     row_out=row_out, group=group, lanes=lanes, tile_rows=tile_rows,
                     pick_low=pick_low, pick_high=pick_high, delay=delay):
                rows = pl.ds(pl.multiple_of(index * tile_rows, tile_rows), tile_rows)
                low_sel = pick_low[rows, :]
                high_sel = pick_high[rows, :]
                lower = None
                upper = None
                for piece in range(PIECES):
                    term = jnp.dot(low_sel, parts[0, piece, pl.ds(0, depth), pl.ds(0, lanes)],
                                   preferred_element_type=jnp.float32)
                    lower = term if lower is None else lower + term
                    term = jnp.dot(high_sel, parts[1, piece, pl.ds(0, depth), pl.ds(0, lanes)],
                                   preferred_element_type=jnp.float32)
                    upper = term if upper is None else upper + term
                amount = delay[rows, :]
                for bit in (1, 2, 4, 8):
                    upper = jnp.where((amount & bit) != 0, pltpu.roll(upper, bit, 1), upper)
                merged = lower + upper
                if target is out_ref:
                    pack[...] = merged
                    even = pack[pl.ds(0, tile_rows // 2, stride=2), :]
                    odd = pack[pl.ds(1, tile_rows // 2, stride=2), :]
                    lane = lax.broadcasted_iota(jnp.int32, even.shape, 1)
                    start = pl.multiple_of(index * (tile_rows // 2), tile_rows // 2)
                    target[pl.ds(start, tile_rows // 2), :] = jnp.where(
                        lane < SUB_HALO, pltpu.roll(even, SUB_HALO, 1), odd
                    )
                    return carry
                for member in range(group):
                    start = pl.multiple_of((first_band + member) * row_out + index * tile_rows, tile_rows)
                    target[pl.ds(start, tile_rows), :] = merged[:, member * width : (member + 1) * width]
                return carry

            lax.fori_loop(0, row_out // tile_rows, tile, 0)
        source = target


def run_matmul_levels(state, first_rows, second_rows, shifts, levels, plan):
    width = state.shape[1]
    tables = []
    for level, (row_in, row_out, bands_out, depth) in zip(levels, plan):
        columns = jnp.arange(depth, dtype=jnp.int32)[None, :]
        tables.append((first_rows[level, :row_out, None] == columns).astype(jnp.bfloat16))
        tables.append((second_rows[level, :row_out, None] == columns).astype(jnp.bfloat16))
        tables.append(shifts[level, :row_out, None])
    buf_rows = max(p[1] * p[2] for p in plan)
    depth_most = max(p[3] for p in plan)
    vmem = pl.BlockSpec(memory_space=pltpu.VMEM)
    return pl.pallas_call(
        functools.partial(matmul_kernel, plan),
        out_shape=jax.ShapeDtypeStruct((plan[-1][1] * plan[-1][2] // 2, width), jnp.float32),
        in_specs=[vmem] * (1 + len(tables)),
        out_specs=vmem,
        scratch_shapes=[
            pltpu.VMEM((buf_rows, width), jnp.float32),
            pltpu.VMEM((buf_rows, width), jnp.float32),
            pltpu.VMEM((2, PIECES, depth_most, 2 * width), jnp.bfloat16),
            pltpu.VMEM((min(TILE, plan[-1][1]), width), jnp.float32),
        ],
        compiler_params=pltpu.CompilerParams(vmem_limit_bytes=60 * 1024 * 1024),
    )(state, *tables)


def harmonic_kernel(spectrum_ref, offset_ref, out_ref, power_ref):
    fundamentals = out_ref.shape[1]
    power_ref[...] = jnp.transpose(spectrum_ref[...])
    total = None
    for order in range(HARM):
        stride = order + 1
        offset = jnp.broadcast_to(offset_ref[order], (fundamentals, power_ref.shape[1]))
        term = power_ref[pl.ds(0, fundamentals, stride=stride), :]
        for phase in range(1, stride):
            picked = power_ref[pl.ds(phase, fundamentals, stride=stride), :]
            term = jnp.where(offset == phase, picked, term)
        total = term if total is None else total + term
    out_ref[...] = jnp.transpose(total * (1.0 / HARM))


def delayed(value, amount):
    rolled = pltpu.roll(value, amount, 2)
    previous = jnp.concatenate([rolled[-1:], rolled[:-1]], axis=0)
    lane = lax.broadcasted_iota(jnp.int32, value.shape, 2)
    return jnp.where(lane < amount, previous, rolled)


def local_kernel(plan, sub, base, table_ref, x_ref, out_ref, *bufs):
    count = len(plan)
    final = bufs[-2]
    source = bufs[-1]
    source[...] = x_ref[...].astype(jnp.float32)
    for step, (row_in, row_out, bands_out) in enumerate(plan):
        target = final if step == count - 1 else bufs[step]

        def body(row, carry, source=source, target=target, step=step,
                 bands_out=bands_out, last=step == count - 1):
            lower = source[table_ref[0, step, row], :, pl.ds(0, bands_out, stride=2), :]
            upper = source[table_ref[1, step, row], :, pl.ds(1, bands_out, stride=2), :]
            merged = lower + delayed(upper, table_ref[2, step, row])
            if last:
                target[:, pl.ds(row, 1), :] = merged
            else:
                target[row] = merged
            return carry

        lax.fori_loop(0, row_out, body, 0, unroll=min(row_out, 32 if bands_out <= 2 else 16))
        source = target
    for dest in range(out_ref.shape[0]):
        start = base + sub * dest
        slab, offset = start // LANES, start % LANES
        if offset == 0:
            out_ref[dest] = final[slab]
        else:
            lane = lax.broadcasted_iota(jnp.int32, final.shape[1:], 1)
            head = pltpu.roll(final[slab], LANES - offset, 1)
            tail = pltpu.roll(final[slab + 1], LANES - offset, 1)
            out_ref[dest] = jnp.where(lane < LANES - offset, head, tail)


def run_local(state, tables, plan, parts, sub, base):
    slabs = state.shape[1]
    rows_last = plan[-1][1]
    smem = pl.BlockSpec(memory_space=pltpu.SMEM)
    vmem = pl.BlockSpec(memory_space=pltpu.VMEM)
    scratch = [pltpu.VMEM((p[1], slabs, p[2], LANES), jnp.float32) for p in plan[:-1]]
    scratch.append(pltpu.VMEM((slabs, rows_last, LANES), jnp.float32))
    scratch.append(pltpu.VMEM(state.shape, jnp.float32))
    return pl.pallas_call(
        functools.partial(local_kernel, plan, sub, base),
        out_shape=jax.ShapeDtypeStruct((parts, rows_last, sub + SUB_HALO), jnp.float32),
        in_specs=[smem, vmem],
        out_specs=vmem,
        scratch_shapes=scratch,
        compiler_params=pltpu.CompilerParams(vmem_limit_bytes=56 * 1024 * 1024),
    )(tables, state)


def spectra(series, harmonic_bins):
    count = series.shape[0]
    total = series.shape[1]
    outer = DFT_OUTER
    inner = total // outer
    half_inner = inner // 2
    highest = lax.Precision.HIGHEST
    grid = series.reshape(count, outer, inner)
    outer_index = jnp.arange(outer, dtype=jnp.int32)
    inner_index = jnp.arange(inner, dtype=jnp.int32)
    half_index = jnp.arange(half_inner, dtype=jnp.int32)
    angle_outer = (
        2.0
        * math.pi
        / outer
        * (outer_index[:, None] * outer_index[None, :] % outer).astype(jnp.float32)
    )
    outer_table = jnp.concatenate([jnp.cos(angle_outer), jnp.sin(angle_outer)], axis=1)
    section_one = jnp.einsum("npq,pk->nkq", grid, outer_table, precision=highest)
    section_re = section_one[:, :outer]
    section_im = -section_one[:, outer:]
    angle_twist = (
        2.0
        * math.pi
        / total
        * (outer_index[:, None] * inner_index[None, :] % total).astype(jnp.float32)
    )
    twist_cos = jnp.cos(angle_twist)
    twist_sin = jnp.sin(angle_twist)
    rotated = jnp.stack(
        [
            section_re * twist_cos + section_im * twist_sin,
            section_im * twist_cos - section_re * twist_sin,
        ]
    )
    angle_inner = (
        2.0
        * math.pi
        / inner
        * (inner_index[:, None] * half_index[None, :] % inner).astype(jnp.float32)
    )
    inner_table = jnp.concatenate([jnp.cos(angle_inner), jnp.sin(angle_inner)], axis=1)
    section_two = jnp.einsum("snkq,qm->snkm", rotated, inner_table, precision=highest)
    final_re = section_two[0, :, :, :half_inner] + section_two[1, :, :, half_inner:]
    final_im = section_two[1, :, :, :half_inner] - section_two[0, :, :, half_inner:]
    spectrum_power = (final_re * final_re + final_im * final_im) / (C * total)
    spectrum_power = jnp.transpose(spectrum_power, (0, 2, 1)).reshape(count, total // 2)
    fundamentals = harmonic_bins.shape[1]
    fundamental = jnp.arange(fundamentals, dtype=jnp.int32)
    stride = jnp.arange(1, HARM + 1, dtype=jnp.int32)[:, None]
    offsets = (harmonic_bins - stride * fundamental[None, :])[:, :, None]
    vmem = pl.BlockSpec(memory_space=pltpu.VMEM)
    harmonic = pl.pallas_call(
        harmonic_kernel,
        out_shape=jax.ShapeDtypeStruct((count, fundamentals), jnp.float32),
        in_specs=[vmem, vmem],
        out_specs=vmem,
        scratch_shapes=[pltpu.VMEM((total // 2, count), jnp.float32)],
    )(spectrum_power, offsets)
    return spectrum_power, harmonic


def on_device(filterbank, first_rows, second_rows, shifts, harmonic_bins):
    channels = filterbank.shape[0]
    samples = filterbank.shape[1]
    local_levels = channels.bit_length() - 1
    chan_count = lax.axis_size("chan")
    tm_count = lax.axis_size("tm")
    cross_levels = chan_count.bit_length() - 1
    levels = local_levels + cross_levels
    rim = lax.ppermute(
        filterbank[:, samples - RAW_HALO :],
        "tm",
        [(source, source + 1) for source in range(tm_count - 1)],
    )
    widened = jnp.concatenate([rim, filterbank], axis=1)
    local_plan = [
        (2**level, 2 ** (level + 1), channels >> (level + 1)) for level in range(local_levels)
    ]
    sub = samples // chan_count
    pieces = run_local(
        widened.reshape(channels, -1, LANES).transpose(1, 0, 2)[None],
        jnp.stack([first_rows, second_rows, shifts])[:, :local_levels, :channels],
        local_plan,
        chan_count,
        sub,
        RAW_HALO - SUB_HALO,
    )
    cross_tables = jnp.stack([first_rows, second_rows, shifts])[:, local_levels:]
    pieces, cross_tables = lax.optimization_barrier((pieces, cross_tables))
    window = sub + SUB_HALO
    layers = lax.all_to_all(pieces, "chan", split_axis=0, concat_axis=0, tiled=True)
    cross_plan = []
    bands = chan_count
    for level in range(local_levels, levels):
        bands //= 2
        rows_in = min(2**level, NDM)
        cross_plan.append((rows_in, min(2 ** (level + 1), NDM), bands, min(rows_in, NDM // 2)))
    plane = run_matmul_levels(
        layers.reshape(chan_count * channels, window),
        cross_tables[0],
        cross_tables[1],
        cross_tables[2],
        list(range(levels - local_levels)),
        cross_plan,
    )
    groups = chan_count * tm_count
    share = NDM // groups
    outgoing = plane.reshape(groups, share // 2, 2 * sub)
    incoming = lax.all_to_all(outgoing, ("chan", "tm"), split_axis=0, concat_axis=0, tiled=True)
    series = (
        incoming.reshape(chan_count, tm_count, share // 2, 2, sub)
        .transpose(2, 3, 1, 0, 4)
        .reshape(share, tm_count * samples)
    )
    return spectra(series, harmonic_bins)


def solution(mesh):
    in_specs = (P("chan", "tm"), P(), P(), P(), P())
    out_specs = (P(("chan", "tm"), None), P(("chan", "tm"), None))
    return jax.shard_map(
        on_device, mesh=mesh, in_specs=in_specs, out_specs=out_specs, check_vma=False
    )
```

```python
import functools
import math

import jax
import jax.numpy as jnp
from jax import lax
from jax.experimental import pallas as pl
from jax.experimental.pallas import tpu as pltpu
from jax.sharding import PartitionSpec as P

C = 4096
NDM = 2048
SHIFT = 16
DFT_OUTER = 64
HARM = 8
RAW_HALO = 256
SUB_HALO = 64
TILE = 1024
LANES = 128
PIECES = 2


def shift_right(value, amount):
    width = value.shape[-1]
    pad = [(0, 0)] * (value.ndim - 1) + [(amount, 0)]
    return jnp.pad(value, pad)[..., :width]


def merge_level(paired, rows_first, rows_second, delays):
    lower_bands = jnp.take(paired[0::2], rows_first, axis=1)
    upper_bands = jnp.take(paired[1::2], rows_second, axis=1)
    delay_col = delays[None, :, None]
    shifted = upper_bands
    for bit in (1, 2, 4, 8):
        shifted = jnp.where((delay_col & bit) != 0, shift_right(shifted, bit), shifted)
    return lower_bands + shifted


def level_merge(layers, first_rows, second_rows, shifts, level):
    count = min(2 ** (level + 1), NDM)
    return merge_level(
        layers, first_rows[level, :count], second_rows[level, :count], shifts[level, :count]
    )


def split_pieces(block):
    high = block.astype(jnp.bfloat16)
    low = (block - high.astype(jnp.float32)).astype(jnp.bfloat16)
    return high, low


def matmul_kernel(plan, x_ref, *refs):
    count = len(plan)
    tables = refs[: 3 * count]
    out_ref, buf_a, buf_b, parts, pack = refs[3 * count :]
    width = x_ref.shape[1]
    source = x_ref
    for step, (row_in, row_out, bands_out, depth) in enumerate(plan):
        pick_low, pick_high, delay = tables[3 * step : 3 * step + 3]
        target = out_ref if step == count - 1 else (buf_a, buf_b)[step % 2]
        group = 2 if bands_out >= 2 else 1
        lanes = group * width
        tile_rows = min(TILE, row_out)
        for first_band in range(0, bands_out, group):
            for member in range(group):
                band = first_band + member
                for side in range(2):
                    block = source[pl.ds((2 * band + side) * row_in, depth), :]
                    for piece, value in enumerate(split_pieces(block)):
                        parts[side, piece, pl.ds(0, depth), pl.ds(member * width, width)] = value

            def tile(index, carry, target=target, first_band=first_band, depth=depth,
                     row_out=row_out, group=group, lanes=lanes, tile_rows=tile_rows,
                     pick_low=pick_low, pick_high=pick_high, delay=delay):
                rows = pl.ds(pl.multiple_of(index * tile_rows, tile_rows), tile_rows)
                low_sel = pick_low[rows, :]
                high_sel = pick_high[rows, :]
                lower = None
                upper = None
                for piece in range(PIECES):
                    term = jnp.dot(low_sel, parts[0, piece, pl.ds(0, depth), pl.ds(0, lanes)],
                                   preferred_element_type=jnp.float32)
                    lower = term if lower is None else lower + term
                    term = jnp.dot(high_sel, parts[1, piece, pl.ds(0, depth), pl.ds(0, lanes)],
                                   preferred_element_type=jnp.float32)
                    upper = term if upper is None else upper + term
                amount = delay[rows, :]
                for bit in (1, 2, 4, 8):
                    upper = jnp.where((amount & bit) != 0, pltpu.roll(upper, bit, 1), upper)
                merged = lower + upper
                if target is out_ref:
                    pack[...] = merged
                    even = pack[pl.ds(0, tile_rows // 2, stride=2), :]
                    odd = pack[pl.ds(1, tile_rows // 2, stride=2), :]
                    lane = lax.broadcasted_iota(jnp.int32, even.shape, 1)
                    start = pl.multiple_of(index * (tile_rows // 2), tile_rows // 2)
                    target[pl.ds(start, tile_rows // 2), :] = jnp.where(
                        lane < SUB_HALO, pltpu.roll(even, SUB_HALO, 1), odd
                    )
                    return carry
                for member in range(group):
                    start = pl.multiple_of((first_band + member) * row_out + index * tile_rows, tile_rows)
                    target[pl.ds(start, tile_rows), :] = merged[:, member * width : (member + 1) * width]
                return carry

            lax.fori_loop(0, row_out // tile_rows, tile, 0)
        source = target


def run_matmul_levels(state, first_rows, second_rows, shifts, levels, plan):
    width = state.shape[1]
    tables = []
    for level, (row_in, row_out, bands_out, depth) in zip(levels, plan):
        columns = jnp.arange(depth, dtype=jnp.int32)[None, :]
        tables.append((first_rows[level, :row_out, None] == columns).astype(jnp.bfloat16))
        tables.append((second_rows[level, :row_out, None] == columns).astype(jnp.bfloat16))
        tables.append(shifts[level, :row_out, None])
    buf_rows = max(p[1] * p[2] for p in plan)
    depth_most = max(p[3] for p in plan)
    vmem = pl.BlockSpec(memory_space=pltpu.VMEM)
    return pl.pallas_call(
        functools.partial(matmul_kernel, plan),
        out_shape=jax.ShapeDtypeStruct((plan[-1][1] * plan[-1][2] // 2, width), jnp.float32),
        in_specs=[vmem] * (1 + len(tables)),
        out_specs=vmem,
        scratch_shapes=[
            pltpu.VMEM((buf_rows, width), jnp.float32),
            pltpu.VMEM((buf_rows, width), jnp.float32),
            pltpu.VMEM((2, PIECES, depth_most, 2 * width), jnp.bfloat16),
            pltpu.VMEM((min(TILE, plan[-1][1]), width), jnp.float32),
        ],
        compiler_params=pltpu.CompilerParams(vmem_limit_bytes=60 * 1024 * 1024),
    )(state, *tables)


def harmonic_kernel(spectrum_ref, offset_ref, out_ref, power_ref):
    fundamentals = out_ref.shape[1]
    power_ref[...] = jnp.transpose(spectrum_ref[...])
    total = None
    for order in range(HARM):
        stride = order + 1
        offset = jnp.broadcast_to(offset_ref[order], (fundamentals, power_ref.shape[1]))
        term = power_ref[pl.ds(0, fundamentals, stride=stride), :]
        for phase in range(1, stride):
            picked = power_ref[pl.ds(phase, fundamentals, stride=stride), :]
            term = jnp.where(offset == phase, picked, term)
        total = term if total is None else total + term
    out_ref[...] = jnp.transpose(total * (1.0 / HARM))


def delayed(value, amount):
    rolled = pltpu.roll(value, amount, 2)
    previous = jnp.concatenate([rolled[-1:], rolled[:-1]], axis=0)
    lane = lax.broadcasted_iota(jnp.int32, value.shape, 2)
    return jnp.where(lane < amount, previous, rolled)


def local_kernel(plan, sub, base, table_ref, x_ref, out_ref, *bufs):
    count = len(plan)
    final = bufs[-1]
    source = x_ref
    for step, (row_in, row_out, bands_out) in enumerate(plan):
        target = final if step == count - 1 else bufs[step]

        def body(row, carry, source=source, target=target, step=step,
                 bands_out=bands_out, last=step == count - 1):
            lower = source[table_ref[0, step, row], :, pl.ds(0, bands_out, stride=2), :]
            upper = source[table_ref[1, step, row], :, pl.ds(1, bands_out, stride=2), :]
            merged = lower + delayed(upper, table_ref[2, step, row])
            if last:
                target[:, pl.ds(row, 1), :] = merged
            else:
                target[row] = merged
            return carry

        lax.fori_loop(0, row_out, body, 0, unroll=min(row_out, 32 if bands_out <= 2 else 16))
        source = target
    for dest in range(out_ref.shape[0]):
        start = base + sub * dest
        slab, offset = start // LANES, start % LANES
        if offset == 0:
            out_ref[dest] = final[slab]
        else:
            lane = lax.broadcasted_iota(jnp.int32, final.shape[1:], 1)
            head = pltpu.roll(final[slab], LANES - offset, 1)
            tail = pltpu.roll(final[slab + 1], LANES - offset, 1)
            out_ref[dest] = jnp.where(lane < LANES - offset, head, tail)


def run_local(state, tables, plan, parts, sub, base):
    slabs = state.shape[1]
    rows_last = plan[-1][1]
    smem = pl.BlockSpec(memory_space=pltpu.SMEM)
    vmem = pl.BlockSpec(memory_space=pltpu.VMEM)
    scratch = [pltpu.VMEM((p[1], slabs, p[2], LANES), jnp.float32) for p in plan[:-1]]
    scratch.append(pltpu.VMEM((slabs, rows_last, LANES), jnp.float32))
    return pl.pallas_call(
        functools.partial(local_kernel, plan, sub, base),
        out_shape=jax.ShapeDtypeStruct((parts, rows_last, sub + SUB_HALO), jnp.float32),
        in_specs=[smem, vmem],
        out_specs=vmem,
        scratch_shapes=scratch,
        compiler_params=pltpu.CompilerParams(vmem_limit_bytes=56 * 1024 * 1024),
    )(tables, state)


def spectra(series, harmonic_bins):
    count = series.shape[0]
    total = series.shape[1]
    outer = DFT_OUTER
    inner = total // outer
    half_inner = inner // 2
    highest = lax.Precision.HIGH
    grid = series.reshape(count, outer, inner)
    outer_index = jnp.arange(outer, dtype=jnp.int32)
    inner_index = jnp.arange(inner, dtype=jnp.int32)
    half_index = jnp.arange(half_inner, dtype=jnp.int32)
    angle_outer = (
        2.0
        * math.pi
        / outer
        * (outer_index[:, None] * outer_index[None, :] % outer).astype(jnp.float32)
    )
    outer_table = jnp.concatenate([jnp.cos(angle_outer), jnp.sin(angle_outer)], axis=1)
    section_one = jnp.einsum("npq,pk->nkq", grid, outer_table, precision=highest)
    section_re = section_one[:, :outer]
    section_im = -section_one[:, outer:]
    angle_twist = (
        2.0
        * math.pi
        / total
        * (outer_index[:, None] * inner_index[None, :] % total).astype(jnp.float32)
    )
    twist_cos = jnp.cos(angle_twist)
    twist_sin = jnp.sin(angle_twist)
    rotated = jnp.stack(
        [
            section_re * twist_cos + section_im * twist_sin,
            section_im * twist_cos - section_re * twist_sin,
        ]
    )
    angle_inner = (
        2.0
        * math.pi
        / inner
        * (inner_index[:, None] * half_index[None, :] % inner).astype(jnp.float32)
    )
    inner_table = jnp.concatenate([jnp.cos(angle_inner), jnp.sin(angle_inner)], axis=1)
    section_two = jnp.einsum("snkq,qm->snkm", rotated, inner_table, precision=highest)
    final_re = section_two[0, :, :, :half_inner] + section_two[1, :, :, half_inner:]
    final_im = section_two[1, :, :, :half_inner] - section_two[0, :, :, half_inner:]
    spectrum_power = (final_re * final_re + final_im * final_im) / (C * total)
    spectrum_power = jnp.transpose(spectrum_power, (0, 2, 1)).reshape(count, total // 2)
    fundamentals = harmonic_bins.shape[1]
    fundamental = jnp.arange(fundamentals, dtype=jnp.int32)
    stride = jnp.arange(1, HARM + 1, dtype=jnp.int32)[:, None]
    offsets = (harmonic_bins - stride * fundamental[None, :])[:, :, None]
    vmem = pl.BlockSpec(memory_space=pltpu.VMEM)
    harmonic = pl.pallas_call(
        harmonic_kernel,
        out_shape=jax.ShapeDtypeStruct((count, fundamentals), jnp.float32),
        in_specs=[vmem, vmem],
        out_specs=vmem,
        scratch_shapes=[pltpu.VMEM((total // 2, count), jnp.float32)],
    )(spectrum_power, offsets)
    return spectrum_power, harmonic


def on_device(filterbank, first_rows, second_rows, shifts, harmonic_bins):
    channels = filterbank.shape[0]
    samples = filterbank.shape[1]
    local_levels = channels.bit_length() - 1
    chan_count = lax.axis_size("chan")
    tm_count = lax.axis_size("tm")
    cross_levels = chan_count.bit_length() - 1
    levels = local_levels + cross_levels
    rim = lax.ppermute(
        filterbank[:, samples - RAW_HALO :],
        "tm",
        [(source, source + 1) for source in range(tm_count - 1)],
    )
    widened = jnp.concatenate([rim, filterbank], axis=1)
    local_plan = [
        (2**level, 2 ** (level + 1), channels >> (level + 1)) for level in range(local_levels)
    ]
    sub = samples // chan_count
    pieces = run_local(
        widened.astype(jnp.float32).reshape(channels, -1, LANES).transpose(1, 0, 2)[None],
        jnp.stack([first_rows, second_rows, shifts])[:, :local_levels, :channels],
        local_plan,
        chan_count,
        sub,
        RAW_HALO - SUB_HALO,
    )
    cross_tables = jnp.stack([first_rows, second_rows, shifts])[:, local_levels:]
    pieces, cross_tables = lax.optimization_barrier((pieces, cross_tables))
    window = sub + SUB_HALO
    layers = lax.all_to_all(pieces, "chan", split_axis=0, concat_axis=0, tiled=True)
    cross_plan = []
    bands = chan_count
    for level in range(local_levels, levels):
        bands //= 2
        rows_in = min(2**level, NDM)
        cross_plan.append((rows_in, min(2 ** (level + 1), NDM), bands, min(rows_in, NDM // 2)))
    plane = run_matmul_levels(
        layers.reshape(chan_count * channels, window),
        cross_tables[0],
        cross_tables[1],
        cross_tables[2],
        list(range(levels - local_levels)),
        cross_plan,
    )
    groups = chan_count * tm_count
    share = NDM // groups
    outgoing = plane.reshape(groups, share // 2, 2 * sub)
    incoming = lax.all_to_all(outgoing, ("chan", "tm"), split_axis=0, concat_axis=0, tiled=True)
    series = (
        incoming.reshape(chan_count, tm_count, share // 2, 2, sub)
        .transpose(2, 3, 1, 0, 4)
        .reshape(share, tm_count * samples)
    )
    return spectra(series, harmonic_bins)


def solution(mesh):
    in_specs = (P("chan", "tm"), P(), P(), P(), P())
    out_specs = (P(("chan", "tm"), None), P(("chan", "tm"), None))
    return jax.shard_map(
        on_device, mesh=mesh, in_specs=in_specs, out_specs=out_specs, check_vma=False
    )
```

```python
import functools
import math

import jax
import jax.numpy as jnp
from jax import lax
from jax.experimental import pallas as pl
from jax.experimental.pallas import tpu as pltpu
from jax.sharding import PartitionSpec as P

C = 4096
NDM = 2048
SHIFT = 16
DFT_OUTER = 64
HARM = 8
RAW_HALO = 256
SUB_HALO = 64
TILE = 1024
LANES = 128
PIECES = 2


def shift_right(value, amount):
    width = value.shape[-1]
    pad = [(0, 0)] * (value.ndim - 1) + [(amount, 0)]
    return jnp.pad(value, pad)[..., :width]


def merge_level(paired, rows_first, rows_second, delays):
    lower_bands = jnp.take(paired[0::2], rows_first, axis=1)
    upper_bands = jnp.take(paired[1::2], rows_second, axis=1)
    delay_col = delays[None, :, None]
    shifted = upper_bands
    for bit in (1, 2, 4, 8):
        shifted = jnp.where((delay_col & bit) != 0, shift_right(shifted, bit), shifted)
    return lower_bands + shifted


def level_merge(layers, first_rows, second_rows, shifts, level):
    count = min(2 ** (level + 1), NDM)
    return merge_level(
        layers, first_rows[level, :count], second_rows[level, :count], shifts[level, :count]
    )


def split_pieces(block):
    high = block.astype(jnp.bfloat16)
    low = (block - high.astype(jnp.float32)).astype(jnp.bfloat16)
    return high, low


def matmul_kernel(plan, x_ref, *refs):
    count = len(plan)
    tables = refs[: 3 * count]
    out_ref, buf_a, buf_b, parts, pack = refs[3 * count :]
    width = x_ref.shape[1]
    source = x_ref
    for step, (row_in, row_out, bands_out, depth) in enumerate(plan):
        pick_low, pick_high, delay = tables[3 * step : 3 * step + 3]
        target = out_ref if step == count - 1 else (buf_a, buf_b)[step % 2]
        group = 2 if bands_out >= 2 else 1
        lanes = group * width
        tile_rows = min(TILE, row_out)
        for first_band in range(0, bands_out, group):
            for member in range(group):
                band = first_band + member
                for side in range(2):
                    block = source[pl.ds((2 * band + side) * row_in, depth), :]
                    for piece, value in enumerate(split_pieces(block)):
                        parts[side, piece, pl.ds(0, depth), pl.ds(member * width, width)] = value

            def tile(index, carry, target=target, first_band=first_band, depth=depth,
                     row_out=row_out, group=group, lanes=lanes, tile_rows=tile_rows,
                     pick_low=pick_low, pick_high=pick_high, delay=delay):
                rows = pl.ds(pl.multiple_of(index * tile_rows, tile_rows), tile_rows)
                low_sel = pick_low[rows, :]
                high_sel = pick_high[rows, :]
                lower = None
                upper = None
                for piece in range(PIECES):
                    term = jnp.dot(low_sel, parts[0, piece, pl.ds(0, depth), pl.ds(0, lanes)],
                                   preferred_element_type=jnp.float32)
                    lower = term if lower is None else lower + term
                    term = jnp.dot(high_sel, parts[1, piece, pl.ds(0, depth), pl.ds(0, lanes)],
                                   preferred_element_type=jnp.float32)
                    upper = term if upper is None else upper + term
                amount = delay[rows, :]
                for bit in (1, 2, 4, 8):
                    upper = jnp.where((amount & bit) != 0, pltpu.roll(upper, bit, 1), upper)
                merged = lower + upper
                if target is out_ref:
                    pack[...] = merged
                    even = pack[pl.ds(0, tile_rows // 2, stride=2), :]
                    odd = pack[pl.ds(1, tile_rows // 2, stride=2), :]
                    lane = lax.broadcasted_iota(jnp.int32, even.shape, 1)
                    start = pl.multiple_of(index * (tile_rows // 2), tile_rows // 2)
                    target[pl.ds(start, tile_rows // 2), :] = jnp.where(
                        lane < SUB_HALO, pltpu.roll(even, SUB_HALO, 1), odd
                    )
                    return carry
                for member in range(group):
                    start = pl.multiple_of((first_band + member) * row_out + index * tile_rows, tile_rows)
                    target[pl.ds(start, tile_rows), :] = merged[:, member * width : (member + 1) * width]
                return carry

            lax.fori_loop(0, row_out // tile_rows, tile, 0)
        source = target


def run_matmul_levels(state, first_rows, second_rows, shifts, levels, plan):
    width = state.shape[1]
    tables = []
    for level, (row_in, row_out, bands_out, depth) in zip(levels, plan):
        columns = jnp.arange(depth, dtype=jnp.int32)[None, :]
        tables.append((first_rows[level, :row_out, None] == columns).astype(jnp.bfloat16))
        tables.append((second_rows[level, :row_out, None] == columns).astype(jnp.bfloat16))
        tables.append(shifts[level, :row_out, None])
    buf_rows = max(p[1] * p[2] for p in plan)
    depth_most = max(p[3] for p in plan)
    vmem = pl.BlockSpec(memory_space=pltpu.VMEM)
    return pl.pallas_call(
        functools.partial(matmul_kernel, plan),
        out_shape=jax.ShapeDtypeStruct((plan[-1][1] * plan[-1][2] // 2, width), jnp.float32),
        in_specs=[vmem] * (1 + len(tables)),
        out_specs=vmem,
        scratch_shapes=[
            pltpu.VMEM((buf_rows, width), jnp.float32),
            pltpu.VMEM((buf_rows, width), jnp.float32),
            pltpu.VMEM((2, PIECES, depth_most, 2 * width), jnp.bfloat16),
            pltpu.VMEM((min(TILE, plan[-1][1]), width), jnp.float32),
        ],
        compiler_params=pltpu.CompilerParams(vmem_limit_bytes=60 * 1024 * 1024),
    )(state, *tables)


def harmonic_kernel(spectrum_ref, offset_ref, out_ref, power_ref):
    fundamentals = out_ref.shape[1]
    power_ref[...] = jnp.transpose(spectrum_ref[...])
    total = None
    for order in range(HARM):
        stride = order + 1
        offset = jnp.broadcast_to(offset_ref[order], (fundamentals, power_ref.shape[1]))
        term = power_ref[pl.ds(0, fundamentals, stride=stride), :]
        for phase in range(1, stride):
            picked = power_ref[pl.ds(phase, fundamentals, stride=stride), :]
            term = jnp.where(offset == phase, picked, term)
        total = term if total is None else total + term
    out_ref[...] = jnp.transpose(total * (1.0 / HARM))


def delayed(value, amount):
    rolled = pltpu.roll(value, amount, 2)
    previous = jnp.concatenate([rolled[-1:], rolled[:-1]], axis=0)
    lane = lax.broadcasted_iota(jnp.int32, value.shape, 2)
    return jnp.where(lane < amount, previous, rolled)


def local_kernel(plan, sub, base, table_ref, x_ref, out_ref, *bufs):
    count = len(plan)
    final = bufs[-1]
    source = x_ref
    for step, (row_in, row_out, bands_out) in enumerate(plan):
        target = final if step == count - 1 else bufs[step]

        def body(row, carry, source=source, target=target, step=step,
                 bands_out=bands_out, last=step == count - 1):
            lower = source[table_ref[0, step, row], :, pl.ds(0, bands_out, stride=2), :]
            upper = source[table_ref[1, step, row], :, pl.ds(1, bands_out, stride=2), :]
            merged = lower + delayed(upper, table_ref[2, step, row])
            if last:
                target[:, pl.ds(row, 1), :] = merged
            else:
                target[row] = merged
            return carry

        lax.fori_loop(0, row_out, body, 0, unroll=min(row_out, 32 if bands_out <= 4 else 16))
        source = target
    for dest in range(out_ref.shape[0]):
        start = base + sub * dest
        slab, offset = start // LANES, start % LANES
        if offset == 0:
            out_ref[dest] = final[slab]
        else:
            lane = lax.broadcasted_iota(jnp.int32, final.shape[1:], 1)
            head = pltpu.roll(final[slab], LANES - offset, 1)
            tail = pltpu.roll(final[slab + 1], LANES - offset, 1)
            out_ref[dest] = jnp.where(lane < LANES - offset, head, tail)


def run_local(state, tables, plan, parts, sub, base):
    slabs = state.shape[1]
    rows_last = plan[-1][1]
    smem = pl.BlockSpec(memory_space=pltpu.SMEM)
    vmem = pl.BlockSpec(memory_space=pltpu.VMEM)
    scratch = [pltpu.VMEM((p[1], slabs, p[2], LANES), jnp.float32) for p in plan[:-1]]
    scratch.append(pltpu.VMEM((slabs, rows_last, LANES), jnp.float32))
    return pl.pallas_call(
        functools.partial(local_kernel, plan, sub, base),
        out_shape=jax.ShapeDtypeStruct((parts, rows_last, sub + SUB_HALO), jnp.float32),
        in_specs=[smem, vmem],
        out_specs=vmem,
        scratch_shapes=scratch,
        compiler_params=pltpu.CompilerParams(vmem_limit_bytes=56 * 1024 * 1024),
    )(tables, state)


def spectra(series, harmonic_bins):
    count = series.shape[0]
    total = series.shape[1]
    outer = DFT_OUTER
    inner = total // outer
    half_inner = inner // 2
    highest = lax.Precision.HIGH
    grid = series.reshape(count, outer, inner)
    outer_index = jnp.arange(outer, dtype=jnp.int32)
    inner_index = jnp.arange(inner, dtype=jnp.int32)
    half_index = jnp.arange(half_inner, dtype=jnp.int32)
    angle_outer = (
        2.0
        * math.pi
        / outer
        * (outer_index[:, None] * outer_index[None, :] % outer).astype(jnp.float32)
    )
    outer_table = jnp.concatenate([jnp.cos(angle_outer), jnp.sin(angle_outer)], axis=1)
    section_one = jnp.einsum("npq,pk->nkq", grid, outer_table, precision=highest)
    section_re = section_one[:, :outer]
    section_im = -section_one[:, outer:]
    angle_twist = (
        2.0
        * math.pi
        / total
        * (outer_index[:, None] * inner_index[None, :] % total).astype(jnp.float32)
    )
    twist_cos = jnp.cos(angle_twist)
    twist_sin = jnp.sin(angle_twist)
    rotated = jnp.stack(
        [
            section_re * twist_cos + section_im * twist_sin,
            section_im * twist_cos - section_re * twist_sin,
        ]
    )
    angle_inner = (
        2.0
        * math.pi
        / inner
        * (inner_index[:, None] * half_index[None, :] % inner).astype(jnp.float32)
    )
    inner_table = jnp.concatenate([jnp.cos(angle_inner), jnp.sin(angle_inner)], axis=1)
    section_two = jnp.einsum("snkq,qm->snkm", rotated, inner_table, precision=highest)
    final_re = section_two[0, :, :, :half_inner] + section_two[1, :, :, half_inner:]
    final_im = section_two[1, :, :, :half_inner] - section_two[0, :, :, half_inner:]
    spectrum_power = (final_re * final_re + final_im * final_im) / (C * total)
    spectrum_power = jnp.transpose(spectrum_power, (0, 2, 1)).reshape(count, total // 2)
    fundamentals = harmonic_bins.shape[1]
    fundamental = jnp.arange(fundamentals, dtype=jnp.int32)
    stride = jnp.arange(1, HARM + 1, dtype=jnp.int32)[:, None]
    offsets = (harmonic_bins - stride * fundamental[None, :])[:, :, None]
    vmem = pl.BlockSpec(memory_space=pltpu.VMEM)
    harmonic = pl.pallas_call(
        harmonic_kernel,
        out_shape=jax.ShapeDtypeStruct((count, fundamentals), jnp.float32),
        in_specs=[vmem, vmem],
        out_specs=vmem,
        scratch_shapes=[pltpu.VMEM((total // 2, count), jnp.float32)],
    )(spectrum_power, offsets)
    return spectrum_power, harmonic


def on_device(filterbank, first_rows, second_rows, shifts, harmonic_bins):
    channels = filterbank.shape[0]
    samples = filterbank.shape[1]
    local_levels = channels.bit_length() - 1
    chan_count = lax.axis_size("chan")
    tm_count = lax.axis_size("tm")
    cross_levels = chan_count.bit_length() - 1
    levels = local_levels + cross_levels
    rim = lax.ppermute(
        filterbank[:, samples - RAW_HALO :],
        "tm",
        [(source, source + 1) for source in range(tm_count - 1)],
    )
    widened = jnp.concatenate([rim, filterbank], axis=1)
    local_plan = [
        (2**level, 2 ** (level + 1), channels >> (level + 1)) for level in range(local_levels)
    ]
    sub = samples // chan_count
    pieces = run_local(
        widened.astype(jnp.float32).reshape(channels, -1, LANES).transpose(1, 0, 2)[None],
        jnp.stack([first_rows, second_rows, shifts])[:, :local_levels, :channels],
        local_plan,
        chan_count,
        sub,
        RAW_HALO - SUB_HALO,
    )
    cross_tables = jnp.stack([first_rows, second_rows, shifts])[:, local_levels:]
    pieces, cross_tables = lax.optimization_barrier((pieces, cross_tables))
    window = sub + SUB_HALO
    layers = lax.all_to_all(pieces, "chan", split_axis=0, concat_axis=0, tiled=True)
    cross_plan = []
    bands = chan_count
    for level in range(local_levels, levels):
        bands //= 2
        rows_in = min(2**level, NDM)
        cross_plan.append((rows_in, min(2 ** (level + 1), NDM), bands, min(rows_in, NDM // 2)))
    plane = run_matmul_levels(
        layers.reshape(chan_count * channels, window),
        cross_tables[0],
        cross_tables[1],
        cross_tables[2],
        list(range(levels - local_levels)),
        cross_plan,
    )
    groups = chan_count * tm_count
    share = NDM // groups
    outgoing = plane.reshape(groups, share // 2, 2 * sub)
    incoming = lax.all_to_all(outgoing, ("chan", "tm"), split_axis=0, concat_axis=0, tiled=True)
    series = (
        incoming.reshape(chan_count, tm_count, share // 2, 2, sub)
        .transpose(2, 3, 1, 0, 4)
        .reshape(share, tm_count * samples)
    )
    return spectra(series, harmonic_bins)


def solution(mesh):
    in_specs = (P("chan", "tm"), P(), P(), P(), P())
    out_specs = (P(("chan", "tm"), None), P(("chan", "tm"), None))
    return jax.shard_map(
        on_device, mesh=mesh, in_specs=in_specs, out_specs=out_specs, check_vma=False
    )
```
